32 devices in a mesh: group: 2 (over x), wide: 16 (over z, y, core).
Axes of the slice: x: 2, y: 2, z: 4, core: 2. Of those that a mesh axis runs over, the one named last changes fastest.
Arguments:
- stream_index: int32 [2], P('group'), parts along dimension 0, may hold values from 0 to 16777215
- forcing: bfloat16 [32, 1536, 1536], P('group', 'wide'), parts along dimension 0, may hold values from -144 to 144
Outputs:
- pressure: bfloat16 [32, 1536, 1536], P('group', 'wide'), parts along dimension 0
The draws below stay inside these ranges and needn't reach their ends.
There are 2 independent parts, one for each index of `group`. The reference program is written for one: setup_inputs(seed, part) draws one part's arguments, and reference() takes and returns one part's arrays. A program takes and returns all parts, laid end to end along the dimension named above; each array names one. Nothing has to cross between parts.
All inputs are finite; a program needn't handle non-finite values.
Results may differ from the reference program's by a relative error of at most 0.0045.
Values may be sent and summed in bfloat16 or wider, within the bound.
No kernel may reach another device: no remote copies, remote signals or barrier semaphores. Data moves between devices by JAX's collectives and lax.ppermute only.
A program may use at most 192 MiB of HBM per device.

```python
import math
import jax
import jax.numpy as jnp
from jax import lax

LEN_X = 1536
LEN_Y = 1536
ITERS = 4
NZ = 16


def levels(key, extent, cuts, low, largest):
    factor_of = 1.0
    for dim, parts in cuts:
        draws = jax.random.uniform(jax.random.fold_in(jax.random.fold_in(key, 6), dim), (parts,), jnp.float32, low / len(cuts), largest / len(cuts))
        factor_of = factor_of * jnp.repeat(jnp.exp(draws), extent[dim] // parts).reshape((-1,) + (1,) * (len(extent) - 1 - dim))
    return factor_of


def scatter_about(rng, shape, spread, most, pieces=(), held_as=jnp.bfloat16):
    level = levels(rng, shape, pieces, -0.22, 0.18) if pieces else 1.0
    entries = jax.random.normal(rng, shape, jnp.float32) * spread * level
    return jnp.minimum(jnp.maximum(entries, -most), most).astype(held_as)


def setup_inputs(seed: int = 0, part: int = 0) -> dict:
    splits = jax.random.split(jax.random.key(seed), 3)
    part_splits = jax.random.split(jax.random.fold_in(splits[2], part), 3)
    stream_index = jax.random.randint(part_splits[0], (1,), 0, 16777216).astype(jnp.int32)
    forcing = scatter_about(part_splits[1], (NZ, LEN_X, LEN_Y), 24.0, 144.0, ((1, 16),))
    return {"stream_index": stream_index, "forcing": forcing}


def scramble(value):
    value = value ^ value >> 16 & 65535
    value = value * 73244475
    value = value ^ value >> 16 & 65535
    value = value * 73244475
    value = value ^ value >> 16 & 65535
    return value

def cosine_basis(length):
    row_idx = lax.broadcasted_iota(jnp.int32, (length, length), 0)
    mode_idx = lax.broadcasted_iota(jnp.int32, (length, length), 1)
    phase = (2 * row_idx + 1) * mode_idx % (4 * length)
    angle = phase.astype(jnp.float32) * (math.pi / (2.0 * length))
    weights = jnp.where(mode_idx == 0, math.sqrt(1.0 / length), math.sqrt(2.0 / length))
    return (weights * jnp.cos(angle)).astype(jnp.bfloat16)

def coefficient_plane(stream_key, mode_z, depth):
    mode_x = lax.broadcasted_iota(jnp.int32, (LEN_X, LEN_Y), 0)
    mode_y = lax.broadcasted_iota(jnp.int32, (LEN_X, LEN_Y), 1)
    counter = (mode_z * LEN_X + mode_x) * LEN_Y + mode_y
    bits_a = scramble(2 * counter ^ stream_key)
    bits_b = scramble(2 * counter + 1 ^ stream_key)
    uniform_a = (bits_a >> 8 & 16777215).astype(jnp.float32) * 2.0 ** (-24) + 2.0 ** (-25)
    uniform_b = (bits_b >> 8 & 16777215).astype(jnp.float32) * 2.0 ** (-24) + 2.0 ** (-25)
    noise = jnp.sqrt(-2.0 * jnp.log(uniform_a)) * jnp.cos(2.0 * math.pi * uniform_b)
    freq_x = mode_x.astype(jnp.float32) * (math.pi / LEN_X)
    freq_y = mode_y.astype(jnp.float32) * (math.pi / LEN_Y)
    freq_z = mode_z.astype(jnp.float32) * (math.pi / depth)
    amplitude = 1.0 / jnp.sqrt(0.05 + freq_x * freq_x + freq_y * freq_y + freq_z * freq_z)
    return (amplitude * noise).astype(jnp.bfloat16)

def contract_last(left, table):
    return lax.dot_general(left, table, (((left.ndim - 1,), (1,)), ((), ())), preferred_element_type=jnp.float32)

def operate(press, perm):
    total = jnp.zeros_like(press)
    for axis in range(3):
        widths = [(0, 0), (0, 0), (0, 0)]
        widths[axis] = (1, 1)
        padded_p = jnp.pad(press, widths)
        padded_k = jnp.pad(perm, widths)
        size_here = press.shape[axis]
        for start in (0, 2):
            near_p = lax.slice_in_dim(padded_p, start, start + size_here, axis=axis)
            near_k = lax.slice_in_dim(padded_k, start, start + size_here, axis=axis)
            total = total + 0.5 * (perm + near_k) * (press - near_p)
    return total

def reference(stream_index, forcing):
    depth = forcing.shape[0]
    stream_key = scramble(stream_index[0] ^ 1540483477)
    basis_x = cosine_basis(LEN_X)
    basis_y = cosine_basis(LEN_Y)
    basis_z = cosine_basis(depth)

    def one_plane(mode_z):
        coeff = coefficient_plane(stream_key, mode_z, depth)
        rows = jnp.dot(basis_x, coeff, preferred_element_type=jnp.float32).astype(jnp.bfloat16)
        return contract_last(rows, basis_y).astype(jnp.bfloat16)
    planes = lax.map(one_plane, jnp.arange(depth, dtype=jnp.int32))
    field = jnp.dot(basis_z, planes.reshape(depth, LEN_X * LEN_Y), preferred_element_type=jnp.float32)
    field = field.reshape(depth, LEN_X, LEN_Y)
    perm = jnp.exp(1.5 * jnp.tanh(2.0 * field))
    source = forcing.astype(jnp.float32)
    theta = 27.9
    delta = 26.1
    sigma = theta / delta
    rho = 1.0 / sigma
    step = source / theta
    press = step
    for count in range(ITERS - 1):
        resid = source - operate(press, perm)
        rho_next = 1.0 / (2.0 * sigma - rho)
        step = rho_next * rho * step + 2.0 * rho_next / delta * resid
        press = press + step
        rho = rho_next
    return press.astype(jnp.bfloat16)
```

```python
import functools
import math

import jax
import jax.numpy as jnp
from jax import lax
from jax.experimental import pallas as pl
from jax.experimental.pallas import tpu as pltpu
from jax.sharding import PartitionSpec as P

LEN_X = 1536
LEN_Y = 1536
ITERS = 4


def with_halo(block, sides, width):
    for axis, dim in sides:
        count = lax.axis_size(axis)
        forward = [(i, i + 1) for i in range(count - 1)]
        backward = [(target, source) for source, target in forward]
        low = lax.ppermute(
            lax.slice_in_dim(block, block.shape[dim] - width, None, axis=dim), axis, forward
        )
        high = lax.ppermute(lax.slice_in_dim(block, 0, width, axis=dim), axis, backward)
        block = jnp.concatenate([low, block, high], axis=dim)
    return block


def scramble(value):
    value = value ^ value >> 16 & 65535
    value = value * 73244475
    value = value ^ value >> 16 & 65535
    value = value * 73244475
    value = value ^ value >> 16 & 65535
    return value


def cosine_basis(length):
    row_idx = lax.broadcasted_iota(jnp.int32, (length, length), 0)
    mode_idx = lax.broadcasted_iota(jnp.int32, (length, length), 1)
    phase = (2 * row_idx + 1) * mode_idx % (4 * length)
    angle = phase.astype(jnp.float32) * (math.pi / (2.0 * length))
    weights = jnp.where(mode_idx == 0, math.sqrt(1.0 / length), math.sqrt(2.0 / length))
    return (weights * jnp.cos(angle)).astype(jnp.bfloat16)


def coefficient_plane(stream_key, mode_z, depth):
    mode_x = lax.broadcasted_iota(jnp.int32, (LEN_X, LEN_Y), 0)
    mode_y = lax.broadcasted_iota(jnp.int32, (LEN_X, LEN_Y), 1)
    counter = (mode_z * LEN_X + mode_x) * LEN_Y + mode_y
    bits_a = scramble(2 * counter ^ stream_key)
    bits_b = scramble(2 * counter + 1 ^ stream_key)
    uniform_a = (bits_a >> 8 & 16777215).astype(jnp.float32) * 2.0 ** (-24) + 2.0 ** (-25)
    uniform_b = (bits_b >> 8 & 16777215).astype(jnp.float32) * 2.0 ** (-24) + 2.0 ** (-25)
    noise = jnp.sqrt(-2.0 * jnp.log(uniform_a)) * jnp.cos(2.0 * math.pi * uniform_b)
    freq_x = mode_x.astype(jnp.float32) * (math.pi / LEN_X)
    freq_y = mode_y.astype(jnp.float32) * (math.pi / LEN_Y)
    freq_z = mode_z.astype(jnp.float32) * (math.pi / depth)
    amplitude = 1.0 / jnp.sqrt(0.05 + freq_x * freq_x + freq_y * freq_y + freq_z * freq_z)
    return (amplitude * noise).astype(jnp.bfloat16)


def contract_last(left, table):
    return lax.dot_general(
        left, table, (((left.ndim - 1,), (1,)), ((), ())), preferred_element_type=jnp.float32
    )


def operate(wide_p, wide_k):
    center_p = wide_p[:, 1:-1]
    center_k = wide_k[:, 1:-1]
    total = 0.5 * (center_k + wide_k[:, 2:]) * (center_p - wide_p[:, 2:])
    total = total + 0.5 * (center_k + wide_k[:, :-2]) * (center_p - wide_p[:, :-2])
    for axis in (0, 2):
        widths = [(0, 0), (0, 0), (0, 0)]
        widths[axis] = (1, 1)
        padded_p = jnp.pad(center_p, widths)
        padded_k = jnp.pad(center_k, widths)
        size_here = center_p.shape[axis]
        for start in (0, 2):
            near_p = lax.slice_in_dim(padded_p, start, start + size_here, axis=axis)
            near_k = lax.slice_in_dim(padded_k, start, start + size_here, axis=axis)
            total = total + 0.5 * (center_k + near_k) * (center_p - near_p)
    return total


def plain_body(stream_index, forcing):
    depth = forcing.shape[0]
    planes_here = depth // lax.axis_size("wide")
    stream_key = scramble(stream_index[0] ^ 1540483477)
    basis_x = cosine_basis(LEN_X)
    basis_y = cosine_basis(LEN_Y)
    basis_z = cosine_basis(depth)
    first_mode = lax.axis_index("wide") * planes_here
    own_modes = first_mode + jnp.arange(planes_here, dtype=jnp.int32)

    def rows_for(mode_z):
        coeff = coefficient_plane(stream_key, mode_z, depth)
        return jnp.dot(basis_x, coeff, preferred_element_type=jnp.float32).astype(jnp.bfloat16)

    def both_axes(mode_z):
        return contract_last(rows_for(mode_z), basis_y).astype(jnp.bfloat16)

    planes = lax.map(both_axes, own_modes)
    block = lax.all_to_all(planes, "wide", split_axis=1, concat_axis=0, tiled=True)
    count_z, count_x, count_y = block.shape
    field = jnp.dot(
        basis_z, block.reshape(count_z, count_x * count_y), preferred_element_type=jnp.float32
    )
    field = field.reshape(count_z, count_x, count_y)
    perm = jnp.exp(1.5 * jnp.tanh(2.0 * field))
    source = forcing.astype(jnp.float32)
    theta = 27.9
    delta = 26.1
    sigma = theta / delta
    rho = 1.0 / sigma
    step = source / theta
    press = step
    perm_wide = with_halo(perm.astype(jnp.bfloat16), (("wide", 1),), 1).astype(perm.dtype)
    for count in range(ITERS - 1):
        press_wide = with_halo(press, (("wide", 1),), 1)
        resid = source - operate(press_wide, perm_wide)
        rho_next = 1.0 / (2.0 * sigma - rho)
        step = rho_next * rho * step + 2.0 * rho_next / delta * resid
        press = press + step
        rho = rho_next
    return press.astype(jnp.bfloat16)


WIDE = 16
DEPTH = 16
HALO = ITERS - 1
TILE = 16
VMEM_LIMIT = 58 << 20
THETA = 27.9
DELTA = 26.1
SIN_PI = (
    3.141592640144167, -5.16771008404795, 2.550077528430638, -0.5982912997813382, 0.077657661199004
)
MULT = 73244475


def cos_turns(turns, amplitude, negative=False):
    coeffs = [c * math.sqrt(2.0 * amplitude) for c in SIN_PI]
    square = turns * turns
    poly = coeffs[4] * square + coeffs[3]
    for c in coeffs[2::-1]:
        poly = poly * square + c
    sine = poly * turns
    return sine * sine - amplitude if negative else amplitude - sine * sine


def turns_of(phase, period):
    return (phase - jnp.floor(phase * (1.0 / period) + 0.5) * period) * (1.0 / period)


def srl(value, count):
    return lax.shift_right_logical(value, jnp.int32(count))


def basis_into(out_ref, cos_ref, sin_ref, big_cos_ref, big_sin_ref, length, rows):
    period = 4.0 * length
    tiles = length // rows

    def phases(table_rows, of_row, cos_out, sin_out, weighted):
        def part(i, carry):
            r = lax.broadcasted_iota(jnp.int32, (8, 128), 0) + i * 8
            factor = of_row(r).astype(jnp.float32)
            at = pl.ds(pl.multiple_of(i * 8, 8), 8)
            for j in range(length // 128):
                k = lax.broadcasted_iota(jnp.int32, (8, 128), 1).astype(jnp.float32) + 128.0 * j
                phase = factor * k
                cosine = cos_turns(turns_of(phase, period), 1.0)
                sine = cos_turns(turns_of(phase - length, period), 1.0)
                if weighted:
                    weight = jnp.where(k == 0.0, math.sqrt(1.0 / length), math.sqrt(2.0 / length))
                    cosine = cosine * weight
                    sine = sine * weight
                cos_out[at, j * 128 : (j + 1) * 128] = cosine
                sin_out[at, j * 128 : (j + 1) * 128] = sine
            return carry

        lax.fori_loop(0, table_rows // 8, part, 0)

    phases(rows, lambda r: 2 * r + 1, cos_ref, sin_ref, True)
    phases(tiles, lambda t: 2 * rows * t, big_cos_ref, big_sin_ref, False)

    def tile(group, carry):
        group_at = pl.ds(pl.multiple_of(group * 8, 8), 8)
        for j in range(length // 128):
            cols = slice(j * 128, (j + 1) * 128)
            big_cos = big_cos_ref[group_at, cols]
            big_sin = big_sin_ref[group_at, cols]
            for t in range(8):
                at = pl.ds(pl.multiple_of((group * 8 + t) * rows, rows), rows)
                value = cos_ref[:, cols] * big_cos[t : t + 1] - sin_ref[:, cols] * big_sin[t : t + 1]
                out_ref[at, cols] = value.astype(jnp.bfloat16)
        return carry

    lax.fori_loop(0, tiles // 8, tile, 0)


def coefficients_into(out_ref, key, mode_z, depth, rows):
    const = 2.0 * math.log(2.0)
    key_low = key & 1023
    key_high = key & ~1023

    def part(i, carry):
        r = lax.broadcasted_iota(jnp.int32, (rows, 128), 0) + i * rows
        at = pl.ds(pl.multiple_of(i * rows, rows), rows)
        freq_x = r.astype(jnp.float32) * (math.pi / LEN_X)
        freq_z = mode_z.astype(jnp.float32) * (math.pi / depth)
        row_part = (0.05 + freq_x * freq_x + freq_z * freq_z) * -const
        base = (r + mode_z * LEN_X) * (2 * LEN_Y)
        lane = lax.broadcasted_iota(jnp.int32, (1, 128), 1)
        for j in range(LEN_Y // 128):
            if j % 4 == 0:
                top = (base + j * 256) ^ key_high
                top = top ^ srl(top, 16)
                delta = jnp.where(((top ^ key_low) & 1) == 0, MULT, -MULT)
            freq_y = (lane + j * 128).astype(jnp.float32) * (math.pi / LEN_Y)
            denom = row_part + freq_y * freq_y * -const
            a = (top ^ (((lane + (j % 4) * 128) * 2) ^ key_low)) * MULT
            b = a + delta
            a = (a ^ srl(a, 16)) * MULT
            b = (b ^ srl(b, 16)) * MULT
            a = srl(a ^ srl(a, 16), 8)
            b = (b ^ srl(b, 16)) >> 8
            u = a.astype(jnp.float32) * 2.0 ** (-24) + 2.0 ** (-25)
            turns = b.astype(jnp.float32) * 2.0 ** (-24) + 2.0 ** (-25)
            bits = jnp.minimum(jnp.log2(u), -1e-30)
            size = bits * lax.rsqrt(bits * denom)
            value = size * cos_turns(turns, const, negative=True)
            out_ref[at, j * 128 : (j + 1) * 128] = value.astype(jnp.bfloat16)
        return carry

    lax.fori_loop(0, LEN_X // rows, part, 0)


def transform_into(out_ref, left_ref, coef_ref, rows_ref, basis_ref):
    for n in range(0, LEN_Y, 256):
        cols = slice(n, n + 256)
        rows_ref[:, cols] = jnp.dot(
            left_ref[...], coef_ref[:, cols], preferred_element_type=jnp.float32
        ).astype(jnp.bfloat16)
    for n in range(0, LEN_Y, 256):
        cols = slice(n, n + 256)
        out_ref[:, cols] = contract_last(rows_ref[...], basis_ref[cols, :]).astype(jnp.bfloat16)


def first_planes_kernel(
    scalars, out_ref, basis_out, basis, coef, rows, cos_a, sin_a, cos_b, sin_b, sem, *, depth, count
):
    basis_into(basis, cos_a, sin_a, cos_b, sin_b, LEN_X, 64)
    copy = pltpu.make_async_copy(basis, basis_out, sem)
    copy.start()
    coefficients_into(coef, scalars[0], scalars[1], depth, 64)
    left = basis.at[pl.ds(pl.multiple_of(scalars[2], count), count), :]
    transform_into(out_ref, left, coef, rows, basis)
    copy.wait()


def first_planes(scalars, depth, count):
    return pl.pallas_call(
        functools.partial(first_planes_kernel, depth=depth, count=count),
        in_specs=[pl.BlockSpec(memory_space=pltpu.SMEM)],
        out_specs=[pl.BlockSpec(memory_space=pltpu.VMEM), pl.BlockSpec(memory_space=pl.ANY)],
        out_shape=[
            jax.ShapeDtypeStruct((count, LEN_Y), jnp.bfloat16),
            jax.ShapeDtypeStruct((LEN_X, LEN_X), jnp.bfloat16),
        ],
        scratch_shapes=[
            pltpu.VMEM((LEN_X, LEN_X), jnp.bfloat16),
            pltpu.VMEM((LEN_X, LEN_Y), jnp.bfloat16),
            pltpu.VMEM((count, LEN_Y), jnp.bfloat16),
            pltpu.VMEM((64, LEN_X), jnp.float32),
            pltpu.VMEM((64, LEN_X), jnp.float32),
            pltpu.VMEM((LEN_X // 64, LEN_X), jnp.float32),
            pltpu.VMEM((LEN_X // 64, LEN_X), jnp.float32),
            pltpu.SemaphoreType.DMA,
        ],
        compiler_params=pltpu.CompilerParams(vmem_limit_bytes=VMEM_LIMIT),
        name="first_planes",
    )(scalars)


def more_planes_kernel(scalars, basis_in, out_ref, basis, left, coef, rows, sem, *, depth, count):
    half = count // 2
    copies = [pltpu.make_async_copy(basis_in, basis, sem.at[0])]
    for n in range(2):
        source = basis_in.at[pl.ds(pl.multiple_of(scalars[2 + n], half), half), :]
        copies.append(pltpu.make_async_copy(source, left.at[pl.ds(n * half, half), :], sem.at[1 + n]))
    for copy in copies:
        copy.start()
    coefficients_into(coef, scalars[0], scalars[1], depth, 64)
    for copy in copies:
        copy.wait()
    transform_into(out_ref, left, coef, rows, basis)


def more_planes(scalars, basis, depth, count):
    return pl.pallas_call(
        functools.partial(more_planes_kernel, depth=depth, count=count),
        in_specs=[pl.BlockSpec(memory_space=pltpu.SMEM), pl.BlockSpec(memory_space=pl.ANY)],
        out_specs=pl.BlockSpec(memory_space=pltpu.VMEM),
        out_shape=jax.ShapeDtypeStruct((count, LEN_Y), jnp.bfloat16),
        scratch_shapes=[
            pltpu.VMEM((LEN_X, LEN_X), jnp.bfloat16),
            pltpu.VMEM((count, LEN_X), jnp.bfloat16),
            pltpu.VMEM((LEN_X, LEN_Y), jnp.bfloat16),
            pltpu.VMEM((count, LEN_Y), jnp.bfloat16),
            pltpu.SemaphoreType.DMA((3,)),
        ],
        compiler_params=pltpu.CompilerParams(vmem_limit_bytes=VMEM_LIMIT),
        name="more_planes",
    )(scalars, basis)


def swap_matrix(depth):
    size = depth * TILE
    row = lax.broadcasted_iota(jnp.int32, (size, size), 0)
    col = lax.broadcasted_iota(jnp.int32, (size, size), 1)
    return (col == (row % depth) * TILE + row // depth).astype(jnp.bfloat16)


def turn_kernel(matrix, in_ref, out_ref):
    tile = in_ref[...].reshape(matrix.shape[1], LEN_Y)
    turned = jnp.dot(matrix[...], tile, preferred_element_type=jnp.float32)
    out_ref[...] = turned.astype(jnp.bfloat16).reshape(out_ref.shape)


def turn(matrix, forcing):
    depth, count, _ = forcing.shape
    return pl.pallas_call(
        turn_kernel,
        grid=(count // TILE,),
        in_specs=[
            pl.BlockSpec(matrix.shape, lambda i: (0, 0)),
            pl.BlockSpec((depth, TILE, LEN_Y), lambda i: (0, i, 0)),
        ],
        out_specs=pl.BlockSpec((TILE, depth, LEN_Y), lambda i: (i, 0, 0)),
        out_shape=jax.ShapeDtypeStruct((count, depth, LEN_Y), jnp.bfloat16),
        compiler_params=pltpu.CompilerParams(vmem_limit_bytes=VMEM_LIMIT),
        name="turn",
    )(matrix, forcing)


def perm_kernel(matrix, a_ref, b_ref, c_ref, out_ref):
    field = None
    start = 0
    for ref in (a_ref, b_ref, c_ref):
        size = ref.shape[0] * TILE
        part = jnp.dot(
            matrix[:, start : start + size],
            ref[...].reshape(size, LEN_Y),
            preferred_element_type=jnp.float32,
        )
        field = part if field is None else field + part
        start += size
    out_ref[...] = jnp.exp(1.5 * jnp.tanh(2.0 * field)).astype(jnp.bfloat16).reshape(out_ref.shape)


def permeability(matrix, parts):
    count = parts[0].shape[1]
    depth = sum(part.shape[0] for part in parts)
    return pl.pallas_call(
        perm_kernel,
        grid=(count // TILE,),
        in_specs=[pl.BlockSpec(matrix.shape, lambda i: (0, 0))]
        + [pl.BlockSpec((part.shape[0], TILE, LEN_Y), lambda i: (0, i, 0)) for part in parts],
        out_specs=pl.BlockSpec((TILE, depth, LEN_Y), lambda i: (i, 0, 0)),
        out_shape=jax.ShapeDtypeStruct((count, depth, LEN_Y), jnp.bfloat16),
        compiler_params=pltpu.CompilerParams(vmem_limit_bytes=VMEM_LIMIT),
        name="permeability",
    )(matrix, *parts)


def chebyshev():
    sigma = THETA / DELTA
    rho = 1.0 / sigma
    pairs = []
    for _ in range(ITERS - 1):
        rho_next = 1.0 / (2.0 * sigma - rho)
        pairs.append((rho_next * rho, 2.0 * rho_next / DELTA))
        rho = rho_next
    return pairs


def solve_kernel(
    flags, swap, f_in, f_low, f_high, k_in, k_low, k_high, out_ref, f, kb, kh, pa, pb, tile, flux, sem
):
    count, depth, _ = f_in.shape
    total = count + 2 * HALO
    copies = []
    for n, (low, mid, high, target) in enumerate(((f_low, f_in, f_high, f), (k_low, k_in, k_high, kb))):
        for m, (ref, start) in enumerate(((low, 0), (mid, HALO), (high, HALO + count))):
            copies.append(
                pltpu.make_async_copy(ref, target.at[pl.ds(start, ref.shape[0])], sem.at[3 * n + m])
            )
    for copy in copies:
        copy.start()
    for copy in copies:
        copy.wait()

    def prepare(e, carry):
        kh[e] = 0.5 * kb[e].astype(jnp.float32)
        pa[e] = f[e].astype(jnp.float32) * (1.0 / THETA)
        return carry

    lax.fori_loop(0, total, prepare, 0)
    lane = lax.broadcasted_iota(jnp.int32, (depth, 128), 1)
    level = lax.broadcasted_iota(jnp.int32, (depth, 128), 0)
    blocks = LEN_Y // 128

    def cols(j):
        return slice(j * 128, (j + 1) * 128)

    def up(value):
        return jnp.where(level == depth - 1, 0.0, pltpu.roll(value, depth - 1, 0))

    def iteration(first, last, src, store):
        for j in range(blocks):
            k_here = kh[first - 1, :, cols(j)]
            k_next = kh[first, :, cols(j)]
            flux[:, cols(j)] = (k_here + k_next) * (src[first - 1, :, cols(j)] - src[first, :, cols(j)])

        def row(e, carry):
            p = src[e, :, cols(0)]
            k = kh[e, :, cols(0)]
            p_turn = pltpu.roll(p, 127, 1)
            k_turn = pltpu.roll(k, 127, 1)
            before = None
            for j in range(blocks):
                if j + 1 < blocks:
                    p_after = src[e, :, cols(j + 1)]
                    k_after = kh[e, :, cols(j + 1)]
                    p_after_turn = pltpu.roll(p_after, 127, 1)
                    k_after_turn = pltpu.roll(k_after, 127, 1)
                else:
                    p_after = k_after = None
                    p_after_turn = k_after_turn = 0.0
                p_right = jnp.where(lane == 127, p_after_turn, p_turn)
                k_right = jnp.where(lane == 127, k_after_turn, k_turn)
                flow_y = (k + k_right) * (p - p_right)
                flow_turn = pltpu.roll(flow_y, 1, 1)
                left = jnp.where(lane == 0, -k * p if before is None else before, flow_turn)
                before = flow_turn
                flow_z = (k + up(k)) * (p - up(p))
                under = jnp.where(level == 0, -k * p, pltpu.roll(flow_z, 1, 0))
                flow_x = (k + kh[e + 1, :, cols(j)]) * (p - src[e + 1, :, cols(j)])
                out = (flow_x - flux[:, cols(j)]) + (flow_y - left) + (flow_z - under)
                flux[:, cols(j)] = flow_x
                store(e, j, p, out)
                p, k, p_turn, k_turn = p_after, k_after, p_after_turn, k_after_turn
            return carry

        return row

    def clear(ref, first, last):
        @pl.when(flags[0] == 0)
        def _():
            for e in range(first, HALO):
                ref[e] = jnp.zeros(ref.shape[1:], ref.dtype)

        @pl.when(flags[1] == 0)
        def _():
            for e in range(HALO + count, last):
                ref[e] = jnp.zeros(ref.shape[1:], ref.dtype)

    (a1, b1), (a2, b2), (a3, b3) = chebyshev()

    def store_one(e, j, p, out):
        pb[e, :, cols(j)] = (1.0 + a1 + b1 * THETA) * p - b1 * out

    def store_two(e, j, p, out):
        old = f[e, :, cols(j)].astype(jnp.float32)
        pa[e, :, cols(j)] = (1.0 + a2) * p + (b2 - a2 / THETA) * old - b2 * out

    lax.fori_loop(1, total - 1, iteration(1, total - 1, pa, store_one), 0)
    clear(pb, 1, total - 1)
    lax.fori_loop(2, total - 2, iteration(2, total - 2, pb, store_two), 0)
    clear(pa, 2, total - 2)

    def store_three(e, j, p, out):
        source = f[e, :, cols(j)].astype(jnp.float32)
        value = (1.0 + a3) * p - a3 * pb[e, :, cols(j)] + b3 * (source - out)
        tile[(e - HALO) % TILE, :, cols(j)] = value.astype(jnp.bfloat16)

    row = iteration(HALO, total - HALO, pa, store_three)

    def strip(t, carry):
        lax.fori_loop(HALO + t * TILE, HALO + (t + 1) * TILE, row, 0)
        turned = jnp.dot(
            swap[...], tile[...].reshape(TILE * depth, LEN_Y), preferred_element_type=jnp.float32
        )
        out_ref[:, pl.ds(pl.multiple_of(t * TILE, TILE), TILE), :] = turned.astype(jnp.bfloat16).reshape(
            depth, TILE, LEN_Y
        )
        return carry

    lax.fori_loop(0, count // TILE, strip, 0)


def solve(flags, swap, f_parts, k_parts):
    count, depth, _ = f_parts[0].shape
    total = count + 2 * HALO
    anywhere = pl.BlockSpec(memory_space=pl.ANY)
    return pl.pallas_call(
        solve_kernel,
        in_specs=[pl.BlockSpec(memory_space=pltpu.SMEM), pl.BlockSpec(memory_space=pltpu.VMEM)]
        + [anywhere] * 6,
        out_specs=pl.BlockSpec(memory_space=pltpu.VMEM),
        out_shape=jax.ShapeDtypeStruct((depth, count, LEN_Y), jnp.bfloat16),
        scratch_shapes=[
            pltpu.VMEM((total, depth, LEN_Y), jnp.bfloat16),
            pltpu.VMEM((total, depth, LEN_Y), jnp.bfloat16),
            pltpu.VMEM((total, depth, LEN_Y), jnp.float32),
            pltpu.VMEM((total, depth, LEN_Y), jnp.float32),
            pltpu.VMEM((total, depth, LEN_Y), jnp.float32),
            pltpu.VMEM((TILE, depth, LEN_Y), jnp.bfloat16),
            pltpu.VMEM((depth, LEN_Y), jnp.float32),
            pltpu.SemaphoreType.DMA((6,)),
        ],
        compiler_params=pltpu.CompilerParams(vmem_limit_bytes=VMEM_LIMIT),
        name="solve",
    )(flags, swap, *f_parts, *k_parts)


def edges(block):
    forward = [(i, i + 1) for i in range(WIDE - 1)]
    backward = [(target, source) for source, target in forward]
    low = lax.ppermute(block[-HALO:], "wide", forward)
    high = lax.ppermute(block[:HALO], "wide", backward)
    return block, low, high


def basis_columns(modes, length):
    row_idx = lax.broadcasted_iota(jnp.int32, (length, length), 0)
    phase = (2 * row_idx + 1) * modes[None, :] % (4 * length)
    angle = phase.astype(jnp.float32) * (math.pi / (2.0 * length))
    weights = jnp.where(modes[None, :] == 0, math.sqrt(1.0 / length), math.sqrt(2.0 / length))
    return (weights * jnp.cos(angle)).astype(jnp.bfloat16)


def body(stream_index, forcing):
    depth, count, _ = forcing.shape
    index = lax.axis_index("wide")
    core = index % 2
    side = index // 2 % 2
    far = index // 4 % 2
    color = side ^ far
    key = scramble(stream_index[0] ^ 1540483477)
    own = index // 2 * 2 * count
    shared = DEPTH // 2 + 4 * color + 2 * core

    first, basis = first_planes(
        jnp.stack([key, index % 8, index // 8 * 8 * count]).astype(jnp.int32), depth, 8 * count
    )
    groups = [list(range(8)), list(range(8, 16))]
    part_a = lax.all_to_all(
        first.reshape(8, count, LEN_Y), "wide", 0, 0, axis_index_groups=groups, tiled=True
    )

    def pairwise(mode, other, basis, groups):
        low = jnp.minimum(own, other)
        high = jnp.maximum(own, other)
        out = more_planes(jnp.stack([key, mode, low, high]).astype(jnp.int32), basis, depth, 4 * count)
        part = lax.all_to_all(
            out.reshape(4, count, LEN_Y), "wide", 0, 0, axis_index_groups=groups, tiled=True
        )
        return part

    far_groups = [[s, s + 1, s + 4, s + 5] for s in (0, 2, 8, 10)]
    side_groups = [[s, s + 1, s + 2, s + 3] for s in (0, 4, 8, 12)]
    part_b = pairwise(shared, (index ^ 4) // 2 * 2 * count, basis, far_groups)
    part_c = pairwise(shared + 1, (index ^ 2) // 2 * 2 * count, basis, side_groups)
    slot = jnp.arange(4, dtype=jnp.int32)
    modes_b = DEPTH // 2 + 4 * (slot // 2 ^ side) + 2 * (slot % 2)
    modes_c = DEPTH // 2 + 4 * (slot // 2 ^ far) + 2 * (slot % 2) + 1
    modes = jnp.concatenate([jnp.arange(8, dtype=jnp.int32), modes_b, modes_c])

    swap = swap_matrix(depth)
    f_parts = edges(turn(swap, forcing))
    basis_z = basis_columns(modes, depth)
    eye = jnp.eye(TILE, dtype=jnp.bfloat16)
    mixing = (eye[:, None, None, :] * basis_z[None, :, :, None]).reshape(TILE * depth, depth * TILE)
    k_parts = edges(permeability(mixing, [part_a, part_b, part_c]))
    flags = jnp.stack([index > 0, index < WIDE - 1]).astype(jnp.int32)
    return solve(flags, swap, f_parts, k_parts)


def solution(mesh):
    special = mesh.shape["wide"] == WIDE
    return jax.shard_map(
        body if special else plain_body,
        mesh=mesh,
        in_specs=(P("group"), P("group", "wide", None)),
        out_specs=P("group", "wide", None),
        check_vma=False,
    )
```

```python
import functools
import math

import jax
import jax.numpy as jnp
from jax import lax
from jax.experimental import pallas as pl
from jax.experimental.pallas import tpu as pltpu
from jax.sharding import PartitionSpec as P

LEN_X = 1536
LEN_Y = 1536
ITERS = 4


def with_halo(block, sides, width):
    for axis, dim in sides:
        count = lax.axis_size(axis)
        forward = [(i, i + 1) for i in range(count - 1)]
        backward = [(target, source) for source, target in forward]
        low = lax.ppermute(
            lax.slice_in_dim(block, block.shape[dim] - width, None, axis=dim), axis, forward
        )
        high = lax.ppermute(lax.slice_in_dim(block, 0, width, axis=dim), axis, backward)
        block = jnp.concatenate([low, block, high], axis=dim)
    return block


def scramble(value):
    value = value ^ value >> 16 & 65535
    value = value * 73244475
    value = value ^ value >> 16 & 65535
    value = value * 73244475
    value = value ^ value >> 16 & 65535
    return value


def cosine_basis(length):
    row_idx = lax.broadcasted_iota(jnp.int32, (length, length), 0)
    mode_idx = lax.broadcasted_iota(jnp.int32, (length, length), 1)
    phase = (2 * row_idx + 1) * mode_idx % (4 * length)
    angle = phase.astype(jnp.float32) * (math.pi / (2.0 * length))
    weights = jnp.where(mode_idx == 0, math.sqrt(1.0 / length), math.sqrt(2.0 / length))
    return (weights * jnp.cos(angle)).astype(jnp.bfloat16)


def coefficient_plane(stream_key, mode_z, depth):
    mode_x = lax.broadcasted_iota(jnp.int32, (LEN_X, LEN_Y), 0)
    mode_y = lax.broadcasted_iota(jnp.int32, (LEN_X, LEN_Y), 1)
    counter = (mode_z * LEN_X + mode_x) * LEN_Y + mode_y
    bits_a = scramble(2 * counter ^ stream_key)
    bits_b = scramble(2 * counter + 1 ^ stream_key)
    uniform_a = (bits_a >> 8 & 16777215).astype(jnp.float32) * 2.0 ** (-24) + 2.0 ** (-25)
    uniform_b = (bits_b >> 8 & 16777215).astype(jnp.float32) * 2.0 ** (-24) + 2.0 ** (-25)
    noise = jnp.sqrt(-2.0 * jnp.log(uniform_a)) * jnp.cos(2.0 * math.pi * uniform_b)
    freq_x = mode_x.astype(jnp.float32) * (math.pi / LEN_X)
    freq_y = mode_y.astype(jnp.float32) * (math.pi / LEN_Y)
    freq_z = mode_z.astype(jnp.float32) * (math.pi / depth)
    amplitude = 1.0 / jnp.sqrt(0.05 + freq_x * freq_x + freq_y * freq_y + freq_z * freq_z)
    return (amplitude * noise).astype(jnp.bfloat16)


def contract_last(left, table):
    return lax.dot_general(
        left, table, (((left.ndim - 1,), (1,)), ((), ())), preferred_element_type=jnp.float32
    )


def operate(wide_p, wide_k):
    center_p = wide_p[:, 1:-1]
    center_k = wide_k[:, 1:-1]
    total = 0.5 * (center_k + wide_k[:, 2:]) * (center_p - wide_p[:, 2:])
    total = total + 0.5 * (center_k + wide_k[:, :-2]) * (center_p - wide_p[:, :-2])
    for axis in (0, 2):
        widths = [(0, 0), (0, 0), (0, 0)]
        widths[axis] = (1, 1)
        padded_p = jnp.pad(center_p, widths)
        padded_k = jnp.pad(center_k, widths)
        size_here = center_p.shape[axis]
        for start in (0, 2):
            near_p = lax.slice_in_dim(padded_p, start, start + size_here, axis=axis)
            near_k = lax.slice_in_dim(padded_k, start, start + size_here, axis=axis)
            total = total + 0.5 * (center_k + near_k) * (center_p - near_p)
    return total


def plain_body(stream_index, forcing):
    depth = forcing.shape[0]
    planes_here = depth // lax.axis_size("wide")
    stream_key = scramble(stream_index[0] ^ 1540483477)
    basis_x = cosine_basis(LEN_X)
    basis_y = cosine_basis(LEN_Y)
    basis_z = cosine_basis(depth)
    first_mode = lax.axis_index("wide") * planes_here
    own_modes = first_mode + jnp.arange(planes_here, dtype=jnp.int32)

    def rows_for(mode_z):
        coeff = coefficient_plane(stream_key, mode_z, depth)
        return jnp.dot(basis_x, coeff, preferred_element_type=jnp.float32).astype(jnp.bfloat16)

    def both_axes(mode_z):
        return contract_last(rows_for(mode_z), basis_y).astype(jnp.bfloat16)

    planes = lax.map(both_axes, own_modes)
    block = lax.all_to_all(planes, "wide", split_axis=1, concat_axis=0, tiled=True)
    count_z, count_x, count_y = block.shape
    field = jnp.dot(
        basis_z, block.reshape(count_z, count_x * count_y), preferred_element_type=jnp.float32
    )
    field = field.reshape(count_z, count_x, count_y)
    perm = jnp.exp(1.5 * jnp.tanh(2.0 * field))
    source = forcing.astype(jnp.float32)
    theta = 27.9
    delta = 26.1
    sigma = theta / delta
    rho = 1.0 / sigma
    step = source / theta
    press = step
    perm_wide = with_halo(perm.astype(jnp.bfloat16), (("wide", 1),), 1).astype(perm.dtype)
    for count in range(ITERS - 1):
        press_wide = with_halo(press, (("wide", 1),), 1)
        resid = source - operate(press_wide, perm_wide)
        rho_next = 1.0 / (2.0 * sigma - rho)
        step = rho_next * rho * step + 2.0 * rho_next / delta * resid
        press = press + step
        rho = rho_next
    return press.astype(jnp.bfloat16)


WIDE = 16
DEPTH = 16
HALO = ITERS - 1
PARTS = 4
TILE = 16
VMEM_LIMIT = 58 << 20
THETA = 27.9
DELTA = 26.1
SIN_PI = (
    3.141592640144167, -5.16771008404795, 2.550077528430638, -0.5982912997813382, 0.077657661199004
)
MULT = 73244475


def cos_turns(turns, amplitude, negative=False):
    coeffs = [c * math.sqrt(2.0 * amplitude) for c in SIN_PI]
    square = turns * turns
    poly = coeffs[4] * square + coeffs[3]
    for c in coeffs[2::-1]:
        poly = poly * square + c
    sine = poly * turns
    return sine * sine - amplitude if negative else amplitude - sine * sine


def turns_of(phase, period):
    return (phase - jnp.floor(phase * (1.0 / period) + 0.5) * period) * (1.0 / period)


def srl(value, count):
    return lax.shift_right_logical(value, jnp.int32(count))


def basis_into(out_ref, cos_ref, sin_ref, big_cos_ref, big_sin_ref, length, rows):
    period = 4.0 * length
    tiles = length // rows

    def phases(table_rows, of_row, cos_out, sin_out, weighted):
        def part(i, carry):
            r = lax.broadcasted_iota(jnp.int32, (8, 128), 0) + i * 8
            factor = of_row(r).astype(jnp.float32)
            at = pl.ds(pl.multiple_of(i * 8, 8), 8)
            for j in range(length // 128):
                k = lax.broadcasted_iota(jnp.int32, (8, 128), 1).astype(jnp.float32) + 128.0 * j
                phase = factor * k
                cosine = cos_turns(turns_of(phase, period), 1.0)
                sine = cos_turns(turns_of(phase - length, period), 1.0)
                if weighted:
                    weight = jnp.where(k == 0.0, math.sqrt(1.0 / length), math.sqrt(2.0 / length))
                    cosine = cosine * weight
                    sine = sine * weight
                cos_out[at, j * 128 : (j + 1) * 128] = cosine
                sin_out[at, j * 128 : (j + 1) * 128] = sine
            return carry

        lax.fori_loop(0, table_rows // 8, part, 0)

    phases(rows, lambda r: 2 * r + 1, cos_ref, sin_ref, True)
    phases(tiles, lambda t: 2 * rows * t, big_cos_ref, big_sin_ref, False)

    def tile(group, carry):
        group_at = pl.ds(pl.multiple_of(group * 8, 8), 8)
        for j in range(length // 128):
            cols = slice(j * 128, (j + 1) * 128)
            big_cos = big_cos_ref[group_at, cols]
            big_sin = big_sin_ref[group_at, cols]
            for t in range(8):
                at = pl.ds(pl.multiple_of((group * 8 + t) * rows, rows), rows)
                value = cos_ref[:, cols] * big_cos[t : t + 1] - sin_ref[:, cols] * big_sin[t : t + 1]
                out_ref[at, cols] = value.astype(jnp.bfloat16)
        return carry

    lax.fori_loop(0, tiles // 8, tile, 0)


def coefficients_into(out_ref, key, mode_z, depth, rows):
    const = 2.0 * math.log(2.0)
    key_low = key & 1023
    key_high = key & ~1023

    def part(i, carry):
        r = lax.broadcasted_iota(jnp.int32, (rows, 128), 0) + i * rows
        at = pl.ds(pl.multiple_of(i * rows, rows), rows)
        freq_x = r.astype(jnp.float32) * (math.pi / LEN_X)
        freq_z = mode_z.astype(jnp.float32) * (math.pi / depth)
        row_part = (0.05 + freq_x * freq_x + freq_z * freq_z) * -const
        base = (r + mode_z * LEN_X) * (2 * LEN_Y)
        lane = lax.broadcasted_iota(jnp.int32, (1, 128), 1)
        for j in range(LEN_Y // 128):
            if j % 4 == 0:
                top = (base + j * 256) ^ key_high
                top = top ^ srl(top, 16)
                delta = jnp.where(((top ^ key_low) & 1) == 0, MULT, -MULT)
            freq_y = (lane + j * 128).astype(jnp.float32) * (math.pi / LEN_Y)
            denom = row_part + freq_y * freq_y * -const
            a = (top ^ (((lane + (j % 4) * 128) * 2) ^ key_low)) * MULT
            b = a + delta
            a = (a ^ srl(a, 16)) * MULT
            b = (b ^ srl(b, 16)) * MULT
            a = srl(a ^ srl(a, 16), 8)
            b = (b ^ srl(b, 16)) >> 8
            u = a.astype(jnp.float32) * 2.0 ** (-24) + 2.0 ** (-25)
            turns = b.astype(jnp.float32) * 2.0 ** (-24) + 2.0 ** (-25)
            bits = jnp.minimum(jnp.log2(u), -1e-30)
            size = bits * lax.rsqrt(bits * denom)
            value = size * cos_turns(turns, const, negative=True)
            out_ref[at, j * 128 : (j + 1) * 128] = value.astype(jnp.bfloat16)
        return carry

    lax.fori_loop(0, LEN_X // rows, part, 0)


def transform_into(out_refs, left_ref, coef_ref, rows_ref, basis_ref):
    for n in range(0, LEN_Y, 256):
        cols = slice(n, n + 256)
        rows_ref[:, cols] = jnp.dot(
            left_ref[...], coef_ref[:, cols], preferred_element_type=jnp.float32
        ).astype(jnp.bfloat16)
    size = rows_ref.shape[0] // len(out_refs)
    for n in range(0, LEN_Y, 256):
        cols = slice(n, n + 256)
        value = contract_last(rows_ref[...], basis_ref[cols, :]).astype(jnp.bfloat16)
        for m, out_ref in enumerate(out_refs):
            out_ref[:, cols] = value[m * size : (m + 1) * size]


def first_planes_kernel(
    scalars, out_ref, basis_out, basis, coef, rows, cos_a, sin_a, cos_b, sin_b, sem, *, depth, count
):
    basis_into(basis, cos_a, sin_a, cos_b, sin_b, LEN_X, 64)
    copy = pltpu.make_async_copy(basis, basis_out, sem)
    copy.start()
    coefficients_into(coef, scalars[0], scalars[1], depth, 64)
    left = basis.at[pl.ds(pl.multiple_of(scalars[2], count), count), :]
    transform_into([out_ref], left, coef, rows, basis)
    copy.wait()


def first_planes(scalars, depth, count):
    return pl.pallas_call(
        functools.partial(first_planes_kernel, depth=depth, count=count),
        in_specs=[pl.BlockSpec(memory_space=pltpu.SMEM)],
        out_specs=[pl.BlockSpec(memory_space=pltpu.VMEM), pl.BlockSpec(memory_space=pl.ANY)],
        out_shape=[
            jax.ShapeDtypeStruct((count, LEN_Y), jnp.bfloat16),
            jax.ShapeDtypeStruct((LEN_X, LEN_X), jnp.bfloat16),
        ],
        scratch_shapes=[
            pltpu.VMEM((LEN_X, LEN_X), jnp.bfloat16),
            pltpu.VMEM((LEN_X, LEN_Y), jnp.bfloat16),
            pltpu.VMEM((count, LEN_Y), jnp.bfloat16),
            pltpu.VMEM((64, LEN_X), jnp.float32),
            pltpu.VMEM((64, LEN_X), jnp.float32),
            pltpu.VMEM((LEN_X // 64, LEN_X), jnp.float32),
            pltpu.VMEM((LEN_X // 64, LEN_X), jnp.float32),
            pltpu.SemaphoreType.DMA,
        ],
        compiler_params=pltpu.CompilerParams(vmem_limit_bytes=VMEM_LIMIT),
        cost_estimate=pl.CostEstimate(flops=25_000_000_000, transcendentals=0, bytes_accessed=8_000_000),
        name="first_planes",
    )(scalars)


def more_planes_kernel(scalars, basis_in, *refs, depth):
    out_refs = refs[:PARTS]
    basis, left, coef, rows, sem = refs[PARTS:]
    size = out_refs[0].shape[0]
    copies = [pltpu.make_async_copy(basis_in, basis, sem.at[PARTS])]
    for n in range(PARTS):
        source = basis_in.at[pl.ds(pl.multiple_of(scalars[2 + n], size), size), :]
        copies.append(pltpu.make_async_copy(source, left.at[pl.ds(n * size, size), :], sem.at[n]))
    for copy in copies:
        copy.start()
    coefficients_into(coef, scalars[0], scalars[1], depth, 64)
    for copy in copies:
        copy.wait()
    transform_into(out_refs, left, coef, rows, basis)


def more_planes(scalars, basis, depth, size):
    return pl.pallas_call(
        functools.partial(more_planes_kernel, depth=depth),
        in_specs=[pl.BlockSpec(memory_space=pltpu.SMEM), pl.BlockSpec(memory_space=pl.ANY)],
        out_specs=[pl.BlockSpec(memory_space=pltpu.VMEM)] * PARTS,
        out_shape=[jax.ShapeDtypeStruct((size, LEN_Y), jnp.bfloat16)] * PARTS,
        scratch_shapes=[
            pltpu.VMEM((LEN_X, LEN_X), jnp.bfloat16),
            pltpu.VMEM((PARTS * size, LEN_X), jnp.bfloat16),
            pltpu.VMEM((LEN_X, LEN_Y), jnp.bfloat16),
            pltpu.VMEM((PARTS * size, LEN_Y), jnp.bfloat16),
            pltpu.SemaphoreType.DMA((PARTS + 1,)),
        ],
        compiler_params=pltpu.CompilerParams(vmem_limit_bytes=VMEM_LIMIT),
        cost_estimate=pl.CostEstimate(flops=20_000_000_000, transcendentals=0, bytes_accessed=8_000_000),
        name="more_planes",
    )(scalars, basis)


def swap_matrix(depth):
    size = depth * TILE
    row = lax.broadcasted_iota(jnp.int32, (size, size), 0)
    col = lax.broadcasted_iota(jnp.int32, (size, size), 1)
    return (col == (row % depth) * TILE + row // depth).astype(jnp.bfloat16)


def turn_kernel(matrix, in_ref, out_ref):
    tile = in_ref[...].reshape(matrix.shape[1], LEN_Y)
    turned = jnp.dot(matrix[...], tile, preferred_element_type=jnp.float32)
    out_ref[...] = turned.astype(jnp.bfloat16).reshape(out_ref.shape)


def turn(matrix, forcing):
    depth, count, _ = forcing.shape
    return pl.pallas_call(
        turn_kernel,
        grid=(count // TILE,),
        in_specs=[
            pl.BlockSpec(matrix.shape, lambda i: (0, 0)),
            pl.BlockSpec((depth, TILE, LEN_Y), lambda i: (0, i, 0)),
        ],
        out_specs=pl.BlockSpec((TILE, depth, LEN_Y), lambda i: (i, 0, 0)),
        out_shape=jax.ShapeDtypeStruct((count, depth, LEN_Y), jnp.bfloat16),
        compiler_params=pltpu.CompilerParams(vmem_limit_bytes=VMEM_LIMIT),
        cost_estimate=pl.CostEstimate(flops=1_300_000_000, transcendentals=0, bytes_accessed=10_000_000),
        name="turn",
    )(matrix, forcing)


def perm_kernel(matrix, *refs):
    out_ref = refs[-1]
    a_ref = refs[0]
    split = a_ref.shape[0] * TILE
    field = jnp.dot(
        matrix[:, :split], a_ref[...].reshape(split, LEN_Y), preferred_element_type=jnp.float32
    )
    rest = jnp.concatenate([ref[...] for ref in refs[1:-1]], axis=0)
    field = field + jnp.dot(matrix[:, split:], rest, preferred_element_type=jnp.float32)
    out_ref[...] = jnp.exp(1.5 * jnp.tanh(2.0 * field)).astype(jnp.bfloat16).reshape(out_ref.shape)


def permeability(matrix, block, planes):
    modes, count, _ = block.shape
    depth = modes + len(planes)
    return pl.pallas_call(
        perm_kernel,
        grid=(count // TILE,),
        in_specs=[
            pl.BlockSpec(matrix.shape, lambda i: (0, 0)),
            pl.BlockSpec((modes, TILE, LEN_Y), lambda i: (0, i, 0)),
        ]
        + [pl.BlockSpec((TILE, LEN_Y), lambda i: (i, 0)) for _ in planes],
        out_specs=pl.BlockSpec((TILE, depth, LEN_Y), lambda i: (i, 0, 0)),
        out_shape=jax.ShapeDtypeStruct((count, depth, LEN_Y), jnp.bfloat16),
        compiler_params=pltpu.CompilerParams(vmem_limit_bytes=VMEM_LIMIT),
        cost_estimate=pl.CostEstimate(flops=1_300_000_000, transcendentals=0, bytes_accessed=10_000_000),
        name="permeability",
    )(matrix, block, *planes)


def chebyshev():
    sigma = THETA / DELTA
    rho = 1.0 / sigma
    pairs = []
    for _ in range(ITERS - 1):
        rho_next = 1.0 / (2.0 * sigma - rho)
        pairs.append((rho_next * rho, 2.0 * rho_next / DELTA))
        rho = rho_next
    return pairs


def solve_kernel(
    flags, swap, f_in, f_low, f_high, k_in, k_low, k_high, out_ref, f, kb, kh, pa, pb, tile, flux, sem
):
    count, depth, _ = f_in.shape
    total = count + 2 * HALO
    copies = []
    for n, (low, mid, high, target) in enumerate(((f_low, f_in, f_high, f), (k_low, k_in, k_high, kb))):
        for m, (ref, start) in enumerate(((low, 0), (mid, HALO), (high, HALO + count))):
            copies.append(
                pltpu.make_async_copy(ref, target.at[pl.ds(start, ref.shape[0])], sem.at[3 * n + m])
            )
    for copy in copies:
        copy.start()
    for copy in copies:
        copy.wait()

    def prepare(e, carry):
        kh[e] = 0.5 * kb[e].astype(jnp.float32)
        pa[e] = f[e].astype(jnp.float32) * (1.0 / THETA)
        return carry

    lax.fori_loop(0, total, prepare, 0)
    lane = lax.broadcasted_iota(jnp.int32, (depth, 128), 1)
    level = lax.broadcasted_iota(jnp.int32, (depth, 128), 0)
    blocks = LEN_Y // 128

    def cols(j):
        return slice(j * 128, (j + 1) * 128)

    def up(value):
        return jnp.where(level == depth - 1, 0.0, pltpu.roll(value, depth - 1, 0))

    def iteration(first, last, src, store):
        for j in range(blocks):
            k_here = kh[first - 1, :, cols(j)]
            k_next = kh[first, :, cols(j)]
            flux[:, cols(j)] = (k_here + k_next) * (src[first - 1, :, cols(j)] - src[first, :, cols(j)])

        def row(e, carry):
            p = src[e, :, cols(0)]
            k = kh[e, :, cols(0)]
            p_turn = pltpu.roll(p, 127, 1)
            k_turn = pltpu.roll(k, 127, 1)
            before = None
            for j in range(blocks):
                if j + 1 < blocks:
                    p_after = src[e, :, cols(j + 1)]
                    k_after = kh[e, :, cols(j + 1)]
                    p_after_turn = pltpu.roll(p_after, 127, 1)
                    k_after_turn = pltpu.roll(k_after, 127, 1)
                else:
                    p_after = k_after = None
                    p_after_turn = k_after_turn = 0.0
                p_right = jnp.where(lane == 127, p_after_turn, p_turn)
                k_right = jnp.where(lane == 127, k_after_turn, k_turn)
                flow_y = (k + k_right) * (p - p_right)
                flow_turn = pltpu.roll(flow_y, 1, 1)
                left = jnp.where(lane == 0, -k * p if before is None else before, flow_turn)
                before = flow_turn
                flow_z = (k + up(k)) * (p - up(p))
                under = jnp.where(level == 0, -k * p, pltpu.roll(flow_z, 1, 0))
                flow_x = (k + kh[e + 1, :, cols(j)]) * (p - src[e + 1, :, cols(j)])
                out = (flow_x - flux[:, cols(j)]) + (flow_y - left) + (flow_z - under)
                flux[:, cols(j)] = flow_x
                store(e, j, p, out)
                p, k, p_turn, k_turn = p_after, k_after, p_after_turn, k_after_turn
            return carry

        return row

    def clear(ref, first, last):
        @pl.when(flags[0] == 0)
        def _():
            for e in range(first, HALO):
                ref[e] = jnp.zeros(ref.shape[1:], ref.dtype)

        @pl.when(flags[1] == 0)
        def _():
            for e in range(HALO + count, last):
                ref[e] = jnp.zeros(ref.shape[1:], ref.dtype)

    (a1, b1), (a2, b2), (a3, b3) = chebyshev()

    def store_one(e, j, p, out):
        pb[e, :, cols(j)] = (1.0 + a1 + b1 * THETA) * p - b1 * out

    def store_two(e, j, p, out):
        old = f[e, :, cols(j)].astype(jnp.float32)
        pa[e, :, cols(j)] = (1.0 + a2) * p + (b2 - a2 / THETA) * old - b2 * out

    lax.fori_loop(1, total - 1, iteration(1, total - 1, pa, store_one), 0)
    clear(pb, 1, total - 1)
    lax.fori_loop(2, total - 2, iteration(2, total - 2, pb, store_two), 0)
    clear(pa, 2, total - 2)

    def store_three(e, j, p, out):
        source = f[e, :, cols(j)].astype(jnp.float32)
        value = (1.0 + a3) * p - a3 * pb[e, :, cols(j)] + b3 * (source - out)
        tile[(e - HALO) % TILE, :, cols(j)] = value.astype(jnp.bfloat16)

    row = iteration(HALO, total - HALO, pa, store_three)

    def strip(t, carry):
        lax.fori_loop(HALO + t * TILE, HALO + (t + 1) * TILE, row, 0)
        turned = jnp.dot(
            swap[...], tile[...].reshape(TILE * depth, LEN_Y), preferred_element_type=jnp.float32
        )
        out_ref[:, pl.ds(pl.multiple_of(t * TILE, TILE), TILE), :] = turned.astype(jnp.bfloat16).reshape(
            depth, TILE, LEN_Y
        )
        return carry

    lax.fori_loop(0, count // TILE, strip, 0)


def solve(flags, swap, f_parts, k_parts):
    count, depth, _ = f_parts[0].shape
    total = count + 2 * HALO
    anywhere = pl.BlockSpec(memory_space=pl.ANY)
    return pl.pallas_call(
        solve_kernel,
        in_specs=[pl.BlockSpec(memory_space=pltpu.SMEM), pl.BlockSpec(memory_space=pltpu.VMEM)]
        + [anywhere] * 6,
        out_specs=pl.BlockSpec(memory_space=pltpu.VMEM),
        out_shape=jax.ShapeDtypeStruct((depth, count, LEN_Y), jnp.bfloat16),
        scratch_shapes=[
            pltpu.VMEM((total, depth, LEN_Y), jnp.bfloat16),
            pltpu.VMEM((total, depth, LEN_Y), jnp.bfloat16),
            pltpu.VMEM((total, depth, LEN_Y), jnp.float32),
            pltpu.VMEM((total, depth, LEN_Y), jnp.float32),
            pltpu.VMEM((total, depth, LEN_Y), jnp.float32),
            pltpu.VMEM((TILE, depth, LEN_Y), jnp.bfloat16),
            pltpu.VMEM((depth, LEN_Y), jnp.float32),
            pltpu.SemaphoreType.DMA((6,)),
        ],
        compiler_params=pltpu.CompilerParams(vmem_limit_bytes=VMEM_LIMIT),
        name="solve",
    )(flags, swap, *f_parts, *k_parts)


def edges(block):
    forward = [(i, i + 1) for i in range(WIDE - 1)]
    backward = [(target, source) for source, target in forward]
    low = lax.ppermute(block[-HALO:], "wide", forward)
    high = lax.ppermute(block[:HALO], "wide", backward)
    return block, low, high


def basis_columns(modes, length):
    row_idx = lax.broadcasted_iota(jnp.int32, (length, length), 0)
    phase = (2 * row_idx + 1) * modes[None, :] % (4 * length)
    angle = phase.astype(jnp.float32) * (math.pi / (2.0 * length))
    weights = jnp.where(modes[None, :] == 0, math.sqrt(1.0 / length), math.sqrt(2.0 / length))
    return (weights * jnp.cos(angle)).astype(jnp.bfloat16)


def body(stream_index, forcing):
    depth, count, _ = forcing.shape
    index = lax.axis_index("wide")
    core = index & 1
    color = (index >> 1 ^ index >> 2) & 1
    key = scramble(stream_index[0] ^ 1540483477)
    shared = DEPTH // 2 + 4 * color + 2 * core

    scalars = jnp.stack([key, index & 7, (index >> 3) * (8 * count)]).astype(jnp.int32)
    first, basis = first_planes(scalars, depth, 8 * count)
    groups = [list(range(8)), list(range(8, 16))]
    block = lax.all_to_all(
        first.reshape(8, count, LEN_Y), "wide", 0, 0, axis_index_groups=groups, tiled=True
    )

    def pairwise(mode, bit):
        flips = (0, 1, bit, bit ^ 1)
        scalars = jnp.stack([key, mode] + [(index ^ flip) * count for flip in flips]).astype(jnp.int32)
        out = more_planes(scalars, basis, depth, count)
        return [out[0]] + [
            lax.ppermute(piece, "wide", [(i, i ^ flip) for i in range(WIDE)])
            for piece, flip in zip(out[1:], flips[1:])
        ]

    planes = pairwise(shared, 4) + pairwise(shared + 1, 2)
    half = DEPTH // 2
    shared_modes = jnp.stack(
        [half + 4 * (color ^ b) + 2 * (core ^ c) + a for a in (0, 1) for b in (0, 1) for c in (0, 1)]
    )
    modes = jnp.concatenate([jnp.arange(half, dtype=jnp.int32), shared_modes])
    swap = swap_matrix(depth)
    f_parts = edges(turn(swap, forcing))
    basis_z = basis_columns(modes, depth)
    eye = jnp.eye(TILE, dtype=jnp.bfloat16)
    mixing = (eye[:, None, None, :] * basis_z[None, :, :, None]).reshape(TILE * depth, depth * TILE)
    k_parts = edges(permeability(mixing, block, planes))
    flags = jnp.stack([index > 0, index < WIDE - 1]).astype(jnp.int32)
    return solve(flags, swap, f_parts, k_parts)


def solution(mesh):
    special = mesh.shape["wide"] == WIDE
    return jax.shard_map(
        body if special else plain_body,
        mesh=mesh,
        in_specs=(P("group"), P("group", "wide", None)),
        out_specs=P("group", "wide", None),
        check_vma=False,
    )
```

```python
import functools
import math

import jax
import jax.numpy as jnp
from jax import lax
from jax.experimental import pallas as pl
from jax.experimental.pallas import tpu as pltpu
from jax.sharding import PartitionSpec as P

LEN_X = 1536
LEN_Y = 1536
ITERS = 4


def with_halo(block, sides, width):
    for axis, dim in sides:
        count = lax.axis_size(axis)
        forward = [(i, i + 1) for i in range(count - 1)]
        backward = [(target, source) for source, target in forward]
        low = lax.ppermute(
            lax.slice_in_dim(block, block.shape[dim] - width, None, axis=dim), axis, forward
        )
        high = lax.ppermute(lax.slice_in_dim(block, 0, width, axis=dim), axis, backward)
        block = jnp.concatenate([low, block, high], axis=dim)
    return block


def scramble(value):
    value = value ^ value >> 16 & 65535
    value = value * 73244475
    value = value ^ value >> 16 & 65535
    value = value * 73244475
    value = value ^ value >> 16 & 65535
    return value


def cosine_basis(length):
    row_idx = lax.broadcasted_iota(jnp.int32, (length, length), 0)
    mode_idx = lax.broadcasted_iota(jnp.int32, (length, length), 1)
    phase = (2 * row_idx + 1) * mode_idx % (4 * length)
    angle = phase.astype(jnp.float32) * (math.pi / (2.0 * length))
    weights = jnp.where(mode_idx == 0, math.sqrt(1.0 / length), math.sqrt(2.0 / length))
    return (weights * jnp.cos(angle)).astype(jnp.bfloat16)


def coefficient_plane(stream_key, mode_z, depth):
    mode_x = lax.broadcasted_iota(jnp.int32, (LEN_X, LEN_Y), 0)
    mode_y = lax.broadcasted_iota(jnp.int32, (LEN_X, LEN_Y), 1)
    counter = (mode_z * LEN_X + mode_x) * LEN_Y + mode_y
    bits_a = scramble(2 * counter ^ stream_key)
    bits_b = scramble(2 * counter + 1 ^ stream_key)
    uniform_a = (bits_a >> 8 & 16777215).astype(jnp.float32) * 2.0 ** (-24) + 2.0 ** (-25)
    uniform_b = (bits_b >> 8 & 16777215).astype(jnp.float32) * 2.0 ** (-24) + 2.0 ** (-25)
    noise = jnp.sqrt(-2.0 * jnp.log(uniform_a)) * jnp.cos(2.0 * math.pi * uniform_b)
    freq_x = mode_x.astype(jnp.float32) * (math.pi / LEN_X)
    freq_y = mode_y.astype(jnp.float32) * (math.pi / LEN_Y)
    freq_z = mode_z.astype(jnp.float32) * (math.pi / depth)
    amplitude = 1.0 / jnp.sqrt(0.05 + freq_x * freq_x + freq_y * freq_y + freq_z * freq_z)
    return (amplitude * noise).astype(jnp.bfloat16)


def contract_last(left, table):
    return lax.dot_general(
        left, table, (((left.ndim - 1,), (1,)), ((), ())), preferred_element_type=jnp.float32
    )


def operate(wide_p, wide_k):
    center_p = wide_p[:, 1:-1]
    center_k = wide_k[:, 1:-1]
    total = 0.5 * (center_k + wide_k[:, 2:]) * (center_p - wide_p[:, 2:])
    total = total + 0.5 * (center_k + wide_k[:, :-2]) * (center_p - wide_p[:, :-2])
    for axis in (0, 2):
        widths = [(0, 0), (0, 0), (0, 0)]
        widths[axis] = (1, 1)
        padded_p = jnp.pad(center_p, widths)
        padded_k = jnp.pad(center_k, widths)
        size_here = center_p.shape[axis]
        for start in (0, 2):
            near_p = lax.slice_in_dim(padded_p, start, start + size_here, axis=axis)
            near_k = lax.slice_in_dim(padded_k, start, start + size_here, axis=axis)
            total = total + 0.5 * (center_k + near_k) * (center_p - near_p)
    return total


def plain_body(stream_index, forcing):
    depth = forcing.shape[0]
    planes_here = depth // lax.axis_size("wide")
    stream_key = scramble(stream_index[0] ^ 1540483477)
    basis_x = cosine_basis(LEN_X)
    basis_y = cosine_basis(LEN_Y)
    basis_z = cosine_basis(depth)
    first_mode = lax.axis_index("wide") * planes_here
    own_modes = first_mode + jnp.arange(planes_here, dtype=jnp.int32)

    def rows_for(mode_z):
        coeff = coefficient_plane(stream_key, mode_z, depth)
        return jnp.dot(basis_x, coeff, preferred_element_type=jnp.float32).astype(jnp.bfloat16)

    def both_axes(mode_z):
        return contract_last(rows_for(mode_z), basis_y).astype(jnp.bfloat16)

    planes = lax.map(both_axes, own_modes)
    block = lax.all_to_all(planes, "wide", split_axis=1, concat_axis=0, tiled=True)
    count_z, count_x, count_y = block.shape
    field = jnp.dot(
        basis_z, block.reshape(count_z, count_x * count_y), preferred_element_type=jnp.float32
    )
    field = field.reshape(count_z, count_x, count_y)
    perm = jnp.exp(1.5 * jnp.tanh(2.0 * field))
    source = forcing.astype(jnp.float32)
    theta = 27.9
    delta = 26.1
    sigma = theta / delta
    rho = 1.0 / sigma
    step = source / theta
    press = step
    perm_wide = with_halo(perm.astype(jnp.bfloat16), (("wide", 1),), 1).astype(perm.dtype)
    for count in range(ITERS - 1):
        press_wide = with_halo(press, (("wide", 1),), 1)
        resid = source - operate(press_wide, perm_wide)
        rho_next = 1.0 / (2.0 * sigma - rho)
        step = rho_next * rho * step + 2.0 * rho_next / delta * resid
        press = press + step
        rho = rho_next
    return press.astype(jnp.bfloat16)


WIDE = 16
DEPTH = 16
HALO = ITERS - 1
PARTS = 4
TILE = 16
VMEM_LIMIT = 60 << 20
THETA = 27.9
DELTA = 26.1
SIN_PI = (
    3.141592640144167, -5.16771008404795, 2.550077528430638, -0.5982912997813382, 0.077657661199004
)
MULT = 73244475


def cos_turns(turns, amplitude, negative=False):
    coeffs = [c * math.sqrt(2.0 * amplitude) for c in SIN_PI]
    square = turns * turns
    poly = coeffs[4] * square + coeffs[3]
    for c in coeffs[2::-1]:
        poly = poly * square + c
    sine = poly * turns
    return sine * sine - amplitude if negative else amplitude - sine * sine


def turns_of(phase, period):
    return (phase - jnp.floor(phase * (1.0 / period) + 0.5) * period) * (1.0 / period)


def srl(value, count):
    return lax.shift_right_logical(value, jnp.int32(count))


def basis_into(out_ref, cos_ref, sin_ref, big_cos_ref, big_sin_ref, length, rows):
    period = 4.0 * length
    tiles = length // rows

    def phases(table_rows, of_row, cos_out, sin_out, weighted):
        def part(i, carry):
            r = lax.broadcasted_iota(jnp.int32, (8, 128), 0) + i * 8
            factor = of_row(r).astype(jnp.float32)
            at = pl.ds(pl.multiple_of(i * 8, 8), 8)
            for j in range(length // 128):
                k = lax.broadcasted_iota(jnp.int32, (8, 128), 1).astype(jnp.float32) + 128.0 * j
                phase = factor * k
                cosine = cos_turns(turns_of(phase, period), 1.0)
                sine = cos_turns(turns_of(phase - length, period), 1.0)
                if weighted:
                    weight = jnp.where(k == 0.0, math.sqrt(1.0 / length), math.sqrt(2.0 / length))
                    cosine = cosine * weight
                    sine = sine * weight
                cos_out[at, j * 128 : (j + 1) * 128] = cosine
                sin_out[at, j * 128 : (j + 1) * 128] = sine
            return carry

        lax.fori_loop(0, table_rows // 8, part, 0)

    phases(rows, lambda r: 2 * r + 1, cos_ref, sin_ref, True)
    phases(tiles, lambda t: 2 * rows * t, big_cos_ref, big_sin_ref, False)

    def tile(group, carry):
        group_at = pl.ds(pl.multiple_of(group * 8, 8), 8)
        for j in range(length // 128):
            cols = slice(j * 128, (j + 1) * 128)
            big_cos = big_cos_ref[group_at, cols]
            big_sin = big_sin_ref[group_at, cols]
            for t in range(8):
                at = pl.ds(pl.multiple_of((group * 8 + t) * rows, rows), rows)
                value = cos_ref[:, cols] * big_cos[t : t + 1] - sin_ref[:, cols] * big_sin[t : t + 1]
                out_ref[at, cols] = value.astype(jnp.bfloat16)
        return carry

    lax.fori_loop(0, tiles // 8, tile, 0)


def coefficients_into(out_ref, key, mode_z, depth, rows):
    const = 2.0 * math.log(2.0)
    key_low = key & 1023
    key_high = key & ~1023

    def part(i, carry):
        r = lax.broadcasted_iota(jnp.int32, (rows, 128), 0) + i * rows
        at = pl.ds(pl.multiple_of(i * rows, rows), rows)
        freq_x = r.astype(jnp.float32) * (math.pi / LEN_X)
        freq_z = mode_z.astype(jnp.float32) * (math.pi / depth)
        row_part = (0.05 + freq_x * freq_x + freq_z * freq_z) * -const
        base = (r + mode_z * LEN_X) * (2 * LEN_Y)
        lane = lax.broadcasted_iota(jnp.int32, (1, 128), 1)
        for j in range(LEN_Y // 128):
            if j % 4 == 0:
                top = (base + j * 256) ^ key_high
                top = top ^ srl(top, 16)
                delta = jnp.where(((top ^ key_low) & 1) == 0, MULT, -MULT)
            freq_y = (lane + j * 128).astype(jnp.float32) * (math.pi / LEN_Y)
            denom = row_part + freq_y * freq_y * -const
            a = (top ^ (((lane + (j % 4) * 128) * 2) ^ key_low)) * MULT
            b = a + delta
            a = (a ^ srl(a, 16)) * MULT
            b = (b ^ srl(b, 16)) * MULT
            a = srl(a ^ srl(a, 16), 8)
            b = (b ^ srl(b, 16)) >> 8
            u = a.astype(jnp.float32) * 2.0 ** (-24) + 2.0 ** (-25)
            turns = b.astype(jnp.float32) * 2.0 ** (-24) + 2.0 ** (-25)
            bits = jnp.minimum(jnp.log2(u), -1e-30)
            size = bits * lax.rsqrt(bits * denom)
            value = size * cos_turns(turns, const, negative=True)
            out_ref[at, j * 128 : (j + 1) * 128] = value.astype(jnp.bfloat16)
        return carry

    lax.fori_loop(0, LEN_X // rows, part, 0)


def transform_into(out_refs, left_ref, coef_ref, rows_ref, basis_ref):
    for n in range(0, LEN_Y, 256):
        cols = slice(n, n + 256)
        rows_ref[:, cols] = jnp.dot(
            left_ref[...], coef_ref[:, cols], preferred_element_type=jnp.float32
        ).astype(jnp.bfloat16)
    size = rows_ref.shape[0] // len(out_refs)
    for n in range(0, LEN_Y, 256):
        cols = slice(n, n + 256)
        value = contract_last(rows_ref[...], basis_ref[cols, :]).astype(jnp.bfloat16)
        for m, out_ref in enumerate(out_refs):
            out_ref[:, cols] = value[m * size : (m + 1) * size]


def first_planes_kernel(
    scalars, out_ref, basis_out, basis, coef, rows, cos_a, sin_a, cos_b, sin_b, sem, *, depth, count
):
    basis_into(basis, cos_a, sin_a, cos_b, sin_b, LEN_X, 64)
    copy = pltpu.make_async_copy(basis, basis_out, sem)
    copy.start()
    coefficients_into(coef, scalars[0], scalars[1], depth, 64)
    left = basis.at[pl.ds(pl.multiple_of(scalars[2], count), count), :]
    transform_into([out_ref], left, coef, rows, basis)
    copy.wait()


def first_planes(scalars, depth, count):
    return pl.pallas_call(
        functools.partial(first_planes_kernel, depth=depth, count=count),
        in_specs=[pl.BlockSpec(memory_space=pltpu.SMEM)],
        out_specs=[pl.BlockSpec(memory_space=pltpu.VMEM), pl.BlockSpec(memory_space=pl.ANY)],
        out_shape=[
            jax.ShapeDtypeStruct((count, LEN_Y), jnp.bfloat16),
            jax.ShapeDtypeStruct((LEN_X, LEN_X), jnp.bfloat16),
        ],
        scratch_shapes=[
            pltpu.VMEM((LEN_X, LEN_X), jnp.bfloat16),
            pltpu.VMEM((LEN_X, LEN_Y), jnp.bfloat16),
            pltpu.VMEM((count, LEN_Y), jnp.bfloat16),
            pltpu.VMEM((64, LEN_X), jnp.float32),
            pltpu.VMEM((64, LEN_X), jnp.float32),
            pltpu.VMEM((LEN_X // 64, LEN_X), jnp.float32),
            pltpu.VMEM((LEN_X // 64, LEN_X), jnp.float32),
            pltpu.SemaphoreType.DMA,
        ],
        compiler_params=pltpu.CompilerParams(vmem_limit_bytes=VMEM_LIMIT),
        cost_estimate=pl.CostEstimate(flops=25_000_000_000, transcendentals=0, bytes_accessed=8_000_000),
        name="first_planes",
    )(scalars)


def more_planes_kernel(scalars, basis_in, *refs, depth):
    out_refs = refs[:PARTS]
    basis, left, coef, rows, sem = refs[PARTS:]
    size = out_refs[0].shape[0]
    copies = [pltpu.make_async_copy(basis_in, basis, sem.at[PARTS])]
    for n in range(PARTS):
        source = basis_in.at[pl.ds(pl.multiple_of(scalars[2 + n], size), size), :]
        copies.append(pltpu.make_async_copy(source, left.at[pl.ds(n * size, size), :], sem.at[n]))
    for copy in copies:
        copy.start()
    coefficients_into(coef, scalars[0], scalars[1], depth, 64)
    for copy in copies:
        copy.wait()
    transform_into(out_refs, left, coef, rows, basis)


def more_planes(scalars, basis, depth, size):
    return pl.pallas_call(
        functools.partial(more_planes_kernel, depth=depth),
        in_specs=[pl.BlockSpec(memory_space=pltpu.SMEM), pl.BlockSpec(memory_space=pl.ANY)],
        out_specs=[pl.BlockSpec(memory_space=pltpu.VMEM)] * PARTS,
        out_shape=[jax.ShapeDtypeStruct((size, LEN_Y), jnp.bfloat16)] * PARTS,
        scratch_shapes=[
            pltpu.VMEM((LEN_X, LEN_X), jnp.bfloat16),
            pltpu.VMEM((PARTS * size, LEN_X), jnp.bfloat16),
            pltpu.VMEM((LEN_X, LEN_Y), jnp.bfloat16),
            pltpu.VMEM((PARTS * size, LEN_Y), jnp.bfloat16),
            pltpu.SemaphoreType.DMA((PARTS + 1,)),
        ],
        compiler_params=pltpu.CompilerParams(vmem_limit_bytes=VMEM_LIMIT),
        cost_estimate=pl.CostEstimate(flops=20_000_000_000, transcendentals=0, bytes_accessed=8_000_000),
        name="more_planes",
    )(scalars, basis)


def perm_kernel(matrix, *refs):
    out_ref = refs[-1]
    a_ref = refs[0]
    split = a_ref.shape[0] * TILE
    field = jnp.dot(
        matrix[:, :split], a_ref[...].reshape(split, LEN_Y), preferred_element_type=jnp.float32
    )
    rest = jnp.concatenate([ref[...] for ref in refs[1:-1]], axis=0)
    field = field + jnp.dot(matrix[:, split:], rest, preferred_element_type=jnp.float32)
    out_ref[...] = jnp.exp(1.5 * jnp.tanh(2.0 * field)).astype(jnp.bfloat16).reshape(out_ref.shape)


def permeability(matrix, block, planes):
    modes, count, _ = block.shape
    depth = modes + len(planes)
    return pl.pallas_call(
        perm_kernel,
        grid=(count // TILE,),
        in_specs=[
            pl.BlockSpec(matrix.shape, lambda i: (0, 0)),
            pl.BlockSpec((modes, TILE, LEN_Y), lambda i: (0, i, 0)),
        ]
        + [pl.BlockSpec((TILE, LEN_Y), lambda i: (i, 0)) for _ in planes],
        out_specs=pl.BlockSpec((depth, TILE, LEN_Y), lambda i: (0, i, 0)),
        out_shape=jax.ShapeDtypeStruct((depth, count, LEN_Y), jnp.bfloat16),
        compiler_params=pltpu.CompilerParams(vmem_limit_bytes=VMEM_LIMIT),
        cost_estimate=pl.CostEstimate(flops=1_300_000_000, transcendentals=0, bytes_accessed=10_000_000),
        name="permeability",
    )(matrix, block, *planes)


def chebyshev():
    sigma = THETA / DELTA
    rho = 1.0 / sigma
    pairs = []
    for _ in range(ITERS - 1):
        rho_next = 1.0 / (2.0 * sigma - rho)
        pairs.append((rho_next * rho, 2.0 * rho_next / DELTA))
        rho = rho_next
    return pairs


def solve_kernel(
    flags, f_in, f_edge, k_in, k_edge, out_ref, kh, ky, pa, pb, pc, stage, turned, mask, fx, fz, sem_in, sem_out
):
    depth, count, _ = f_in.shape
    padded = kh.shape[1]
    tiles = padded // 8
    rows_in = count + TILE
    blocks = LEN_Y // 128
    chunk = stage.shape[2]
    chunks = depth // chunk

    def copies(c, slot):
        found = []
        for n, (mid, edge) in enumerate(((f_in, f_edge), (k_in, k_edge))):
            at = pl.ds(c * chunk, chunk)
            found.append(
                pltpu.make_async_copy(mid.at[at], stage.at[slot, n, :, pl.ds(0, count), :], sem_in.at[slot, n, 0])
            )
            found.append(
                pltpu.make_async_copy(edge.at[at], stage.at[slot, n, :, pl.ds(count, TILE), :], sem_in.at[slot, n, 1])
            )
        return found

    for copy in copies(0, 0):
        copy.start()

    def padded_row(index):
        return (index & 7) * tiles + (index >> 3)

    row = padded_row(lax.broadcasted_iota(jnp.int32, (padded, rows_in), 0))
    source = jnp.where(row < HALO, row + count, jnp.where(row < HALO + count, row - HALO, row))
    spread = (lax.broadcasted_iota(jnp.int32, (padded, rows_in), 1) == source).astype(jnp.bfloat16)
    place = padded_row(lax.broadcasted_iota(jnp.int32, (count, padded), 1))
    gather = (lax.broadcasted_iota(jnp.int32, (count, padded), 0) + HALO == place).astype(jnp.bfloat16)
    row = padded_row(lax.broadcasted_iota(jnp.int32, (padded, 128), 0))
    outside = ((row < HALO) & (flags[0] == 0)) | ((row >= HALO + count) & (flags[1] == 0))
    mask[...] = jnp.where(outside, 0.0, 1.0)
    lane = lax.broadcasted_iota(jnp.int32, (8, 128), 1)

    def cols(j):
        return slice(j * 128, (j + 1) * 128)

    for c in range(chunks):
        slot = c % 2
        if c + 1 < chunks:
            for copy in copies(c + 1, 1 - slot):
                copy.start()
        for copy in copies(c, slot):
            copy.wait()
        for m in range(chunk):
            z = c * chunk + m
            for n in range(0, LEN_Y, 256):
                pa[z, :, n : n + 256] = jnp.dot(
                    spread, stage[slot, 0, m, :, n : n + 256], preferred_element_type=jnp.float32
                ) * (1.0 / THETA)
                kh[z, :, n : n + 256] = 0.5 * jnp.dot(
                    spread, stage[slot, 1, m, :, n : n + 256], preferred_element_type=jnp.float32
                )

    def faces(n, carry):
        z = n // tiles
        at = pl.ds(pl.multiple_of((n - z * tiles) * 8, 8), 8)
        here = kh[z, at, cols(0)]
        turn = pltpu.roll(here, 127, 1)
        for j in range(blocks):
            if j + 1 < blocks:
                after = kh[z, at, cols(j + 1)]
                after_turn = pltpu.roll(after, 127, 1)
            else:
                after, after_turn = None, 0.0
            ky[z, at, cols(j)] = here + jnp.where(lane == 127, after_turn, turn)
            here, turn = after, after_turn
        return carry

    lax.fori_loop(0, depth * tiles, faces, 0)

    def wrapped(value):
        return pltpu.roll(value, 7, 0)

    def sweep(src, store):
        last = slice(padded - 8, padded)

        def begin(z, carry):
            for j in range(blocks):
                flow = (kh[z, last, cols(j)] + wrapped(kh[z, 0:8, cols(j)])) * (
                    src[z, last, cols(j)] - wrapped(src[z, 0:8, cols(j)])
                )
                fx[z, :, cols(j)] = pltpu.roll(flow, 1, 0)
            return carry

        lax.fori_loop(0, depth, begin, 0)

        def tile(i, wrap):
            at = pl.ds(i * 8, 8) if wrap else pl.ds(pl.multiple_of(i * 8, 8), 8)
            factor = mask[at, :]
            for j in range(blocks):
                fz[:, cols(j)] = -kh[0, at, cols(j)] * src[0, at, cols(j)]

            def level(z, top):
                def beside(ref, j):
                    if wrap:
                        return wrapped(ref[z, 0:8, cols(j)])
                    return ref[z, pl.ds(pl.multiple_of(i * 8 + 8, 8), 8), cols(j)]

                p = src[z, at, cols(0)]
                p_turn = pltpu.roll(p, 127, 1)
                before = None
                for j in range(blocks):
                    k = kh[z, at, cols(j)]
                    if j + 1 < blocks:
                        p_after = src[z, at, cols(j + 1)]
                        p_after_turn = pltpu.roll(p_after, 127, 1)
                    else:
                        p_after, p_after_turn = None, 0.0
                    flow_y = ky[z, at, cols(j)] * (p - jnp.where(lane == 127, p_after_turn, p_turn))
                    flow_turn = pltpu.roll(flow_y, 1, 1)
                    left = jnp.where(lane == 0, -k * p if before is None else before, flow_turn)
                    before = flow_turn
                    if top:
                        flow_z = k * p
                    else:
                        flow_z = (k + kh[z + 1, at, cols(j)]) * (p - src[z + 1, at, cols(j)])
                    flow_x = (k + beside(kh, j)) * (p - beside(src, j))
                    out = (flow_x - fx[z, :, cols(j)]) + (flow_y - left) + (flow_z - fz[:, cols(j)])
                    if not wrap:
                        fx[z, :, cols(j)] = flow_x
                    if not top:
                        fz[:, cols(j)] = flow_z
                    store((z, at, cols(j)), p, out, factor)
                    p, p_turn = p_after, p_after_turn

            def lower(z, carry):
                level(z, False)
                return carry

            lax.fori_loop(0, depth - 1, lower, 0)
            level(depth - 1, True)

        def inner(i, carry):
            tile(i, False)
            return carry

        lax.fori_loop(0, tiles - 1, inner, 0)
        tile(tiles - 1, True)

    (a1, b1), (a2, b2), (a3, b3) = chebyshev()

    def store_one(at, p, out, factor):
        pb[at] = (1.0 + a1 + b1 * THETA) * p - (b1 * factor) * out

    def store_two(at, p, out, factor):
        pc[at] = (1.0 + a2) * p + (b2 * THETA - a2) * pa[at] - (b2 * factor) * out

    def store_three(at, p, out, factor):
        pb[at] = ((1.0 + a3) * p - b3 * out) + (b3 * THETA * pa[at] - a3 * pb[at])

    sweep(pa, store_one)
    sweep(pb, store_two)
    sweep(pc, store_three)

    def leave(z):
        return pltpu.make_async_copy(turned.at[z % 2], out_ref.at[z], sem_out.at[z % 2])

    for z in range(depth):
        if z > 1:
            leave(z - 2).wait()
        for n in range(0, LEN_Y, 256):
            turned[z % 2, :, n : n + 256] = jnp.dot(
                gather, pb[z, :, n : n + 256].astype(jnp.bfloat16), preferred_element_type=jnp.float32
            ).astype(jnp.bfloat16)
        leave(z).start()
    for z in (depth - 2, depth - 1):
        leave(z).wait()


def solve(flags, f, f_edge, k, k_edge):
    depth, count, _ = f.shape
    padded = -(-(count + 2 * HALO) // 8) * 8
    anywhere = pl.BlockSpec(memory_space=pl.ANY)
    whole = pltpu.VMEM((depth, padded, LEN_Y), jnp.float32)
    return pl.pallas_call(
        solve_kernel,
        in_specs=[pl.BlockSpec(memory_space=pltpu.SMEM)] + [anywhere] * 4,
        out_specs=anywhere,
        out_shape=jax.ShapeDtypeStruct((depth, count, LEN_Y), jnp.bfloat16),
        scratch_shapes=[
            whole,
            whole,
            whole,
            whole,
            whole,
            pltpu.VMEM((2, 2, 2, count + TILE, LEN_Y), jnp.bfloat16),
            pltpu.VMEM((2, count, LEN_Y), jnp.bfloat16),
            pltpu.VMEM((padded, 128), jnp.float32),
            pltpu.VMEM((depth, 8, LEN_Y), jnp.float32),
            pltpu.VMEM((8, LEN_Y), jnp.float32),
            pltpu.SemaphoreType.DMA((2, 2, 2)),
            pltpu.SemaphoreType.DMA((2,)),
        ],
        compiler_params=pltpu.CompilerParams(vmem_limit_bytes=VMEM_LIMIT),
        name="solve",
    )(flags, f, f_edge, k, k_edge)


def edges(block):
    forward = [(i, i + 1) for i in range(WIDE - 1)]
    backward = [(target, source) for source, target in forward]
    low = lax.ppermute(block[:, -HALO:], "wide", forward)
    high = lax.ppermute(block[:, :HALO], "wide", backward)
    return jnp.pad(jnp.concatenate([low, high], axis=1), ((0, 0), (0, TILE - 2 * HALO), (0, 0)))


def basis_columns(modes, length):
    row_idx = lax.broadcasted_iota(jnp.int32, (length, length), 0)
    phase = (2 * row_idx + 1) * modes[None, :] % (4 * length)
    angle = phase.astype(jnp.float32) * (math.pi / (2.0 * length))
    weights = jnp.where(modes[None, :] == 0, math.sqrt(1.0 / length), math.sqrt(2.0 / length))
    return (weights * jnp.cos(angle)).astype(jnp.bfloat16)


def body(stream_index, forcing):
    depth, count, _ = forcing.shape
    index = lax.axis_index("wide")
    core = index & 1
    color = (index >> 1 ^ index >> 2) & 1
    key = scramble(stream_index[0] ^ 1540483477)
    shared = DEPTH // 2 + 4 * color + 2 * core

    scalars = jnp.stack([key, index & 7, (index >> 3) * (8 * count)]).astype(jnp.int32)
    first, basis = first_planes(scalars, depth, 8 * count)
    groups = [list(range(8)), list(range(8, 16))]
    block = lax.all_to_all(
        first.reshape(8, count, LEN_Y), "wide", 0, 0, axis_index_groups=groups, tiled=True
    )

    def pairwise(mode, bit):
        flips = (0, 1, bit, bit ^ 1)
        scalars = jnp.stack([key, mode] + [(index ^ flip) * count for flip in flips]).astype(jnp.int32)
        out = more_planes(scalars, basis, depth, count)
        return [out[0]] + [
            lax.ppermute(piece, "wide", [(i, i ^ flip) for i in range(WIDE)])
            for piece, flip in zip(out[1:], flips[1:])
        ]

    planes = pairwise(shared, 4) + pairwise(shared + 1, 2)
    half = DEPTH // 2
    shared_modes = jnp.stack(
        [half + 4 * (color ^ b) + 2 * (core ^ c) + a for a in (0, 1) for b in (0, 1) for c in (0, 1)]
    )
    modes = jnp.concatenate([jnp.arange(half, dtype=jnp.int32), shared_modes])
    basis_z = basis_columns(modes, depth)
    eye = jnp.eye(TILE, dtype=jnp.bfloat16)
    mixing = (basis_z[:, None, :, None] * eye[None, :, None, :]).reshape(depth * TILE, depth * TILE)
    perm = permeability(mixing, block, planes)
    flags = jnp.stack([index > 0, index < WIDE - 1]).astype(jnp.int32)
    return solve(flags, forcing, edges(forcing), perm, edges(perm))


def solution(mesh):
    special = mesh.shape["wide"] == WIDE
    return jax.shard_map(
        body if special else plain_body,
        mesh=mesh,
        in_specs=(P("group"), P("group", "wide", None)),
        out_specs=P("group", "wide", None),
        check_vma=False,
    )
```

```python
import functools
import math

import jax
import jax.numpy as jnp
from jax import lax
from jax.experimental import pallas as pl
from jax.experimental.pallas import tpu as pltpu
from jax.sharding import PartitionSpec as P

LEN_X = 1536
LEN_Y = 1536
ITERS = 4


def with_halo(block, sides, width):
    for axis, dim in sides:
        count = lax.axis_size(axis)
        forward = [(i, i + 1) for i in range(count - 1)]
        backward = [(target, source) for source, target in forward]
        low = lax.ppermute(
            lax.slice_in_dim(block, block.shape[dim] - width, None, axis=dim), axis, forward
        )
        high = lax.ppermute(lax.slice_in_dim(block, 0, width, axis=dim), axis, backward)
        block = jnp.concatenate([low, block, high], axis=dim)
    return block


def scramble(value):
    value = value ^ value >> 16 & 65535
    value = value * 73244475
    value = value ^ value >> 16 & 65535
    value = value * 73244475
    value = value ^ value >> 16 & 65535
    return value


def cosine_basis(length):
    row_idx = lax.broadcasted_iota(jnp.int32, (length, length), 0)
    mode_idx = lax.broadcasted_iota(jnp.int32, (length, length), 1)
    phase = (2 * row_idx + 1) * mode_idx % (4 * length)
    angle = phase.astype(jnp.float32) * (math.pi / (2.0 * length))
    weights = jnp.where(mode_idx == 0, math.sqrt(1.0 / length), math.sqrt(2.0 / length))
    return (weights * jnp.cos(angle)).astype(jnp.bfloat16)


def coefficient_plane(stream_key, mode_z, depth):
    mode_x = lax.broadcasted_iota(jnp.int32, (LEN_X, LEN_Y), 0)
    mode_y = lax.broadcasted_iota(jnp.int32, (LEN_X, LEN_Y), 1)
    counter = (mode_z * LEN_X + mode_x) * LEN_Y + mode_y
    bits_a = scramble(2 * counter ^ stream_key)
    bits_b = scramble(2 * counter + 1 ^ stream_key)
    uniform_a = (bits_a >> 8 & 16777215).astype(jnp.float32) * 2.0 ** (-24) + 2.0 ** (-25)
    uniform_b = (bits_b >> 8 & 16777215).astype(jnp.float32) * 2.0 ** (-24) + 2.0 ** (-25)
    noise = jnp.sqrt(-2.0 * jnp.log(uniform_a)) * jnp.cos(2.0 * math.pi * uniform_b)
    freq_x = mode_x.astype(jnp.float32) * (math.pi / LEN_X)
    freq_y = mode_y.astype(jnp.float32) * (math.pi / LEN_Y)
    freq_z = mode_z.astype(jnp.float32) * (math.pi / depth)
    amplitude = 1.0 / jnp.sqrt(0.05 + freq_x * freq_x + freq_y * freq_y + freq_z * freq_z)
    return (amplitude * noise).astype(jnp.bfloat16)


def contract_last(left, table):
    return lax.dot_general(
        left, table, (((left.ndim - 1,), (1,)), ((), ())), preferred_element_type=jnp.float32
    )


def operate(wide_p, wide_k):
    center_p = wide_p[:, 1:-1]
    center_k = wide_k[:, 1:-1]
    total = 0.5 * (center_k + wide_k[:, 2:]) * (center_p - wide_p[:, 2:])
    total = total + 0.5 * (center_k + wide_k[:, :-2]) * (center_p - wide_p[:, :-2])
    for axis in (0, 2):
        widths = [(0, 0), (0, 0), (0, 0)]
        widths[axis] = (1, 1)
        padded_p = jnp.pad(center_p, widths)
        padded_k = jnp.pad(center_k, widths)
        size_here = center_p.shape[axis]
        for start in (0, 2):
            near_p = lax.slice_in_dim(padded_p, start, start + size_here, axis=axis)
            near_k = lax.slice_in_dim(padded_k, start, start + size_here, axis=axis)
            total = total + 0.5 * (center_k + near_k) * (center_p - near_p)
    return total


def plain_body(stream_index, forcing):
    depth = forcing.shape[0]
    planes_here = depth // lax.axis_size("wide")
    stream_key = scramble(stream_index[0] ^ 1540483477)
    basis_x = cosine_basis(LEN_X)
    basis_y = cosine_basis(LEN_Y)
    basis_z = cosine_basis(depth)
    first_mode = lax.axis_index("wide") * planes_here
    own_modes = first_mode + jnp.arange(planes_here, dtype=jnp.int32)

    def rows_for(mode_z):
        coeff = coefficient_plane(stream_key, mode_z, depth)
        return jnp.dot(basis_x, coeff, preferred_element_type=jnp.float32).astype(jnp.bfloat16)

    def both_axes(mode_z):
        return contract_last(rows_for(mode_z), basis_y).astype(jnp.bfloat16)

    planes = lax.map(both_axes, own_modes)
    block = lax.all_to_all(planes, "wide", split_axis=1, concat_axis=0, tiled=True)
    count_z, count_x, count_y = block.shape
    field = jnp.dot(
        basis_z, block.reshape(count_z, count_x * count_y), preferred_element_type=jnp.float32
    )
    field = field.reshape(count_z, count_x, count_y)
    perm = jnp.exp(1.5 * jnp.tanh(2.0 * field))
    source = forcing.astype(jnp.float32)
    theta = 27.9
    delta = 26.1
    sigma = theta / delta
    rho = 1.0 / sigma
    step = source / theta
    press = step
    perm_wide = with_halo(perm.astype(jnp.bfloat16), (("wide", 1),), 1).astype(perm.dtype)
    for count in range(ITERS - 1):
        press_wide = with_halo(press, (("wide", 1),), 1)
        resid = source - operate(press_wide, perm_wide)
        rho_next = 1.0 / (2.0 * sigma - rho)
        step = rho_next * rho * step + 2.0 * rho_next / delta * resid
        press = press + step
        rho = rho_next
    return press.astype(jnp.bfloat16)


WIDE = 16
DEPTH = 16
HALO = ITERS - 1
PARTS = 4
UNROLL = 2
TILE = 16
FOLD = 16
VMEM_LIMIT = 60 << 20
THETA = 27.9
DELTA = 26.1
SIN_PI = (
    3.141592640144167, -5.16771008404795, 2.550077528430638, -0.5982912997813382, 0.077657661199004
)
MULT = 73244475


def cos_turns(turns, amplitude, negative=False):
    coeffs = [c * math.sqrt(2.0 * amplitude) for c in SIN_PI]
    square = turns * turns
    poly = coeffs[4] * square + coeffs[3]
    for c in coeffs[2::-1]:
        poly = poly * square + c
    sine = poly * turns
    return sine * sine - amplitude if negative else amplitude - sine * sine


def turns_of(phase, period):
    return (phase - jnp.floor(phase * (1.0 / period) + 0.5) * period) * (1.0 / period)


def srl(value, count):
    return lax.shift_right_logical(value, jnp.int32(count))


def angle_tables(cos_out, sin_out, of_row, length, weighted):
    period = 4.0 * length

    def part(i, carry):
        r = lax.broadcasted_iota(jnp.int32, (8, 128), 0) + i * 8
        factor = of_row(r).astype(jnp.float32)
        at = pl.ds(pl.multiple_of(i * 8, 8), 8)
        for j in range(length // 128):
            k = lax.broadcasted_iota(jnp.int32, (8, 128), 1).astype(jnp.float32) + 128.0 * j
            phase = factor * k
            cosine = cos_turns(turns_of(phase, period), 1.0)
            sine = cos_turns(turns_of(phase - length, period), 1.0)
            if weighted:
                weight = jnp.where(k == 0.0, math.sqrt(1.0 / length), math.sqrt(2.0 / length))
                cosine = cosine * weight
                sine = sine * weight
            cos_out[at, j * 128 : (j + 1) * 128] = cosine
            sin_out[at, j * 128 : (j + 1) * 128] = sine
        return carry

    lax.fori_loop(0, cos_out.shape[0] // 8, part, 0)


def basis_into(out_ref, small, big):
    rows = small[0].shape[0]
    length = out_ref.shape[1]
    angle_tables(*small, lambda r: 2 * r + 1, length, True)
    angle_tables(*big, lambda t: 2 * rows * t, length, False)

    def group(g, carry):
        group_at = pl.ds(pl.multiple_of(g * 8, 8), 8)
        for j in range(length // 128):
            cols = slice(j * 128, (j + 1) * 128)
            big_cos = big[0][group_at, cols]
            big_sin = big[1][group_at, cols]
            for t in range(8):
                at = pl.ds(pl.multiple_of((g * 8 + t) * rows, rows), rows)
                value = small[0][:, cols] * big_cos[t : t + 1] - small[1][:, cols] * big_sin[t : t + 1]
                out_ref[at, cols] = value.astype(jnp.bfloat16)
        return carry

    lax.fori_loop(0, big[0].shape[0] // 8, group, 0)


def folded_basis_into(out_ref, small, big, first_row, count, tiles):
    length = out_ref.shape[1]

    def block_row(r):
        return 2 * (first_row + r // FOLD * count - HALO + r % FOLD * tiles) + 1

    angle_tables(*small, block_row, length, True)
    angle_tables(*big, lambda i: 2 * i, length, False)

    def device(d, carry):
        at = pl.ds(pl.multiple_of(d * FOLD, FOLD), FOLD)
        for i in range(tiles):
            to = pl.ds(pl.multiple_of((d * tiles + i) * FOLD, FOLD), FOLD)
            for j in range(length // 128):
                cols = slice(j * 128, (j + 1) * 128)
                value = small[0][at, cols] * big[0][i : i + 1, cols] - small[1][at, cols] * big[1][i : i + 1, cols]
                out_ref[to, cols] = value.astype(jnp.bfloat16)
        return carry

    lax.fori_loop(0, small[0].shape[0] // FOLD, device, 0)


def coefficients_into(out_ref, key, mode_z, depth, rows):
    const = 2.0 * math.log(2.0)
    key_low = key & 1023
    key_high = key & ~1023

    def part(i, carry):
        r = lax.broadcasted_iota(jnp.int32, (rows, 128), 0) + i * rows
        at = pl.ds(pl.multiple_of(i * rows, rows), rows)
        freq_x = r.astype(jnp.float32) * (math.pi / LEN_X)
        freq_z = mode_z.astype(jnp.float32) * (math.pi / depth)
        row_part = (0.05 + freq_x * freq_x + freq_z * freq_z) * -const
        base = (r + mode_z * LEN_X) * (2 * LEN_Y)
        lane = lax.broadcasted_iota(jnp.int32, (1, 128), 1)
        for j in range(LEN_Y // 128):
            if j % 4 == 0:
                top = (base + j * 256) ^ key_high
                top = top ^ srl(top, 16)
                delta = jnp.where(((top ^ key_low) & 1) == 0, MULT, -MULT)
            freq_y = (lane + j * 128).astype(jnp.float32) * (math.pi / LEN_Y)
            denom = row_part + freq_y * freq_y * -const
            a = (top ^ (((lane + (j % 4) * 128) * 2) ^ key_low)) * MULT
            b = a + delta
            a = (a ^ srl(a, 16)) * MULT
            b = (b ^ srl(b, 16)) * MULT
            a = srl(a ^ srl(a, 16), 8)
            b = (b ^ srl(b, 16)) >> 8
            u = a.astype(jnp.float32) * 2.0 ** (-24) + 2.0 ** (-25)
            turns = b.astype(jnp.float32) * 2.0 ** (-24) + 2.0 ** (-25)
            bits = jnp.minimum(jnp.log2(u), -1e-30)
            size = bits * lax.rsqrt(bits * denom)
            value = size * cos_turns(turns, const, negative=True)
            out_ref[at, j * 128 : (j + 1) * 128] = value.astype(jnp.bfloat16)
        return carry

    lax.fori_loop(0, LEN_X // rows, part, 0)


def transform_into(out_refs, left_ref, coef_ref, rows_ref, basis_ref):
    for n in range(0, LEN_Y, 256):
        cols = slice(n, n + 256)
        rows_ref[:, cols] = jnp.dot(
            left_ref[...], coef_ref[:, cols], preferred_element_type=jnp.float32
        ).astype(jnp.bfloat16)
    size = rows_ref.shape[0] // len(out_refs)
    for n in range(0, LEN_Y, 256):
        cols = slice(n, n + 256)
        value = contract_last(rows_ref[...], basis_ref[cols, :])
        for m, out_ref in enumerate(out_refs):
            out_ref[:, cols] = value[m * size : (m + 1) * size].astype(jnp.bfloat16)


def first_planes_kernel(
    scalars, out_ref, basis_out, folded_out, basis, folded, coef, rows, small_cos, small_sin, big_cos, big_sin, sem,
    *, depth, count, tiles
):
    key, index = scalars[0], scalars[1]
    basis_into(basis, (small_cos.at[pl.ds(0, 64)], small_sin.at[pl.ds(0, 64)]), (big_cos, big_sin))
    folded_basis_into(
        folded,
        (small_cos, small_sin),
        (big_cos.at[pl.ds(0, 8)], big_sin.at[pl.ds(0, 8)]),
        (index >> 3) * (8 * count),
        count,
        tiles,
    )
    copies = [
        pltpu.make_async_copy(basis, basis_out, sem.at[0]),
        pltpu.make_async_copy(folded, folded_out, sem.at[1]),
    ]
    for copy in copies:
        copy.start()
    coefficients_into(coef, key, index & 7, depth, 64)
    transform_into([out_ref], folded, coef, rows, basis)
    for copy in copies:
        copy.wait()


def first_planes(scalars, depth, count, tiles):
    total = 8 * tiles * FOLD
    bits = jnp.bfloat16
    return pl.pallas_call(
        functools.partial(first_planes_kernel, depth=depth, count=count, tiles=tiles),
        in_specs=[pl.BlockSpec(memory_space=pltpu.SMEM)],
        out_specs=[pl.BlockSpec(memory_space=pltpu.VMEM)] + [pl.BlockSpec(memory_space=pl.ANY)] * 2,
        out_shape=[
            jax.ShapeDtypeStruct((total, LEN_Y), bits),
            jax.ShapeDtypeStruct((LEN_X, LEN_X), bits),
            jax.ShapeDtypeStruct((total, LEN_X), bits),
        ],
        scratch_shapes=[
            pltpu.VMEM((LEN_X, LEN_X), bits),
            pltpu.VMEM((total, LEN_X), bits),
            pltpu.VMEM((LEN_X, LEN_Y), bits),
            pltpu.VMEM((total, LEN_Y), bits),
            pltpu.VMEM((8 * FOLD, LEN_X), jnp.float32),
            pltpu.VMEM((8 * FOLD, LEN_X), jnp.float32),
            pltpu.VMEM((LEN_X // 64, LEN_X), jnp.float32),
            pltpu.VMEM((LEN_X // 64, LEN_X), jnp.float32),
            pltpu.SemaphoreType.DMA((2,)),
        ],
        compiler_params=pltpu.CompilerParams(vmem_limit_bytes=VMEM_LIMIT),
        cost_estimate=pl.CostEstimate(flops=25_000_000_000, transcendentals=0, bytes_accessed=8_000_000),
        name="first_planes",
    )(scalars)


def shared_mode(index, depth):
    color = (index >> 1 ^ index >> 2) & 1
    return depth // 2 + 4 * color + 2 * (index & 1)


def more_planes_kernel(scalars, basis_in, folded_in, *refs, depth, flips, offset):
    out_refs = refs[:PARTS]
    basis, left, coef, rows, sem = refs[PARTS:]
    size = out_refs[0].shape[0]
    key, index = scalars[0], scalars[1]
    mode = shared_mode(index, depth) + offset
    copies = [pltpu.make_async_copy(basis_in, basis, sem.at[PARTS])]
    for n, flip in enumerate(flips):
        source = folded_in.at[pl.ds(pl.multiple_of((index & 7 ^ flip) * size, size), size), :]
        copies.append(pltpu.make_async_copy(source, left.at[pl.ds(n * size, size), :], sem.at[n]))
    for copy in copies:
        copy.start()
    coefficients_into(coef, key, mode, depth, 64)
    for copy in copies:
        copy.wait()
    transform_into(out_refs, left, coef, rows, basis)


def more_planes(scalars, basis, folded, depth, size, flips, offset):
    anywhere = pl.BlockSpec(memory_space=pl.ANY)
    return pl.pallas_call(
        functools.partial(more_planes_kernel, depth=depth, flips=flips, offset=offset),
        in_specs=[pl.BlockSpec(memory_space=pltpu.SMEM), anywhere, anywhere],
        out_specs=[pl.BlockSpec(memory_space=pltpu.VMEM)] * PARTS,
        out_shape=[jax.ShapeDtypeStruct((size, LEN_Y), jnp.bfloat16)] * PARTS,
        scratch_shapes=[
            pltpu.VMEM((LEN_X, LEN_X), jnp.bfloat16),
            pltpu.VMEM((PARTS * size, LEN_X), jnp.bfloat16),
            pltpu.VMEM((LEN_X, LEN_Y), jnp.bfloat16),
            pltpu.VMEM((PARTS * size, LEN_Y), jnp.bfloat16),
            pltpu.SemaphoreType.DMA((PARTS + 1,)),
        ],
        compiler_params=pltpu.CompilerParams(vmem_limit_bytes=VMEM_LIMIT),
        cost_estimate=pl.CostEstimate(flops=20_000_000_000, transcendentals=0, bytes_accessed=8_000_000),
        name="more_planes",
    )(scalars, basis, folded)


def folded_row(index, tiles):
    return index % FOLD * tiles + index // FOLD


def fold_kernel(f_ref, low_ref, high_ref, out_ref, edge):
    _, count, _ = f_ref.shape
    padded = out_ref.shape[1]
    shape = (padded, count + TILE)
    row = folded_row(lax.broadcasted_iota(jnp.int32, shape, 0), padded // FOLD)
    source = jnp.where(row < HALO, row + count, jnp.where(row < HALO + count, row - HALO, row))
    spread = (lax.broadcasted_iota(jnp.int32, shape, 1) == source).astype(jnp.bfloat16)

    @pl.when(pl.program_id(0) == 0)
    def _():
        edge[...] = jnp.zeros(edge.shape, edge.dtype)

    for m in range(f_ref.shape[0]):
        edge[0:HALO, :] = low_ref[m]
        edge[HALO : 2 * HALO, :] = high_ref[m]
        rows = jnp.concatenate([f_ref[m], edge[...]], axis=0)
        for n in range(0, LEN_Y, 512):
            cols = slice(n, n + 512)
            out_ref[m, :, cols] = jnp.dot(spread, rows[:, cols], preferred_element_type=jnp.float32).astype(
                jnp.bfloat16
            )


def fold(forcing, low, high, padded):
    depth, count, _ = forcing.shape
    return pl.pallas_call(
        fold_kernel,
        grid=(depth // 2,),
        in_specs=[
            pl.BlockSpec((2, count, LEN_Y), lambda z: (z, 0, 0)),
            pl.BlockSpec((2, HALO, LEN_Y), lambda z: (z, 0, 0)),
            pl.BlockSpec((2, HALO, LEN_Y), lambda z: (z, 0, 0)),
        ],
        out_specs=pl.BlockSpec((2, padded, LEN_Y), lambda z: (z, 0, 0)),
        out_shape=jax.ShapeDtypeStruct((depth, padded, LEN_Y), jnp.bfloat16),
        scratch_shapes=[pltpu.VMEM((TILE, LEN_Y), jnp.bfloat16)],
        compiler_params=pltpu.CompilerParams(vmem_limit_bytes=VMEM_LIMIT),
        cost_estimate=pl.CostEstimate(flops=1_300_000_000, transcendentals=0, bytes_accessed=10_000_000),
        name="fold",
    )(forcing, low, high)


def chebyshev():
    sigma = THETA / DELTA
    rho = 1.0 / sigma
    pairs = []
    for _ in range(ITERS - 1):
        rho_next = 1.0 / (2.0 * sigma - rho)
        pairs.append((rho_next * rho, 2.0 * rho_next / DELTA))
        rho = rho_next
    return pairs


def solve_kernel(scalars, slot_modes, forcing, block, *refs):
    planes = refs[:-12]
    out_ref, k_ref, f_ref, p_two, p_three, b_two, b_three, natural, stage, turned, sems, sem_out = refs[-12:]
    modes = block.shape[0]
    depth, padded, _ = k_ref.shape
    count = out_ref.shape[1]
    tiles = padded // FOLD
    blocks = LEN_Y // 128
    index = scalars[1]

    def cols(j):
        return slice(j * 128, (j + 1) * 128)

    def copies(t, slot):
        at = pl.ds(t * FOLD, FOLD)
        found = [pltpu.make_async_copy(block.at[:, at, :], stage.at[slot, pl.ds(0, modes)], sems.at[slot, 0])]
        for n, plane in enumerate(planes):
            found.append(pltpu.make_async_copy(plane.at[at, :], stage.at[slot, modes + n], sems.at[slot, n + 1]))
        return found

    for copy in copies(0, 0):
        copy.start()
    forcing_copy = pltpu.make_async_copy(forcing, f_ref, sems.at[2, 0])

    size = depth * FOLD
    row = lax.broadcasted_iota(jnp.int32, (size, size), 0)
    col = lax.broadcasted_iota(jnp.int32, (size, size), 1)
    mode = jnp.broadcast_to(slot_modes[...], (size, size))
    phase = ((2 * (row // FOLD) + 1) * mode).astype(jnp.float32)
    weight = jnp.where(mode == 0, math.sqrt(1.0 / depth), math.sqrt(2.0 / depth))
    cosine = cos_turns(turns_of(phase, 4.0 * depth), 1.0)
    mixing = jnp.where(row % FOLD == col % FOLD, weight * cosine, 0.0).astype(jnp.bfloat16)

    def inside(start):
        row = folded_row(lax.broadcasted_iota(jnp.int32, (FOLD, 128), 0) + start, tiles)
        outside = ((row < HALO) & (index == 0)) | ((row >= HALO + count) & (index == WIDE - 1))
        return jnp.where(outside, 0.0, 1.0)

    for t in range(tiles):
        slot = t % 2
        if t + 1 < tiles:
            for copy in copies(t + 1, 1 - slot):
                copy.start()
        else:
            forcing_copy.start()
        for copy in copies(t, slot):
            copy.wait()
        keep = inside(t * FOLD)
        for n in range(0, LEN_Y, 512):
            field = jnp.dot(
                mixing,
                stage[slot, :, :, n : n + 512].reshape(size, 512),
                preferred_element_type=jnp.float32,
            ).reshape(depth, FOLD, 512)
            for j in range(n // 128, n // 128 + 4):
                part = field[:, :, j * 128 - n : j * 128 - n + 128]
                value = jnp.exp(1.5 * jnp.tanh(2.0 * part)) * keep[None]
                k_ref[:, t * FOLD : t * FOLD + FOLD, cols(j)] = value.astype(jnp.bfloat16)
    forcing_copy.wait()
    lane = lax.broadcasted_iota(jnp.int32, (FOLD, 128), 1)
    nothing = jnp.zeros((FOLD, 128), jnp.bfloat16)

    def sweep(src, store):
        def tile(i, below, above):
            at = pl.ds(pl.multiple_of(i * FOLD, FOLD), FOLD)
            factor = inside(i * FOLD)

            def level(z, top, flows_z):
                outs = []
                next_flows = []
                k_all = [k_ref[z, at, cols(j)] for j in range(blocks)]
                p_all = [src[z, at, cols(j)] for j in range(blocks)]
                turns = [pltpu.roll(p, 127, 1) for p in p_all] + [nothing]
                k_turns = [pltpu.roll(k, 127, 1) for k in k_all] + [nothing]
                before = None
                for j in range(blocks):
                    k, p = k_all[j], p_all[j]
                    k_right = jnp.where(lane == 127, k_turns[j + 1], k_turns[j])
                    flow_y = (k + k_right) * (p - jnp.where(lane == 127, turns[j + 1], turns[j]))
                    flow_turn = pltpu.roll(flow_y, 1, 1)
                    left = jnp.where(lane == 0, -k * p if before is None else before, flow_turn)
                    before = flow_turn
                    if top:
                        flow_z = k * p
                    else:
                        flow_z = (k + k_ref[z + 1, at, cols(j)]) * (p - src[z + 1, at, cols(j)])
                    flow_x = (k + above(k_ref, z, j)) * (p - above(src, z, j))
                    flow_w = (k + below(k_ref, z, j)) * (p - below(src, z, j))
                    outs.append((flow_x + flow_w) + ((flow_y - left) + (flow_z - flows_z[j])))
                    next_flows.append(flow_z)
                for j in range(blocks):
                    store(z, i, j, at, outs[j].astype(jnp.float32), factor)
                return next_flows

            def group(g, flows_z):
                for u in range(UNROLL):
                    flows_z = level(g * UNROLL + u, False, flows_z)
                return flows_z

            flows = [-k_ref[0, at, cols(j)] * src[0, at, cols(j)] for j in range(blocks)]
            groups = depth // UNROLL - 1
            flows = lax.fori_loop(0, groups, group, flows)
            for u in range(UNROLL):
                z = groups * UNROLL + u
                flows = level(z, z == depth - 1, flows)

        def plain(step):
            def load(ref, z, j, i):
                return ref[z, pl.ds(pl.multiple_of((i + step) * FOLD, FOLD), FOLD), cols(j)]

            return load

        def first(ref, z, j):
            return pltpu.roll(ref[z, padded - FOLD : padded, cols(j)], 1, 0)

        def last(ref, z, j):
            return pltpu.roll(ref[z, 0:FOLD, cols(j)], FOLD - 1, 0)

        def inner(i, carry):
            tile(
                i,
                lambda ref, z, j: plain(-1)(ref, z, j, i),
                lambda ref, z, j: plain(1)(ref, z, j, i),
            )
            return carry

        tile(0, first, lambda ref, z, j: plain(1)(ref, z, j, 0))
        lax.fori_loop(1, tiles - 1, inner, 0)
        tile(tiles - 1, lambda ref, z, j: plain(-1)(ref, z, j, tiles - 1), last)

    (a1, b1), (a2, b2), (a3, b3) = chebyshev()

    def store_one(z, i, j, at, out, factor):
        source = f_ref[z, at, cols(j)].astype(jnp.float32)
        value = ((1.0 + a1) / THETA + b1) * source - (0.5 * b1 / THETA * factor) * out
        p_two[z, at, cols(j)] = value
        b_two[z, at, cols(j)] = value.astype(jnp.bfloat16)

    def store_two(z, i, j, at, out, factor):
        source = f_ref[z, at, cols(j)].astype(jnp.float32)
        value = (1.0 + a2) * p_two[z, at, cols(j)] + (b2 - a2 / THETA) * source - (0.5 * b2 * factor) * out
        p_three[z, at, cols(j)] = value
        b_three[z, at, cols(j)] = value.astype(jnp.bfloat16)

    def store_three(z, i, j, at, out, factor):
        source = f_ref[z, at, cols(j)].astype(jnp.float32)
        old = (1.0 + a3) * p_three[z, at, cols(j)] - a3 * p_two[z, at, cols(j)]
        value = old + (b3 * source - 0.5 * b3 * out)
        for n in range(FOLD // 8):
            to = pl.ds(i + 8 - HALO + 8 * n * tiles, 8, stride=tiles)
            natural[z * blocks + j, to, :] = value[8 * n : 8 * n + 8]

    sweep(f_ref, store_one)
    sweep(b_two, store_two)
    sweep(b_three, store_three)

    def leave(z, slot):
        return pltpu.make_async_copy(turned.at[slot], out_ref.at[z], sem_out.at[slot])

    for z in range(depth):
        slot = z % 2
        if z > 1:
            leave(z - 2, slot).wait()
        for j in range(blocks):
            turned[slot, :, cols(j)] = natural[z * blocks + j, 8 : 8 + count, :].astype(jnp.bfloat16)
        leave(z, slot).start()
    for z in (depth - 2, depth - 1):
        leave(z, z % 2).wait()


def solve(scalars, slot_modes, forcing, block, planes, count):
    depth, padded, _ = forcing.shape
    anywhere = pl.BlockSpec(memory_space=pl.ANY)
    narrow = pltpu.VMEM((depth, padded, LEN_Y), jnp.bfloat16)
    whole = pltpu.VMEM((depth, padded, LEN_Y), jnp.float32)
    return pl.pallas_call(
        solve_kernel,
        in_specs=[pl.BlockSpec(memory_space=pltpu.SMEM), pl.BlockSpec(memory_space=pltpu.VMEM)]
        + [anywhere] * (2 + len(planes)),
        out_specs=anywhere,
        out_shape=jax.ShapeDtypeStruct((depth, count, LEN_Y), jnp.bfloat16),
        scratch_shapes=[
            narrow,
            narrow,
            whole,
            whole,
            narrow,
            narrow,
            pltpu.VMEM((depth * LEN_Y // 128, padded + 8, 128), jnp.float32),
            pltpu.VMEM((2, depth, FOLD, LEN_Y), jnp.bfloat16),
            pltpu.VMEM((2, count, LEN_Y), jnp.bfloat16),
            pltpu.SemaphoreType.DMA((3, 1 + len(planes))),
            pltpu.SemaphoreType.DMA((2,)),
        ],
        compiler_params=pltpu.CompilerParams(vmem_limit_bytes=VMEM_LIMIT),
        name="solve",
    )(scalars, slot_modes, forcing, block, *planes)


def body(stream_index, forcing):
    depth, count, _ = forcing.shape
    index = lax.axis_index("wide")
    scalars = jnp.stack([scramble(stream_index[0] ^ 1540483477), index]).astype(jnp.int32)
    tiles = -(-(count + 2 * HALO) // FOLD)
    padded = tiles * FOLD
    own, basis, folded = first_planes(scalars, depth, count, tiles)
    groups = [list(range(8)), list(range(8, 16))]
    block = lax.all_to_all(
        own.reshape(8, padded, LEN_Y), "wide", 0, 0, axis_index_groups=groups, tiled=True
    )

    def pairwise(offset, bit):
        flips = (0, 1, bit, bit ^ 1)
        out = more_planes(scalars, basis, folded, depth, padded, flips, offset)
        return [out[0]] + [
            lax.ppermute(piece, "wide", [(i, i ^ flip) for i in range(WIDE)])
            for piece, flip in zip(out[1:], flips[1:])
        ]

    planes = pairwise(0, 4) + pairwise(1, 2)
    slot = lax.broadcasted_iota(jnp.int32, (1, depth * FOLD), 1) // FOLD
    flip = jnp.where(slot < 12, (slot & 1) ^ (slot & 2) << 1, (slot & 1) ^ (slot & 2))
    slot_modes = jnp.where(slot < 8, slot, shared_mode(index ^ flip, depth) + (slot >= 12))
    forward = [(i, i + 1) for i in range(WIDE - 1)]
    backward = [(target, source) for source, target in forward]
    low = lax.ppermute(forcing[:, -HALO:], "wide", forward)
    high = lax.ppermute(forcing[:, :HALO], "wide", backward)
    return solve(scalars, slot_modes, fold(forcing, low, high, padded), block, planes, count)


def solution(mesh):
    special = mesh.shape["wide"] == WIDE
    return jax.shard_map(
        body if special else plain_body,
        mesh=mesh,
        in_specs=(P("group"), P("group", "wide", None)),
        out_specs=P("group", "wide", None),
        check_vma=False,
    )
```

```python
import functools
import math

import jax
import jax.numpy as jnp
from jax import lax
from jax.experimental import pallas as pl
from jax.experimental.pallas import tpu as pltpu
from jax.sharding import PartitionSpec as P

LEN_X = 1536
LEN_Y = 1536
ITERS = 4


def with_halo(block, sides, width):
    for axis, dim in sides:
        count = lax.axis_size(axis)
        forward = [(i, i + 1) for i in range(count - 1)]
        backward = [(target, source) for source, target in forward]
        low = lax.ppermute(
            lax.slice_in_dim(block, block.shape[dim] - width, None, axis=dim), axis, forward
        )
        high = lax.ppermute(lax.slice_in_dim(block, 0, width, axis=dim), axis, backward)
        block = jnp.concatenate([low, block, high], axis=dim)
    return block


def scramble(value):
    value = value ^ value >> 16 & 65535
    value = value * 73244475
    value = value ^ value >> 16 & 65535
    value = value * 73244475
    value = value ^ value >> 16 & 65535
    return value


def cosine_basis(length):
    row_idx = lax.broadcasted_iota(jnp.int32, (length, length), 0)
    mode_idx = lax.broadcasted_iota(jnp.int32, (length, length), 1)
    phase = (2 * row_idx + 1) * mode_idx % (4 * length)
    angle = phase.astype(jnp.float32) * (math.pi / (2.0 * length))
    weights = jnp.where(mode_idx == 0, math.sqrt(1.0 / length), math.sqrt(2.0 / length))
    return (weights * jnp.cos(angle)).astype(jnp.bfloat16)


def coefficient_plane(stream_key, mode_z, depth):
    mode_x = lax.broadcasted_iota(jnp.int32, (LEN_X, LEN_Y), 0)
    mode_y = lax.broadcasted_iota(jnp.int32, (LEN_X, LEN_Y), 1)
    counter = (mode_z * LEN_X + mode_x) * LEN_Y + mode_y
    bits_a = scramble(2 * counter ^ stream_key)
    bits_b = scramble(2 * counter + 1 ^ stream_key)
    uniform_a = (bits_a >> 8 & 16777215).astype(jnp.float32) * 2.0 ** (-24) + 2.0 ** (-25)
    uniform_b = (bits_b >> 8 & 16777215).astype(jnp.float32) * 2.0 ** (-24) + 2.0 ** (-25)
    noise = jnp.sqrt(-2.0 * jnp.log(uniform_a)) * jnp.cos(2.0 * math.pi * uniform_b)
    freq_x = mode_x.astype(jnp.float32) * (math.pi / LEN_X)
    freq_y = mode_y.astype(jnp.float32) * (math.pi / LEN_Y)
    freq_z = mode_z.astype(jnp.float32) * (math.pi / depth)
    amplitude = 1.0 / jnp.sqrt(0.05 + freq_x * freq_x + freq_y * freq_y + freq_z * freq_z)
    return (amplitude * noise).astype(jnp.bfloat16)


def contract_last(left, table):
    return lax.dot_general(
        left, table, (((left.ndim - 1,), (1,)), ((), ())), preferred_element_type=jnp.float32
    )


def operate(wide_p, wide_k):
    center_p = wide_p[:, 1:-1]
    center_k = wide_k[:, 1:-1]
    total = 0.5 * (center_k + wide_k[:, 2:]) * (center_p - wide_p[:, 2:])
    total = total + 0.5 * (center_k + wide_k[:, :-2]) * (center_p - wide_p[:, :-2])
    for axis in (0, 2):
        widths = [(0, 0), (0, 0), (0, 0)]
        widths[axis] = (1, 1)
        padded_p = jnp.pad(center_p, widths)
        padded_k = jnp.pad(center_k, widths)
        size_here = center_p.shape[axis]
        for start in (0, 2):
            near_p = lax.slice_in_dim(padded_p, start, start + size_here, axis=axis)
            near_k = lax.slice_in_dim(padded_k, start, start + size_here, axis=axis)
            total = total + 0.5 * (center_k + near_k) * (center_p - near_p)
    return total


def plain_body(stream_index, forcing):
    depth = forcing.shape[0]
    planes_here = depth // lax.axis_size("wide")
    stream_key = scramble(stream_index[0] ^ 1540483477)
    basis_x = cosine_basis(LEN_X)
    basis_y = cosine_basis(LEN_Y)
    basis_z = cosine_basis(depth)
    first_mode = lax.axis_index("wide") * planes_here
    own_modes = first_mode + jnp.arange(planes_here, dtype=jnp.int32)

    def rows_for(mode_z):
        coeff = coefficient_plane(stream_key, mode_z, depth)
        return jnp.dot(basis_x, coeff, preferred_element_type=jnp.float32).astype(jnp.bfloat16)

    def both_axes(mode_z):
        return contract_last(rows_for(mode_z), basis_y).astype(jnp.bfloat16)

    planes = lax.map(both_axes, own_modes)
    block = lax.all_to_all(planes, "wide", split_axis=1, concat_axis=0, tiled=True)
    count_z, count_x, count_y = block.shape
    field = jnp.dot(
        basis_z, block.reshape(count_z, count_x * count_y), preferred_element_type=jnp.float32
    )
    field = field.reshape(count_z, count_x, count_y)
    perm = jnp.exp(1.5 * jnp.tanh(2.0 * field))
    source = forcing.astype(jnp.float32)
    theta = 27.9
    delta = 26.1
    sigma = theta / delta
    rho = 1.0 / sigma
    step = source / theta
    press = step
    perm_wide = with_halo(perm.astype(jnp.bfloat16), (("wide", 1),), 1).astype(perm.dtype)
    for count in range(ITERS - 1):
        press_wide = with_halo(press, (("wide", 1),), 1)
        resid = source - operate(press_wide, perm_wide)
        rho_next = 1.0 / (2.0 * sigma - rho)
        step = rho_next * rho * step + 2.0 * rho_next / delta * resid
        press = press + step
        rho = rho_next
    return press.astype(jnp.bfloat16)


WIDE = 16
DEPTH = 16
HALO = ITERS - 1
PARTS = 4
UNROLL = 4
TILE = 16
FOLD = 16
VMEM_LIMIT = 60 << 20
THETA = 27.9
DELTA = 26.1
SIN_PI = (
    3.141592640144167, -5.16771008404795, 2.550077528430638, -0.5982912997813382, 0.077657661199004
)
MULT = 73244475


def cos_turns(turns, amplitude, negative=False):
    coeffs = [c * math.sqrt(2.0 * amplitude) for c in SIN_PI]
    square = turns * turns
    poly = coeffs[4] * square + coeffs[3]
    for c in coeffs[2::-1]:
        poly = poly * square + c
    sine = poly * turns
    return sine * sine - amplitude if negative else amplitude - sine * sine


def turns_of(phase, period):
    return (phase - jnp.floor(phase * (1.0 / period) + 0.5) * period) * (1.0 / period)


def srl(value, count):
    return lax.shift_right_logical(value, jnp.int32(count))


def angle_tables(cos_out, sin_out, of_row, length, weighted):
    period = 4.0 * length

    def part(i, carry):
        r = lax.broadcasted_iota(jnp.int32, (8, 128), 0) + i * 8
        factor = of_row(r).astype(jnp.float32)
        at = pl.ds(pl.multiple_of(i * 8, 8), 8)
        for j in range(length // 128):
            k = lax.broadcasted_iota(jnp.int32, (8, 128), 1).astype(jnp.float32) + 128.0 * j
            phase = factor * k
            cosine = cos_turns(turns_of(phase, period), 1.0)
            sine = cos_turns(turns_of(phase - length, period), 1.0)
            if weighted:
                weight = jnp.where(k == 0.0, math.sqrt(1.0 / length), math.sqrt(2.0 / length))
                cosine = cosine * weight
                sine = sine * weight
            cos_out[at, j * 128 : (j + 1) * 128] = cosine
            sin_out[at, j * 128 : (j + 1) * 128] = sine
        return carry

    lax.fori_loop(0, cos_out.shape[0] // 8, part, 0)


def basis_into(out_ref, small, big):
    rows = small[0].shape[0]
    length = out_ref.shape[1]
    angle_tables(*small, lambda r: 2 * r + 1, length, True)
    angle_tables(*big, lambda t: 2 * rows * t, length, False)

    def group(g, carry):
        group_at = pl.ds(pl.multiple_of(g * 8, 8), 8)
        for j in range(length // 128):
            cols = slice(j * 128, (j + 1) * 128)
            big_cos = big[0][group_at, cols]
            big_sin = big[1][group_at, cols]
            for t in range(8):
                at = pl.ds(pl.multiple_of((g * 8 + t) * rows, rows), rows)
                value = small[0][:, cols] * big_cos[t : t + 1] - small[1][:, cols] * big_sin[t : t + 1]
                out_ref[at, cols] = value.astype(jnp.bfloat16)
        return carry

    lax.fori_loop(0, big[0].shape[0] // 8, group, 0)


def folded_basis_into(out_ref, small, big, first_row, count, tiles):
    length = out_ref.shape[1]

    def block_row(r):
        return 2 * (first_row + r // FOLD * count - HALO + r % FOLD * tiles) + 1

    angle_tables(*small, block_row, length, True)
    angle_tables(*big, lambda i: 2 * i, length, False)

    def device(d, carry):
        at = pl.ds(pl.multiple_of(d * FOLD, FOLD), FOLD)
        for i in range(tiles):
            to = pl.ds(pl.multiple_of((d * tiles + i) * FOLD, FOLD), FOLD)
            for j in range(length // 128):
                cols = slice(j * 128, (j + 1) * 128)
                value = small[0][at, cols] * big[0][i : i + 1, cols] - small[1][at, cols] * big[1][i : i + 1, cols]
                out_ref[to, cols] = value.astype(jnp.bfloat16)
        return carry

    lax.fori_loop(0, small[0].shape[0] // FOLD, device, 0)


def coefficients_into(out_ref, key, mode_z, depth, rows):
    const = 2.0 * math.log(2.0)
    key_low = key & 1023
    key_high = key & ~1023

    def part(i, carry):
        r = lax.broadcasted_iota(jnp.int32, (rows, 128), 0) + i * rows
        at = pl.ds(pl.multiple_of(i * rows, rows), rows)
        freq_x = r.astype(jnp.float32) * (math.pi / LEN_X)
        freq_z = mode_z.astype(jnp.float32) * (math.pi / depth)
        row_part = (0.05 + freq_x * freq_x + freq_z * freq_z) * -const
        base = (r + mode_z * LEN_X) * (2 * LEN_Y)
        lane = lax.broadcasted_iota(jnp.int32, (1, 128), 1)
        for j in range(LEN_Y // 128):
            if j % 4 == 0:
                top = (base + j * 256) ^ key_high
                top = top ^ srl(top, 16)
                delta = jnp.where(((top ^ key_low) & 1) == 0, MULT, -MULT)
            freq_y = (lane + j * 128).astype(jnp.float32) * (math.pi / LEN_Y)
            denom = row_part + freq_y * freq_y * -const
            a = (top ^ (((lane + (j % 4) * 128) * 2) ^ key_low)) * MULT
            b = a + delta
            a = (a ^ srl(a, 16)) * MULT
            b = (b ^ srl(b, 16)) * MULT
            a = srl(a ^ srl(a, 16), 8)
            b = (b ^ srl(b, 16)) >> 8
            u = a.astype(jnp.float32) * 2.0 ** (-24) + 2.0 ** (-25)
            turns = b.astype(jnp.float32) * 2.0 ** (-24) + 2.0 ** (-25)
            bits = jnp.minimum(jnp.log2(u), -1e-30)
            size = bits * lax.rsqrt(bits * denom)
            value = size * cos_turns(turns, const, negative=True)
            out_ref[at, j * 128 : (j + 1) * 128] = value.astype(jnp.bfloat16)
        return carry

    lax.fori_loop(0, LEN_X // rows, part, 0)


def transform_into(out_refs, left_ref, coef_ref, rows_ref, basis_ref):
    for n in range(0, LEN_Y, 256):
        cols = slice(n, n + 256)
        rows_ref[:, cols] = jnp.dot(
            left_ref[...], coef_ref[:, cols], preferred_element_type=jnp.float32
        ).astype(jnp.bfloat16)
    size = rows_ref.shape[0] // len(out_refs)
    for n in range(0, LEN_Y, 256):
        cols = slice(n, n + 256)
        value = contract_last(rows_ref[...], basis_ref[cols, :])
        for m, out_ref in enumerate(out_refs):
            out_ref[:, cols] = value[m * size : (m + 1) * size].astype(jnp.bfloat16)


def first_planes_kernel(
    scalars, out_ref, basis_out, folded_out, basis, folded, coef, rows, small_cos, small_sin, big_cos, big_sin, sem,
    *, depth, count, tiles
):
    key, index = scalars[0], scalars[1]
    basis_into(basis, (small_cos.at[pl.ds(0, 64)], small_sin.at[pl.ds(0, 64)]), (big_cos, big_sin))
    folded_basis_into(
        folded,
        (small_cos, small_sin),
        (big_cos.at[pl.ds(0, 8)], big_sin.at[pl.ds(0, 8)]),
        (index >> 3) * (8 * count),
        count,
        tiles,
    )
    copies = [
        pltpu.make_async_copy(basis, basis_out, sem.at[0]),
        pltpu.make_async_copy(folded, folded_out, sem.at[1]),
    ]
    for copy in copies:
        copy.start()
    coefficients_into(coef, key, index & 7, depth, 64)
    transform_into([out_ref], folded, coef, rows, basis)
    for copy in copies:
        copy.wait()


def first_planes(scalars, depth, count, tiles):
    total = 8 * tiles * FOLD
    bits = jnp.bfloat16
    return pl.pallas_call(
        functools.partial(first_planes_kernel, depth=depth, count=count, tiles=tiles),
        in_specs=[pl.BlockSpec(memory_space=pltpu.SMEM)],
        out_specs=[pl.BlockSpec(memory_space=pltpu.VMEM)] + [pl.BlockSpec(memory_space=pl.ANY)] * 2,
        out_shape=[
            jax.ShapeDtypeStruct((total, LEN_Y), bits),
            jax.ShapeDtypeStruct((LEN_X, LEN_X), bits),
            jax.ShapeDtypeStruct((total, LEN_X), bits),
        ],
        scratch_shapes=[
            pltpu.VMEM((LEN_X, LEN_X), bits),
            pltpu.VMEM((total, LEN_X), bits),
            pltpu.VMEM((LEN_X, LEN_Y), bits),
            pltpu.VMEM((total, LEN_Y), bits),
            pltpu.VMEM((8 * FOLD, LEN_X), jnp.float32),
            pltpu.VMEM((8 * FOLD, LEN_X), jnp.float32),
            pltpu.VMEM((LEN_X // 64, LEN_X), jnp.float32),
            pltpu.VMEM((LEN_X // 64, LEN_X), jnp.float32),
            pltpu.SemaphoreType.DMA((2,)),
        ],
        compiler_params=pltpu.CompilerParams(vmem_limit_bytes=VMEM_LIMIT),
        cost_estimate=pl.CostEstimate(flops=25_000_000_000, transcendentals=0, bytes_accessed=8_000_000),
        name="first_planes",
    )(scalars)


def shared_mode(index, depth):
    color = (index >> 1 ^ index >> 2) & 1
    return depth // 2 + 4 * color + 2 * (index & 1)


def more_planes_kernel(scalars, basis_in, folded_in, *refs, depth, flips, offset):
    out_refs = refs[:PARTS]
    basis, left, coef, rows, sem = refs[PARTS:]
    size = out_refs[0].shape[0]
    key, index = scalars[0], scalars[1]
    mode = shared_mode(index, depth) + offset
    copies = [pltpu.make_async_copy(basis_in, basis, sem.at[PARTS])]
    for n, flip in enumerate(flips):
        source = folded_in.at[pl.ds(pl.multiple_of((index & 7 ^ flip) * size, size), size), :]
        copies.append(pltpu.make_async_copy(source, left.at[pl.ds(n * size, size), :], sem.at[n]))
    for copy in copies:
        copy.start()
    coefficients_into(coef, key, mode, depth, 64)
    for copy in copies:
        copy.wait()
    transform_into(out_refs, left, coef, rows, basis)


def more_planes(scalars, basis, folded, depth, size, flips, offset):
    anywhere = pl.BlockSpec(memory_space=pl.ANY)
    return pl.pallas_call(
        functools.partial(more_planes_kernel, depth=depth, flips=flips, offset=offset),
        in_specs=[pl.BlockSpec(memory_space=pltpu.SMEM), anywhere, anywhere],
        out_specs=[pl.BlockSpec(memory_space=pltpu.VMEM)] * PARTS,
        out_shape=[jax.ShapeDtypeStruct((size, LEN_Y), jnp.bfloat16)] * PARTS,
        scratch_shapes=[
            pltpu.VMEM((LEN_X, LEN_X), jnp.bfloat16),
            pltpu.VMEM((PARTS * size, LEN_X), jnp.bfloat16),
            pltpu.VMEM((LEN_X, LEN_Y), jnp.bfloat16),
            pltpu.VMEM((PARTS * size, LEN_Y), jnp.bfloat16),
            pltpu.SemaphoreType.DMA((PARTS + 1,)),
        ],
        compiler_params=pltpu.CompilerParams(vmem_limit_bytes=VMEM_LIMIT),
        cost_estimate=pl.CostEstimate(flops=20_000_000_000, transcendentals=0, bytes_accessed=8_000_000),
        name="more_planes",
    )(scalars, basis, folded)


def folded_row(index, tiles):
    return index % FOLD * tiles + index // FOLD


def fold_kernel(f_ref, low_ref, high_ref, out_ref, edge):
    _, count, _ = f_ref.shape
    padded = out_ref.shape[1]
    shape = (padded, count + TILE)
    row = folded_row(lax.broadcasted_iota(jnp.int32, shape, 0), padded // FOLD)
    source = jnp.where(row < HALO, row + count, jnp.where(row < HALO + count, row - HALO, row))
    spread = (lax.broadcasted_iota(jnp.int32, shape, 1) == source).astype(jnp.bfloat16)

    @pl.when(pl.program_id(0) == 0)
    def _():
        edge[...] = jnp.zeros(edge.shape, edge.dtype)

    for m in range(f_ref.shape[0]):
        edge[0:HALO, :] = low_ref[m]
        edge[HALO : 2 * HALO, :] = high_ref[m]
        rows = jnp.concatenate([f_ref[m], edge[...]], axis=0)
        for n in range(0, LEN_Y, 512):
            cols = slice(n, n + 512)
            out_ref[m, :, cols] = jnp.dot(spread, rows[:, cols], preferred_element_type=jnp.float32).astype(
                jnp.bfloat16
            )


def fold(forcing, low, high, padded):
    depth, count, _ = forcing.shape
    return pl.pallas_call(
        fold_kernel,
        grid=(depth // 2,),
        in_specs=[
            pl.BlockSpec((2, count, LEN_Y), lambda z: (z, 0, 0)),
            pl.BlockSpec((2, HALO, LEN_Y), lambda z: (z, 0, 0)),
            pl.BlockSpec((2, HALO, LEN_Y), lambda z: (z, 0, 0)),
        ],
        out_specs=pl.BlockSpec((2, padded, LEN_Y), lambda z: (z, 0, 0)),
        out_shape=jax.ShapeDtypeStruct((depth, padded, LEN_Y), jnp.bfloat16),
        scratch_shapes=[pltpu.VMEM((TILE, LEN_Y), jnp.bfloat16)],
        compiler_params=pltpu.CompilerParams(vmem_limit_bytes=VMEM_LIMIT),
        cost_estimate=pl.CostEstimate(flops=1_300_000_000, transcendentals=0, bytes_accessed=10_000_000),
        name="fold",
    )(forcing, low, high)


def chebyshev():
    sigma = THETA / DELTA
    rho = 1.0 / sigma
    pairs = []
    for _ in range(ITERS - 1):
        rho_next = 1.0 / (2.0 * sigma - rho)
        pairs.append((rho_next * rho, 2.0 * rho_next / DELTA))
        rho = rho_next
    return pairs


def solve_kernel(scalars, slot_modes, forcing, block, *refs):
    planes = refs[:-11]
    out_ref, k_ref, f_ref, p_two, p_three, b_two, b_three, stage, turned, sems, sem_out = refs[-11:]
    modes = block.shape[0]
    depth, padded, _ = k_ref.shape
    count = out_ref.shape[1]
    tiles = padded // FOLD
    blocks = LEN_Y // 128
    index = scalars[1]

    def cols(j):
        return slice(j * 128, (j + 1) * 128)

    def copies(t, slot):
        at = pl.ds(t * FOLD, FOLD)
        found = [pltpu.make_async_copy(block.at[:, at, :], stage.at[slot, pl.ds(0, modes)], sems.at[slot, 0])]
        for n, plane in enumerate(planes):
            found.append(pltpu.make_async_copy(plane.at[at, :], stage.at[slot, modes + n], sems.at[slot, n + 1]))
        return found

    for copy in copies(0, 0):
        copy.start()
    forcing_copy = pltpu.make_async_copy(forcing, f_ref, sems.at[2, 0])

    size = depth * FOLD
    row = lax.broadcasted_iota(jnp.int32, (size, size), 0)
    col = lax.broadcasted_iota(jnp.int32, (size, size), 1)
    mode = jnp.broadcast_to(slot_modes[...], (size, size))
    phase = ((2 * (row // FOLD) + 1) * mode).astype(jnp.float32)
    weight = jnp.where(mode == 0, math.sqrt(1.0 / depth), math.sqrt(2.0 / depth))
    cosine = cos_turns(turns_of(phase, 4.0 * depth), 1.0)
    mixing = jnp.where(row % FOLD == col % FOLD, weight * cosine, 0.0).astype(jnp.bfloat16)

    def inside(start):
        row = folded_row(lax.broadcasted_iota(jnp.int32, (FOLD, 128), 0) + start, tiles)
        outside = ((row < HALO) & (index == 0)) | ((row >= HALO + count) & (index == WIDE - 1))
        return jnp.where(outside, 0.0, 1.0)

    for t in range(tiles):
        slot = t % 2
        if t + 1 < tiles:
            for copy in copies(t + 1, 1 - slot):
                copy.start()
        else:
            forcing_copy.start()
        for copy in copies(t, slot):
            copy.wait()
        keep = inside(t * FOLD)
        for n in range(0, LEN_Y, 512):
            field = jnp.dot(
                mixing,
                stage[slot, :, :, n : n + 512].reshape(size, 512),
                preferred_element_type=jnp.float32,
            ).reshape(depth, FOLD, 512)
            for j in range(n // 128, n // 128 + 4):
                part = field[:, :, j * 128 - n : j * 128 - n + 128]
                value = jnp.exp(1.5 * jnp.tanh(2.0 * part)) * keep[None]
                k_ref[:, t * FOLD : t * FOLD + FOLD, cols(j)] = value.astype(jnp.bfloat16)
    forcing_copy.wait()
    lane = lax.broadcasted_iota(jnp.int32, (FOLD, 128), 1)
    nothing = jnp.zeros((FOLD, 128), jnp.bfloat16)

    def sweep(src, store):
        def tile(i, below, above):
            at = pl.ds(pl.multiple_of(i * FOLD, FOLD), FOLD)
            factor = inside(i * FOLD)

            def level(z, top, flows_z):
                outs = []
                next_flows = []
                k_all = [k_ref[z, at, cols(j)] for j in range(blocks)]
                p_all = [src[z, at, cols(j)] for j in range(blocks)]
                turns = [pltpu.roll(p, 127, 1) for p in p_all] + [nothing]
                k_turns = [pltpu.roll(k, 127, 1) for k in k_all] + [nothing]
                before = None
                for j in range(blocks):
                    k, p = k_all[j], p_all[j]
                    k_right = jnp.where(lane == 127, k_turns[j + 1], k_turns[j])
                    flow_y = (k + k_right) * (p - jnp.where(lane == 127, turns[j + 1], turns[j]))
                    flow_turn = pltpu.roll(flow_y, 1, 1)
                    left = jnp.where(lane == 0, -k * p if before is None else before, flow_turn)
                    before = flow_turn
                    if top:
                        flow_z = k * p
                    else:
                        flow_z = (k + k_ref[z + 1, at, cols(j)]) * (p - src[z + 1, at, cols(j)])
                    flow_x = (k + above(k_ref, z, j)) * (p - above(src, z, j))
                    flow_w = (k + below(k_ref, z, j)) * (p - below(src, z, j))
                    outs.append((flow_x + flow_w) + ((flow_y - left) + (flow_z - flows_z[j])))
                    next_flows.append(flow_z)
                return next_flows, outs

            def keep(z, outs):
                for j in range(blocks):
                    store(z, j, at, outs[j].astype(jnp.float32), factor)

            def levels(first, flows_z):
                found = []
                for u in range(UNROLL):
                    z = first + u
                    flows_z, outs = level(z, isinstance(z, int) and z == depth - 1, flows_z)
                    found.append(outs)
                for u, outs in enumerate(found):
                    keep(first + u, outs)
                return flows_z

            def group(g, flows_z):
                return levels(g * UNROLL, flows_z)

            flows = [-k_ref[0, at, cols(j)] * src[0, at, cols(j)] for j in range(blocks)]
            groups = depth // UNROLL - 1
            flows = lax.fori_loop(0, groups, group, flows)
            levels(groups * UNROLL, flows)

        def plain(step):
            def load(ref, z, j, i):
                return ref[z, pl.ds(pl.multiple_of((i + step) * FOLD, FOLD), FOLD), cols(j)]

            return load

        def first(ref, z, j):
            return pltpu.roll(ref[z, padded - FOLD : padded, cols(j)], 1, 0)

        def last(ref, z, j):
            return pltpu.roll(ref[z, 0:FOLD, cols(j)], FOLD - 1, 0)

        def inner(i, carry):
            tile(
                i,
                lambda ref, z, j: plain(-1)(ref, z, j, i),
                lambda ref, z, j: plain(1)(ref, z, j, i),
            )
            return carry

        tile(0, first, lambda ref, z, j: plain(1)(ref, z, j, 0))
        lax.fori_loop(1, tiles - 1, inner, 0)
        tile(tiles - 1, lambda ref, z, j: plain(-1)(ref, z, j, tiles - 1), last)

    (a1, b1), (a2, b2), (a3, b3) = chebyshev()

    def store_one(z, j, at, out, factor):
        source = f_ref[z, at, cols(j)].astype(jnp.float32)
        value = ((1.0 + a1) / THETA + b1) * source - (0.5 * b1 / THETA * factor) * out
        p_two[z, at, cols(j)] = value
        b_two[z, at, cols(j)] = value.astype(jnp.bfloat16)

    def store_two(z, j, at, out, factor):
        source = f_ref[z, at, cols(j)].astype(jnp.float32)
        value = (1.0 + a2) * p_two[z, at, cols(j)] + (b2 - a2 / THETA) * source - (0.5 * b2 * factor) * out
        p_three[z, at, cols(j)] = value
        b_three[z, at, cols(j)] = value.astype(jnp.bfloat16)

    def store_three(z, j, at, out, factor):
        source = f_ref[z, at, cols(j)].astype(jnp.float32)
        old = (1.0 + a3) * p_three[z, at, cols(j)] - a3 * p_two[z, at, cols(j)]
        b_two[z, at, cols(j)] = (old + (b3 * source - 0.5 * b3 * out)).astype(jnp.bfloat16)

    sweep(f_ref, store_one)
    sweep(b_two, store_two)
    sweep(b_three, store_three)

    shape = (count, padded)
    place = folded_row(lax.broadcasted_iota(jnp.int32, shape, 1), tiles)
    unfold = (lax.broadcasted_iota(jnp.int32, shape, 0) + HALO == place).astype(jnp.bfloat16)

    def leave(z, slot):
        return pltpu.make_async_copy(turned.at[slot], out_ref.at[z], sem_out.at[slot])

    for z in range(depth):
        slot = z % 2
        if z > 1:
            leave(z - 2, slot).wait()
        for n in range(0, LEN_Y, 512):
            turned[slot, :, n : n + 512] = jnp.dot(
                unfold, b_two[z, :, n : n + 512], preferred_element_type=jnp.float32
            ).astype(jnp.bfloat16)
        leave(z, slot).start()
    for z in (depth - 2, depth - 1):
        leave(z, z % 2).wait()


def solve(scalars, slot_modes, forcing, block, planes, count):
    depth, padded, _ = forcing.shape
    anywhere = pl.BlockSpec(memory_space=pl.ANY)
    narrow = pltpu.VMEM((depth, padded, LEN_Y), jnp.bfloat16)
    whole = pltpu.VMEM((depth, padded, LEN_Y), jnp.float32)
    return pl.pallas_call(
        solve_kernel,
        in_specs=[pl.BlockSpec(memory_space=pltpu.SMEM), pl.BlockSpec(memory_space=pltpu.VMEM)]
        + [anywhere] * (2 + len(planes)),
        out_specs=anywhere,
        out_shape=jax.ShapeDtypeStruct((depth, count, LEN_Y), jnp.bfloat16),
        scratch_shapes=[
            narrow,
            narrow,
            whole,
            whole,
            narrow,
            narrow,
            pltpu.VMEM((2, depth, FOLD, LEN_Y), jnp.bfloat16),
            pltpu.VMEM((2, count, LEN_Y), jnp.bfloat16),
            pltpu.SemaphoreType.DMA((3, 1 + len(planes))),
            pltpu.SemaphoreType.DMA((2,)),
        ],
        compiler_params=pltpu.CompilerParams(vmem_limit_bytes=VMEM_LIMIT),
        name="solve",
    )(scalars, slot_modes, forcing, block, *planes)


def body(stream_index, forcing):
    depth, count, _ = forcing.shape
    index = lax.axis_index("wide")
    scalars = jnp.stack([scramble(stream_index[0] ^ 1540483477), index]).astype(jnp.int32)
    tiles = -(-(count + 2 * HALO) // FOLD)
    padded = tiles * FOLD
    own, basis, folded = first_planes(scalars, depth, count, tiles)
    groups = [list(range(8)), list(range(8, 16))]
    block = lax.all_to_all(
        own.reshape(8, padded, LEN_Y), "wide", 0, 0, axis_index_groups=groups, tiled=True
    )

    def pairwise(offset, bit):
        flips = (0, 1, bit, bit ^ 1)
        out = more_planes(scalars, basis, folded, depth, padded, flips, offset)
        return [out[0]] + [
            lax.ppermute(piece, "wide", [(i, i ^ flip) for i in range(WIDE)])
            for piece, flip in zip(out[1:], flips[1:])
        ]

    planes = pairwise(0, 4) + pairwise(1, 2)
    slot = lax.broadcasted_iota(jnp.int32, (1, depth * FOLD), 1) // FOLD
    flip = jnp.where(slot < 12, (slot & 1) ^ (slot & 2) << 1, (slot & 1) ^ (slot & 2))
    slot_modes = jnp.where(slot < 8, slot, shared_mode(index ^ flip, depth) + (slot >= 12))
    forward = [(i, i + 1) for i in range(WIDE - 1)]
    backward = [(target, source) for source, target in forward]
    low = lax.ppermute(forcing[:, -HALO:], "wide", forward)
    high = lax.ppermute(forcing[:, :HALO], "wide", backward)
    return solve(scalars, slot_modes, fold(forcing, low, high, padded), block, planes, count)


def solution(mesh):
    special = mesh.shape["wide"] == WIDE
    return jax.shard_map(
        body if special else plain_body,
        mesh=mesh,
        in_specs=(P("group"), P("group", "wide", None)),
        out_specs=P("group", "wide", None),
        check_vma=False,
    )
```

```python
import functools
import math

import jax
import jax.numpy as jnp
from jax import lax
from jax.experimental import pallas as pl
from jax.experimental.pallas import tpu as pltpu
from jax.sharding import PartitionSpec as P

LEN_X = 1536
LEN_Y = 1536
ITERS = 4


def with_halo(block, sides, width):
    for axis, dim in sides:
        count = lax.axis_size(axis)
        forward = [(i, i + 1) for i in range(count - 1)]
        backward = [(target, source) for source, target in forward]
        low = lax.ppermute(
            lax.slice_in_dim(block, block.shape[dim] - width, None, axis=dim), axis, forward
        )
        high = lax.ppermute(lax.slice_in_dim(block, 0, width, axis=dim), axis, backward)
        block = jnp.concatenate([low, block, high], axis=dim)
    return block


def scramble(value):
    value = value ^ value >> 16 & 65535
    value = value * 73244475
    value = value ^ value >> 16 & 65535
    value = value * 73244475
    value = value ^ value >> 16 & 65535
    return value


def cosine_basis(length):
    row_idx = lax.broadcasted_iota(jnp.int32, (length, length), 0)
    mode_idx = lax.broadcasted_iota(jnp.int32, (length, length), 1)
    phase = (2 * row_idx + 1) * mode_idx % (4 * length)
    angle = phase.astype(jnp.float32) * (math.pi / (2.0 * length))
    weights = jnp.where(mode_idx == 0, math.sqrt(1.0 / length), math.sqrt(2.0 / length))
    return (weights * jnp.cos(angle)).astype(jnp.bfloat16)


def coefficient_plane(stream_key, mode_z, depth):
    mode_x = lax.broadcasted_iota(jnp.int32, (LEN_X, LEN_Y), 0)
    mode_y = lax.broadcasted_iota(jnp.int32, (LEN_X, LEN_Y), 1)
    counter = (mode_z * LEN_X + mode_x) * LEN_Y + mode_y
    bits_a = scramble(2 * counter ^ stream_key)
    bits_b = scramble(2 * counter + 1 ^ stream_key)
    uniform_a = (bits_a >> 8 & 16777215).astype(jnp.float32) * 2.0 ** (-24) + 2.0 ** (-25)
    uniform_b = (bits_b >> 8 & 16777215).astype(jnp.float32) * 2.0 ** (-24) + 2.0 ** (-25)
    noise = jnp.sqrt(-2.0 * jnp.log(uniform_a)) * jnp.cos(2.0 * math.pi * uniform_b)
    freq_x = mode_x.astype(jnp.float32) * (math.pi / LEN_X)
    freq_y = mode_y.astype(jnp.float32) * (math.pi / LEN_Y)
    freq_z = mode_z.astype(jnp.float32) * (math.pi / depth)
    amplitude = 1.0 / jnp.sqrt(0.05 + freq_x * freq_x + freq_y * freq_y + freq_z * freq_z)
    return (amplitude * noise).astype(jnp.bfloat16)


def contract_last(left, table):
    return lax.dot_general(
        left, table, (((left.ndim - 1,), (1,)), ((), ())), preferred_element_type=jnp.float32
    )


def operate(wide_p, wide_k):
    center_p = wide_p[:, 1:-1]
    center_k = wide_k[:, 1:-1]
    total = 0.5 * (center_k + wide_k[:, 2:]) * (center_p - wide_p[:, 2:])
    total = total + 0.5 * (center_k + wide_k[:, :-2]) * (center_p - wide_p[:, :-2])
    for axis in (0, 2):
        widths = [(0, 0), (0, 0), (0, 0)]
        widths[axis] = (1, 1)
        padded_p = jnp.pad(center_p, widths)
        padded_k = jnp.pad(center_k, widths)
        size_here = center_p.shape[axis]
        for start in (0, 2):
            near_p = lax.slice_in_dim(padded_p, start, start + size_here, axis=axis)
            near_k = lax.slice_in_dim(padded_k, start, start + size_here, axis=axis)
            total = total + 0.5 * (center_k + near_k) * (center_p - near_p)
    return total


def plain_body(stream_index, forcing):
    depth = forcing.shape[0]
    planes_here = depth // lax.axis_size("wide")
    stream_key = scramble(stream_index[0] ^ 1540483477)
    basis_x = cosine_basis(LEN_X)
    basis_y = cosine_basis(LEN_Y)
    basis_z = cosine_basis(depth)
    first_mode = lax.axis_index("wide") * planes_here
    own_modes = first_mode + jnp.arange(planes_here, dtype=jnp.int32)

    def rows_for(mode_z):
        coeff = coefficient_plane(stream_key, mode_z, depth)
        return jnp.dot(basis_x, coeff, preferred_element_type=jnp.float32).astype(jnp.bfloat16)

    def both_axes(mode_z):
        return contract_last(rows_for(mode_z), basis_y).astype(jnp.bfloat16)

    planes = lax.map(both_axes, own_modes)
    block = lax.all_to_all(planes, "wide", split_axis=1, concat_axis=0, tiled=True)
    count_z, count_x, count_y = block.shape
    field = jnp.dot(
        basis_z, block.reshape(count_z, count_x * count_y), preferred_element_type=jnp.float32
    )
    field = field.reshape(count_z, count_x, count_y)
    perm = jnp.exp(1.5 * jnp.tanh(2.0 * field))
    source = forcing.astype(jnp.float32)
    theta = 27.9
    delta = 26.1
    sigma = theta / delta
    rho = 1.0 / sigma
    step = source / theta
    press = step
    perm_wide = with_halo(perm.astype(jnp.bfloat16), (("wide", 1),), 1).astype(perm.dtype)
    for count in range(ITERS - 1):
        press_wide = with_halo(press, (("wide", 1),), 1)
        resid = source - operate(press_wide, perm_wide)
        rho_next = 1.0 / (2.0 * sigma - rho)
        step = rho_next * rho * step + 2.0 * rho_next / delta * resid
        press = press + step
        rho = rho_next
    return press.astype(jnp.bfloat16)


WIDE = 16
DEPTH = 16
HALO = ITERS - 1
PARTS = 4
UNROLL = 4
TILE = 16
FOLD = 16
VMEM_LIMIT = 60 << 20
THETA = 27.9
DELTA = 26.1
SIN_PI = (
    3.141592640144167, -5.16771008404795, 2.550077528430638, -0.5982912997813382, 0.077657661199004
)
MULT = 73244475


def cos_turns(turns, amplitude, negative=False):
    coeffs = [c * math.sqrt(2.0 * amplitude) for c in SIN_PI]
    square = turns * turns
    poly = coeffs[4] * square + coeffs[3]
    for c in coeffs[2::-1]:
        poly = poly * square + c
    sine = poly * turns
    return sine * sine - amplitude if negative else amplitude - sine * sine


def turns_of(phase, period):
    return (phase - jnp.floor(phase * (1.0 / period) + 0.5) * period) * (1.0 / period)


def srl(value, count):
    return lax.shift_right_logical(value, jnp.int32(count))


def angle_tables(cos_out, sin_out, of_row, length, weighted):
    period = 4.0 * length

    def part(i, carry):
        r = lax.broadcasted_iota(jnp.int32, (8, 128), 0) + i * 8
        factor = of_row(r).astype(jnp.float32)
        at = pl.ds(pl.multiple_of(i * 8, 8), 8)
        for j in range(length // 128):
            k = lax.broadcasted_iota(jnp.int32, (8, 128), 1).astype(jnp.float32) + 128.0 * j
            phase = factor * k
            cosine = cos_turns(turns_of(phase, period), 1.0)
            sine = cos_turns(turns_of(phase - length, period), 1.0)
            if weighted:
                weight = jnp.where(k == 0.0, math.sqrt(1.0 / length), math.sqrt(2.0 / length))
                cosine = cosine * weight
                sine = sine * weight
            cos_out[at, j * 128 : (j + 1) * 128] = cosine
            sin_out[at, j * 128 : (j + 1) * 128] = sine
        return carry

    lax.fori_loop(0, cos_out.shape[0] // 8, part, 0)


def basis_into(out_ref, small, big):
    rows = small[0].shape[0]
    length = out_ref.shape[1]
    angle_tables(*small, lambda r: 2 * r + 1, length, True)
    angle_tables(*big, lambda t: 2 * rows * t, length, False)

    def group(g, carry):
        group_at = pl.ds(pl.multiple_of(g * 8, 8), 8)
        for j in range(length // 128):
            cols = slice(j * 128, (j + 1) * 128)
            big_cos = big[0][group_at, cols]
            big_sin = big[1][group_at, cols]
            for t in range(8):
                at = pl.ds(pl.multiple_of((g * 8 + t) * rows, rows), rows)
                value = small[0][:, cols] * big_cos[t : t + 1] - small[1][:, cols] * big_sin[t : t + 1]
                out_ref[at, cols] = value.astype(jnp.bfloat16)
        return carry

    lax.fori_loop(0, big[0].shape[0] // 8, group, 0)


def folded_basis_into(out_ref, small, big, first_row, count, tiles):
    length = out_ref.shape[1]

    def block_row(r):
        return 2 * (first_row + r // FOLD * count - HALO + r % FOLD * tiles) + 1

    angle_tables(*small, block_row, length, True)
    angle_tables(*big, lambda i: 2 * i, length, False)

    def device(d, carry):
        at = pl.ds(pl.multiple_of(d * FOLD, FOLD), FOLD)
        for i in range(tiles):
            to = pl.ds(pl.multiple_of((d * tiles + i) * FOLD, FOLD), FOLD)
            for j in range(length // 128):
                cols = slice(j * 128, (j + 1) * 128)
                value = small[0][at, cols] * big[0][i : i + 1, cols] - small[1][at, cols] * big[1][i : i + 1, cols]
                out_ref[to, cols] = value.astype(jnp.bfloat16)
        return carry

    lax.fori_loop(0, small[0].shape[0] // FOLD, device, 0)


def coefficients_into(out_ref, key, mode_z, depth, rows):
    const = 2.0 * math.log(2.0)
    key_low = key & 1023
    key_high = key & ~1023

    def part(i, carry):
        r = lax.broadcasted_iota(jnp.int32, (rows, 128), 0) + i * rows
        at = pl.ds(pl.multiple_of(i * rows, rows), rows)
        freq_x = r.astype(jnp.float32) * (math.pi / LEN_X)
        freq_z = mode_z.astype(jnp.float32) * (math.pi / depth)
        row_part = (0.05 + freq_x * freq_x + freq_z * freq_z) * -const
        base = (r + mode_z * LEN_X) * (2 * LEN_Y)
        lane = lax.broadcasted_iota(jnp.int32, (1, 128), 1)
        for j in range(LEN_Y // 128):
            if j % 4 == 0:
                top = (base + j * 256) ^ key_high
                top = top ^ srl(top, 16)
                delta = jnp.where(((top ^ key_low) & 1) == 0, MULT, -MULT)
            freq_y = (lane + j * 128).astype(jnp.float32) * (math.pi / LEN_Y)
            denom = row_part + freq_y * freq_y * -const
            a = (top ^ (((lane + (j % 4) * 128) * 2) ^ key_low)) * MULT
            b = a + delta
            a = (a ^ srl(a, 16)) * MULT
            b = (b ^ srl(b, 16)) * MULT
            a = srl(a ^ srl(a, 16), 8)
            b = (b ^ srl(b, 16)) >> 8
            u = a.astype(jnp.float32) * 2.0 ** (-24) + 2.0 ** (-25)
            turns = b.astype(jnp.float32) * 2.0 ** (-24) + 2.0 ** (-25)
            bits = jnp.minimum(jnp.log2(u), -1e-30)
            size = bits * lax.rsqrt(bits * denom)
            value = size * cos_turns(turns, const, negative=True)
            out_ref[at, j * 128 : (j + 1) * 128] = value.astype(jnp.bfloat16)
        return carry

    lax.fori_loop(0, LEN_X // rows, part, 0)


def transform_into(out_refs, left_ref, coef_ref, rows_ref, basis_ref):
    for n in range(0, LEN_Y, 256):
        cols = slice(n, n + 256)
        rows_ref[:, cols] = jnp.dot(
            left_ref[...], coef_ref[:, cols], preferred_element_type=jnp.float32
        ).astype(jnp.bfloat16)
    size = rows_ref.shape[0] // len(out_refs)
    for n in range(0, LEN_Y, 256):
        cols = slice(n, n + 256)
        value = contract_last(rows_ref[...], basis_ref[cols, :])
        for m, out_ref in enumerate(out_refs):
            out_ref[:, cols] = value[m * size : (m + 1) * size].astype(jnp.bfloat16)


def first_planes_kernel(
    scalars, out_ref, basis_out, folded_out, basis, folded, coef, rows, small_cos, small_sin, big_cos, big_sin, sem,
    *, depth, count, tiles
):
    key, index = scalars[0], scalars[1]
    basis_into(basis, (small_cos.at[pl.ds(0, 64)], small_sin.at[pl.ds(0, 64)]), (big_cos, big_sin))
    folded_basis_into(
        folded,
        (small_cos, small_sin),
        (big_cos.at[pl.ds(0, 8)], big_sin.at[pl.ds(0, 8)]),
        (index >> 3) * (8 * count),
        count,
        tiles,
    )
    copies = [
        pltpu.make_async_copy(basis, basis_out, sem.at[0]),
        pltpu.make_async_copy(folded, folded_out, sem.at[1]),
    ]
    for copy in copies:
        copy.start()
    coefficients_into(coef, key, index & 7, depth, 64)
    transform_into([out_ref], folded, coef, rows, basis)
    for copy in copies:
        copy.wait()


def first_planes(scalars, depth, count, tiles):
    total = 8 * tiles * FOLD
    bits = jnp.bfloat16
    return pl.pallas_call(
        functools.partial(first_planes_kernel, depth=depth, count=count, tiles=tiles),
        in_specs=[pl.BlockSpec(memory_space=pltpu.SMEM)],
        out_specs=[pl.BlockSpec(memory_space=pltpu.VMEM)] + [pl.BlockSpec(memory_space=pl.ANY)] * 2,
        out_shape=[
            jax.ShapeDtypeStruct((total, LEN_Y), bits),
            jax.ShapeDtypeStruct((LEN_X, LEN_X), bits),
            jax.ShapeDtypeStruct((total, LEN_X), bits),
        ],
        scratch_shapes=[
            pltpu.VMEM((LEN_X, LEN_X), bits),
            pltpu.VMEM((total, LEN_X), bits),
            pltpu.VMEM((LEN_X, LEN_Y), bits),
            pltpu.VMEM((total, LEN_Y), bits),
            pltpu.VMEM((8 * FOLD, LEN_X), jnp.float32),
            pltpu.VMEM((8 * FOLD, LEN_X), jnp.float32),
            pltpu.VMEM((LEN_X // 64, LEN_X), jnp.float32),
            pltpu.VMEM((LEN_X // 64, LEN_X), jnp.float32),
            pltpu.SemaphoreType.DMA((2,)),
        ],
        compiler_params=pltpu.CompilerParams(vmem_limit_bytes=VMEM_LIMIT),
        cost_estimate=pl.CostEstimate(flops=25_000_000_000, transcendentals=0, bytes_accessed=8_000_000),
        name="first_planes",
    )(scalars)


def shared_mode(index, depth):
    color = (index >> 1 ^ index >> 2) & 1
    return depth // 2 + 4 * color + 2 * (index & 1)


def beside_bit(core, offset):
    return 4 >> (core ^ offset)


def more_planes_kernel(scalars, basis_in, folded_in, *refs, depth, offset):
    out_refs = refs[:PARTS]
    basis, left, coef, rows, sem = refs[PARTS:]
    size = out_refs[0].shape[0]
    key, index = scalars[0], scalars[1]
    mode = shared_mode(index, depth) + offset
    copies = [pltpu.make_async_copy(basis_in, basis, sem.at[PARTS])]
    bit = beside_bit(index & 1, offset)
    for n, flip in enumerate((0, 1, bit, bit ^ 1)):
        source = folded_in.at[pl.ds(pl.multiple_of((index & 7 ^ flip) * size, size), size), :]
        copies.append(pltpu.make_async_copy(source, left.at[pl.ds(n * size, size), :], sem.at[n]))
    for copy in copies:
        copy.start()
    coefficients_into(coef, key, mode, depth, 64)
    for copy in copies:
        copy.wait()
    transform_into(out_refs, left, coef, rows, basis)


def more_planes(scalars, basis, folded, depth, size, offset):
    anywhere = pl.BlockSpec(memory_space=pl.ANY)
    return pl.pallas_call(
        functools.partial(more_planes_kernel, depth=depth, offset=offset),
        in_specs=[pl.BlockSpec(memory_space=pltpu.SMEM), anywhere, anywhere],
        out_specs=[pl.BlockSpec(memory_space=pltpu.VMEM)] * PARTS,
        out_shape=[jax.ShapeDtypeStruct((size, LEN_Y), jnp.bfloat16)] * PARTS,
        scratch_shapes=[
            pltpu.VMEM((LEN_X, LEN_X), jnp.bfloat16),
            pltpu.VMEM((PARTS * size, LEN_X), jnp.bfloat16),
            pltpu.VMEM((LEN_X, LEN_Y), jnp.bfloat16),
            pltpu.VMEM((PARTS * size, LEN_Y), jnp.bfloat16),
            pltpu.SemaphoreType.DMA((PARTS + 1,)),
        ],
        compiler_params=pltpu.CompilerParams(vmem_limit_bytes=VMEM_LIMIT),
        cost_estimate=pl.CostEstimate(flops=20_000_000_000, transcendentals=0, bytes_accessed=8_000_000),
        name="more_planes",
    )(scalars, basis, folded)


def folded_row(index, tiles):
    return index % FOLD * tiles + index // FOLD


def fold_kernel(f_ref, low_ref, high_ref, out_ref, edge):
    _, count, _ = f_ref.shape
    padded = out_ref.shape[1]
    shape = (padded, count + TILE)
    row = folded_row(lax.broadcasted_iota(jnp.int32, shape, 0), padded // FOLD)
    source = jnp.where(row < HALO, row + count, jnp.where(row < HALO + count, row - HALO, row))
    spread = (lax.broadcasted_iota(jnp.int32, shape, 1) == source).astype(jnp.bfloat16)

    @pl.when(pl.program_id(0) == 0)
    def _():
        edge[...] = jnp.zeros(edge.shape, edge.dtype)

    for m in range(f_ref.shape[0]):
        edge[0:HALO, :] = low_ref[m]
        edge[HALO : 2 * HALO, :] = high_ref[m]
        rows = jnp.concatenate([f_ref[m], edge[...]], axis=0)
        for n in range(0, LEN_Y, 512):
            cols = slice(n, n + 512)
            out_ref[m, :, cols] = jnp.dot(spread, rows[:, cols], preferred_element_type=jnp.float32).astype(
                jnp.bfloat16
            )


def fold(forcing, low, high, padded):
    depth, count, _ = forcing.shape
    return pl.pallas_call(
        fold_kernel,
        grid=(depth // 2,),
        in_specs=[
            pl.BlockSpec((2, count, LEN_Y), lambda z: (z, 0, 0)),
            pl.BlockSpec((2, HALO, LEN_Y), lambda z: (z, 0, 0)),
            pl.BlockSpec((2, HALO, LEN_Y), lambda z: (z, 0, 0)),
        ],
        out_specs=pl.BlockSpec((2, padded, LEN_Y), lambda z: (z, 0, 0)),
        out_shape=jax.ShapeDtypeStruct((depth, padded, LEN_Y), jnp.bfloat16),
        scratch_shapes=[pltpu.VMEM((TILE, LEN_Y), jnp.bfloat16)],
        compiler_params=pltpu.CompilerParams(vmem_limit_bytes=VMEM_LIMIT),
        cost_estimate=pl.CostEstimate(flops=1_300_000_000, transcendentals=0, bytes_accessed=10_000_000),
        name="fold",
    )(forcing, low, high)


def chebyshev():
    sigma = THETA / DELTA
    rho = 1.0 / sigma
    pairs = []
    for _ in range(ITERS - 1):
        rho_next = 1.0 / (2.0 * sigma - rho)
        pairs.append((rho_next * rho, 2.0 * rho_next / DELTA))
        rho = rho_next
    return pairs


def solve_kernel(scalars, slot_modes, forcing, block, *refs):
    planes = refs[:-12]
    out_ref, k_ref, y_ref, f_ref, p_two, p_three, b_two, b_three, stage, turned, sems, sem_out = refs[-12:]
    modes = block.shape[0]
    depth, padded, _ = k_ref.shape
    count = out_ref.shape[1]
    tiles = padded // FOLD
    blocks = LEN_Y // 128
    index = scalars[1]

    def cols(j):
        return slice(j * 128, (j + 1) * 128)

    def copies(t, slot):
        at = pl.ds(t * FOLD, FOLD)
        found = [pltpu.make_async_copy(block.at[:, at, :], stage.at[slot, pl.ds(0, modes)], sems.at[slot, 0])]
        for n, plane in enumerate(planes):
            found.append(pltpu.make_async_copy(plane.at[at, :], stage.at[slot, modes + n], sems.at[slot, n + 1]))
        return found

    for copy in copies(0, 0):
        copy.start()
    forcing_copy = pltpu.make_async_copy(forcing, f_ref, sems.at[2, 0])

    size = depth * FOLD
    row = lax.broadcasted_iota(jnp.int32, (size, size), 0)
    col = lax.broadcasted_iota(jnp.int32, (size, size), 1)
    mode = jnp.broadcast_to(slot_modes[...], (size, size))
    phase = ((2 * (row // FOLD) + 1) * mode).astype(jnp.float32)
    weight = jnp.where(mode == 0, math.sqrt(1.0 / depth), math.sqrt(2.0 / depth))
    cosine = cos_turns(turns_of(phase, 4.0 * depth), 1.0)
    mixing = jnp.where(row % FOLD == col % FOLD, weight * cosine, 0.0).astype(jnp.bfloat16)

    def inside(start):
        row = folded_row(lax.broadcasted_iota(jnp.int32, (FOLD, 128), 0) + start, tiles)
        outside = ((row < HALO) & (index == 0)) | ((row >= HALO + count) & (index == WIDE - 1))
        return jnp.where(outside, 0.0, 1.0)

    for t in range(tiles):
        slot = t % 2
        if t + 1 < tiles:
            for copy in copies(t + 1, 1 - slot):
                copy.start()
        else:
            forcing_copy.start()
        for copy in copies(t, slot):
            copy.wait()
        keep = inside(t * FOLD)
        for n in range(0, LEN_Y, 512):
            field = jnp.dot(
                mixing,
                stage[slot, :, :, n : n + 512].reshape(size, 512),
                preferred_element_type=jnp.float32,
            ).reshape(depth, FOLD, 512)
            for j in range(n // 128, n // 128 + 4):
                part = field[:, :, j * 128 - n : j * 128 - n + 128]
                value = jnp.exp(1.5 * jnp.tanh(2.0 * part)) * keep[None]
                k_ref[:, t * FOLD : t * FOLD + FOLD, cols(j)] = value.astype(jnp.bfloat16)
    lane = lax.broadcasted_iota(jnp.int32, (FOLD, 128), 1)
    nothing = jnp.zeros((FOLD, 128), jnp.bfloat16)

    def faces(g, carry):
        at = pl.ds(pl.multiple_of(g // (depth // 4) * FOLD, FOLD), FOLD)
        sums = []
        for u in range(4):
            z = g % (depth // 4) * 4 + u
            here = [k_ref[z, at, cols(j)] for j in range(blocks)]
            turns = [pltpu.roll(k, 127, 1) for k in here] + [nothing]
            sums.append((z, [here[j] + jnp.where(lane == 127, turns[j + 1], turns[j]) for j in range(blocks)]))
        for z, values in sums:
            for j in range(blocks):
                y_ref[z, at, cols(j)] = values[j]
        return carry

    lax.fori_loop(0, tiles * depth // 4, faces, 0)
    forcing_copy.wait()

    def sweep(src, store):
        def tile(i, below, above):
            at = pl.ds(pl.multiple_of(i * FOLD, FOLD), FOLD)
            factor = inside(i * FOLD)

            def level(z, top, flows_z):
                outs = []
                next_flows = []
                k_all = [k_ref[z, at, cols(j)] for j in range(blocks)]
                p_all = [src[z, at, cols(j)] for j in range(blocks)]
                turns = [pltpu.roll(p, 127, 1) for p in p_all] + [nothing]
                before = None
                for j in range(blocks):
                    k, p = k_all[j], p_all[j]
                    flow_y = y_ref[z, at, cols(j)] * (p - jnp.where(lane == 127, turns[j + 1], turns[j]))
                    flow_turn = pltpu.roll(flow_y, 1, 1)
                    left = jnp.where(lane == 0, -k * p if before is None else before, flow_turn)
                    before = flow_turn
                    if top:
                        flow_z = k * p
                    else:
                        flow_z = (k + k_ref[z + 1, at, cols(j)]) * (p - src[z + 1, at, cols(j)])
                    flow_x = (k + above(k_ref, z, j)) * (p - above(src, z, j))
                    flow_w = (k + below(k_ref, z, j)) * (p - below(src, z, j))
                    outs.append((flow_x + flow_w) + ((flow_y - left) + (flow_z - flows_z[j])))
                    next_flows.append(flow_z)
                return next_flows, outs

            def keep(z, outs):
                for j in range(blocks):
                    store(z, j, at, outs[j].astype(jnp.float32), factor)

            def levels(first, flows_z):
                found = []
                for u in range(UNROLL):
                    z = first + u
                    flows_z, outs = level(z, isinstance(z, int) and z == depth - 1, flows_z)
                    found.append(outs)
                for u, outs in enumerate(found):
                    keep(first + u, outs)
                return flows_z

            def group(g, flows_z):
                return levels(g * UNROLL, flows_z)

            flows = [-k_ref[0, at, cols(j)] * src[0, at, cols(j)] for j in range(blocks)]
            groups = depth // UNROLL - 1
            flows = lax.fori_loop(0, groups, group, flows)
            levels(groups * UNROLL, flows)

        def plain(step):
            def load(ref, z, j, i):
                return ref[z, pl.ds(pl.multiple_of((i + step) * FOLD, FOLD), FOLD), cols(j)]

            return load

        def first(ref, z, j):
            return pltpu.roll(ref[z, padded - FOLD : padded, cols(j)], 1, 0)

        def last(ref, z, j):
            return pltpu.roll(ref[z, 0:FOLD, cols(j)], FOLD - 1, 0)

        def inner(i, carry):
            tile(
                i,
                lambda ref, z, j: plain(-1)(ref, z, j, i),
                lambda ref, z, j: plain(1)(ref, z, j, i),
            )
            return carry

        tile(0, first, lambda ref, z, j: plain(1)(ref, z, j, 0))
        lax.fori_loop(1, tiles - 1, inner, 0)
        tile(tiles - 1, lambda ref, z, j: plain(-1)(ref, z, j, tiles - 1), last)

    (a1, b1), (a2, b2), (a3, b3) = chebyshev()

    def store_one(z, j, at, out, factor):
        source = f_ref[z, at, cols(j)].astype(jnp.float32)
        value = ((1.0 + a1) / THETA + b1) * source - (0.5 * b1 / THETA * factor) * out
        p_two[z, at, cols(j)] = value
        b_two[z, at, cols(j)] = value.astype(jnp.bfloat16)

    def store_two(z, j, at, out, factor):
        source = f_ref[z, at, cols(j)].astype(jnp.float32)
        value = (1.0 + a2) * p_two[z, at, cols(j)] + (b2 - a2 / THETA) * source - (0.5 * b2 * factor) * out
        p_three[z, at, cols(j)] = value
        b_three[z, at, cols(j)] = value.astype(jnp.bfloat16)

    def store_three(z, j, at, out, factor):
        source = f_ref[z, at, cols(j)].astype(jnp.float32)
        old = (1.0 + a3) * p_three[z, at, cols(j)] - a3 * p_two[z, at, cols(j)]
        b_two[z, at, cols(j)] = (old + (b3 * source - 0.5 * b3 * out)).astype(jnp.bfloat16)

    sweep(f_ref, store_one)
    sweep(b_two, store_two)
    sweep(b_three, store_three)

    shape = (count, padded)
    place = folded_row(lax.broadcasted_iota(jnp.int32, shape, 1), tiles)
    unfold = (lax.broadcasted_iota(jnp.int32, shape, 0) + HALO == place).astype(jnp.bfloat16)

    def leave(z, slot):
        return pltpu.make_async_copy(turned.at[slot], out_ref.at[z], sem_out.at[slot])

    for z in range(depth):
        slot = z % 2
        if z > 1:
            leave(z - 2, slot).wait()
        for n in range(0, LEN_Y, 512):
            turned[slot, :, n : n + 512] = jnp.dot(
                unfold, b_two[z, :, n : n + 512], preferred_element_type=jnp.float32
            ).astype(jnp.bfloat16)
        leave(z, slot).start()
    for z in (depth - 2, depth - 1):
        leave(z, z % 2).wait()


def solve(scalars, slot_modes, forcing, block, planes, count):
    depth, padded, _ = forcing.shape
    anywhere = pl.BlockSpec(memory_space=pl.ANY)
    narrow = pltpu.VMEM((depth, padded, LEN_Y), jnp.bfloat16)
    whole = pltpu.VMEM((depth, padded, LEN_Y), jnp.float32)
    return pl.pallas_call(
        solve_kernel,
        in_specs=[pl.BlockSpec(memory_space=pltpu.SMEM), pl.BlockSpec(memory_space=pltpu.VMEM)]
        + [anywhere] * (2 + len(planes)),
        out_specs=anywhere,
        out_shape=jax.ShapeDtypeStruct((depth, count, LEN_Y), jnp.bfloat16),
        scratch_shapes=[
            narrow,
            narrow,
            narrow,
            whole,
            whole,
            narrow,
            narrow,
            pltpu.VMEM((2, depth, FOLD, LEN_Y), jnp.bfloat16),
            pltpu.VMEM((2, count, LEN_Y), jnp.bfloat16),
            pltpu.SemaphoreType.DMA((3, 1 + len(planes))),
            pltpu.SemaphoreType.DMA((2,)),
        ],
        compiler_params=pltpu.CompilerParams(vmem_limit_bytes=VMEM_LIMIT),
        name="solve",
    )(scalars, slot_modes, forcing, block, *planes)


def body(stream_index, forcing):
    depth, count, _ = forcing.shape
    index = lax.axis_index("wide")
    scalars = jnp.stack([scramble(stream_index[0] ^ 1540483477), index]).astype(jnp.int32)
    tiles = -(-(count + 2 * HALO) // FOLD)
    padded = tiles * FOLD
    own, basis, folded = first_planes(scalars, depth, count, tiles)
    groups = [list(range(8)), list(range(8, 16))]
    block = lax.all_to_all(
        own.reshape(8, padded, LEN_Y), "wide", 0, 0, axis_index_groups=groups, tiled=True
    )

    def pairwise(offset):
        out = more_planes(scalars, basis, folded, depth, padded, offset)
        routes = [
            [(i, i ^ 1) for i in range(WIDE)],
            [(i, i ^ beside_bit(i & 1, offset)) for i in range(WIDE)],
            [(i, i ^ beside_bit(i & 1, offset) ^ 1) for i in range(WIDE)],
        ]
        return [out[0]] + [lax.ppermute(piece, "wide", route) for piece, route in zip(out[1:], routes)]

    planes = pairwise(0) + pairwise(1)
    slot = lax.broadcasted_iota(jnp.int32, (1, depth * FOLD), 1) // FOLD
    offset = (slot >= 12).astype(jnp.int32)
    source = index ^ (slot & 1)
    source = source ^ jnp.where((slot & 2) == 0, 0, beside_bit(source & 1, offset))
    slot_modes = jnp.where(slot < 8, slot, shared_mode(source, depth) + offset)
    forward = [(i, i + 1) for i in range(WIDE - 1)]
    backward = [(target, source) for source, target in forward]
    low = lax.ppermute(forcing[:, -HALO:], "wide", forward)
    high = lax.ppermute(forcing[:, :HALO], "wide", backward)
    return solve(scalars, slot_modes, fold(forcing, low, high, padded), block, planes, count)


def solution(mesh):
    special = mesh.shape["wide"] == WIDE
    return jax.shard_map(
        body if special else plain_body,
        mesh=mesh,
        in_specs=(P("group"), P("group", "wide", None)),
        out_specs=P("group", "wide", None),
        check_vma=False,
    )
```

```python
import functools
import math

import jax
import jax.numpy as jnp
from jax import lax
from jax.experimental import pallas as pl
from jax.experimental.pallas import tpu as pltpu
from jax.sharding import PartitionSpec as P

LEN_X = 1536
LEN_Y = 1536
ITERS = 4


def with_halo(block, sides, width):
    for axis, dim in sides:
        count = lax.axis_size(axis)
        forward = [(i, i + 1) for i in range(count - 1)]
        backward = [(target, source) for source, target in forward]
        low = lax.ppermute(
            lax.slice_in_dim(block, block.shape[dim] - width, None, axis=dim), axis, forward
        )
        high = lax.ppermute(lax.slice_in_dim(block, 0, width, axis=dim), axis, backward)
        block = jnp.concatenate([low, block, high], axis=dim)
    return block


def scramble(value):
    value = value ^ value >> 16 & 65535
    value = value * 73244475
    value = value ^ value >> 16 & 65535
    value = value * 73244475
    value = value ^ value >> 16 & 65535
    return value


def cosine_basis(length):
    row_idx = lax.broadcasted_iota(jnp.int32, (length, length), 0)
    mode_idx = lax.broadcasted_iota(jnp.int32, (length, length), 1)
    phase = (2 * row_idx + 1) * mode_idx % (4 * length)
    angle = phase.astype(jnp.float32) * (math.pi / (2.0 * length))
    weights = jnp.where(mode_idx == 0, math.sqrt(1.0 / length), math.sqrt(2.0 / length))
    return (weights * jnp.cos(angle)).astype(jnp.bfloat16)


def coefficient_plane(stream_key, mode_z, depth):
    mode_x = lax.broadcasted_iota(jnp.int32, (LEN_X, LEN_Y), 0)
    mode_y = lax.broadcasted_iota(jnp.int32, (LEN_X, LEN_Y), 1)
    counter = (mode_z * LEN_X + mode_x) * LEN_Y + mode_y
    bits_a = scramble(2 * counter ^ stream_key)
    bits_b = scramble(2 * counter + 1 ^ stream_key)
    uniform_a = (bits_a >> 8 & 16777215).astype(jnp.float32) * 2.0 ** (-24) + 2.0 ** (-25)
    uniform_b = (bits_b >> 8 & 16777215).astype(jnp.float32) * 2.0 ** (-24) + 2.0 ** (-25)
    noise = jnp.sqrt(-2.0 * jnp.log(uniform_a)) * jnp.cos(2.0 * math.pi * uniform_b)
    freq_x = mode_x.astype(jnp.float32) * (math.pi / LEN_X)
    freq_y = mode_y.astype(jnp.float32) * (math.pi / LEN_Y)
    freq_z = mode_z.astype(jnp.float32) * (math.pi / depth)
    amplitude = 1.0 / jnp.sqrt(0.05 + freq_x * freq_x + freq_y * freq_y + freq_z * freq_z)
    return (amplitude * noise).astype(jnp.bfloat16)


def contract_last(left, table):
    return lax.dot_general(
        left, table, (((left.ndim - 1,), (1,)), ((), ())), preferred_element_type=jnp.float32
    )


def operate(wide_p, wide_k):
    center_p = wide_p[:, 1:-1]
    center_k = wide_k[:, 1:-1]
    total = 0.5 * (center_k + wide_k[:, 2:]) * (center_p - wide_p[:, 2:])
    total = total + 0.5 * (center_k + wide_k[:, :-2]) * (center_p - wide_p[:, :-2])
    for axis in (0, 2):
        widths = [(0, 0), (0, 0), (0, 0)]
        widths[axis] = (1, 1)
        padded_p = jnp.pad(center_p, widths)
        padded_k = jnp.pad(center_k, widths)
        size_here = center_p.shape[axis]
        for start in (0, 2):
            near_p = lax.slice_in_dim(padded_p, start, start + size_here, axis=axis)
            near_k = lax.slice_in_dim(padded_k, start, start + size_here, axis=axis)
            total = total + 0.5 * (center_k + near_k) * (center_p - near_p)
    return total


def plain_body(stream_index, forcing):
    depth = forcing.shape[0]
    planes_here = depth // lax.axis_size("wide")
    stream_key = scramble(stream_index[0] ^ 1540483477)
    basis_x = cosine_basis(LEN_X)
    basis_y = cosine_basis(LEN_Y)
    basis_z = cosine_basis(depth)
    first_mode = lax.axis_index("wide") * planes_here
    own_modes = first_mode + jnp.arange(planes_here, dtype=jnp.int32)

    def rows_for(mode_z):
        coeff = coefficient_plane(stream_key, mode_z, depth)
        return jnp.dot(basis_x, coeff, preferred_element_type=jnp.float32).astype(jnp.bfloat16)

    def both_axes(mode_z):
        return contract_last(rows_for(mode_z), basis_y).astype(jnp.bfloat16)

    planes = lax.map(both_axes, own_modes)
    block = lax.all_to_all(planes, "wide", split_axis=1, concat_axis=0, tiled=True)
    count_z, count_x, count_y = block.shape
    field = jnp.dot(
        basis_z, block.reshape(count_z, count_x * count_y), preferred_element_type=jnp.float32
    )
    field = field.reshape(count_z, count_x, count_y)
    perm = jnp.exp(1.5 * jnp.tanh(2.0 * field))
    source = forcing.astype(jnp.float32)
    theta = 27.9
    delta = 26.1
    sigma = theta / delta
    rho = 1.0 / sigma
    step = source / theta
    press = step
    perm_wide = with_halo(perm.astype(jnp.bfloat16), (("wide", 1),), 1).astype(perm.dtype)
    for count in range(ITERS - 1):
        press_wide = with_halo(press, (("wide", 1),), 1)
        resid = source - operate(press_wide, perm_wide)
        rho_next = 1.0 / (2.0 * sigma - rho)
        step = rho_next * rho * step + 2.0 * rho_next / delta * resid
        press = press + step
        rho = rho_next
    return press.astype(jnp.bfloat16)


WIDE = 16
DEPTH = 16
HALO = ITERS - 1
PARTS = 4
UNROLL = 4
TILE = 16
FOLD = 16
VMEM_LIMIT = 60 << 20
THETA = 27.9
DELTA = 26.1
SIN_PI = (
    3.141592640144167, -5.16771008404795, 2.550077528430638, -0.5982912997813382, 0.077657661199004
)
MULT = 73244475


def cos_turns(turns, amplitude, negative=False):
    coeffs = [c * math.sqrt(2.0 * amplitude) for c in SIN_PI]
    square = turns * turns
    poly = coeffs[4] * square + coeffs[3]
    for c in coeffs[2::-1]:
        poly = poly * square + c
    sine = poly * turns
    return sine * sine - amplitude if negative else amplitude - sine * sine


def turns_of(phase, period):
    return (phase - jnp.floor(phase * (1.0 / period) + 0.5) * period) * (1.0 / period)


def srl(value, count):
    return lax.shift_right_logical(value, jnp.int32(count))


def angle_tables(cos_out, sin_out, of_row, length, weighted):
    period = 4.0 * length

    def part(i, carry):
        r = lax.broadcasted_iota(jnp.int32, (8, 128), 0) + i * 8
        factor = of_row(r).astype(jnp.float32)
        at = pl.ds(pl.multiple_of(i * 8, 8), 8)
        for j in range(length // 128):
            k = lax.broadcasted_iota(jnp.int32, (8, 128), 1).astype(jnp.float32) + 128.0 * j
            phase = factor * k
            cosine = cos_turns(turns_of(phase, period), 1.0)
            sine = cos_turns(turns_of(phase - length, period), 1.0)
            if weighted:
                weight = jnp.where(k == 0.0, math.sqrt(1.0 / length), math.sqrt(2.0 / length))
                cosine = cosine * weight
                sine = sine * weight
            cos_out[at, j * 128 : (j + 1) * 128] = cosine
            sin_out[at, j * 128 : (j + 1) * 128] = sine
        return carry

    lax.fori_loop(0, cos_out.shape[0] // 8, part, 0)


def angle_sums(out, first, second):
    rows, length = second[0].shape
    for m in range(out[0].shape[0] // rows):
        for j in range(length // 128):
            cols = slice(j * 128, (j + 1) * 128)
            cos_a, sin_a = first[0][m : m + 1, cols], first[1][m : m + 1, cols]
            cos_b, sin_b = second[0][:, cols], second[1][:, cols]
            out[0][m * rows : (m + 1) * rows, cols] = cos_a * cos_b - sin_a * sin_b
            out[1][m * rows : (m + 1) * rows, cols] = sin_a * cos_b + cos_a * sin_b


def basis_into(out_ref, small, big, first, second):
    rows = small[0].shape[0]
    length = out_ref.shape[1]
    angle_tables(*first, lambda m: 16 * m, length, True)
    angle_tables(*second, lambda r: 2 * r + 1, length, False)
    angle_sums(small, first, second)
    angle_tables(*big, lambda t: 2 * rows * t, length, False)

    def group(g, carry):
        group_at = pl.ds(pl.multiple_of(g * 8, 8), 8)
        for j in range(length // 128):
            cols = slice(j * 128, (j + 1) * 128)
            big_cos = big[0][group_at, cols]
            big_sin = big[1][group_at, cols]
            for t in range(8):
                at = pl.ds(pl.multiple_of((g * 8 + t) * rows, rows), rows)
                value = small[0][:, cols] * big_cos[t : t + 1] - small[1][:, cols] * big_sin[t : t + 1]
                out_ref[at, cols] = value.astype(jnp.bfloat16)
        return carry

    lax.fori_loop(0, big[0].shape[0] // 8, group, 0)


def folded_basis_into(out_ref, small, big, first, second, first_row, count, tiles):
    length = out_ref.shape[1]

    angle_tables(*first, lambda d: 2 * (first_row + d * count - HALO) + 1, length, True)
    angle_tables(*second, lambda r: 2 * tiles * r, length, False)
    angle_sums(small, first, second)
    angle_tables(*big, lambda i: 2 * i, length, False)

    def device(d, carry):
        at = pl.ds(pl.multiple_of(d * FOLD, FOLD), FOLD)
        for i in range(tiles):
            to = pl.ds(pl.multiple_of((d * tiles + i) * FOLD, FOLD), FOLD)
            for j in range(length // 128):
                cols = slice(j * 128, (j + 1) * 128)
                value = small[0][at, cols] * big[0][i : i + 1, cols] - small[1][at, cols] * big[1][i : i + 1, cols]
                out_ref[to, cols] = value.astype(jnp.bfloat16)
        return carry

    lax.fori_loop(0, small[0].shape[0] // FOLD, device, 0)


def coefficients_into(out_ref, key, mode_z, depth, rows):
    const = 2.0 * math.log(2.0)
    key_low = key & 1023
    key_high = key & ~1023

    def part(i, carry):
        r = lax.broadcasted_iota(jnp.int32, (rows, 128), 0) + i * rows
        at = pl.ds(pl.multiple_of(i * rows, rows), rows)
        freq_x = r.astype(jnp.float32) * (math.pi / LEN_X)
        freq_z = mode_z.astype(jnp.float32) * (math.pi / depth)
        row_part = (0.05 + freq_x * freq_x + freq_z * freq_z) * -const
        base = (r + mode_z * LEN_X) * (2 * LEN_Y)
        lane = lax.broadcasted_iota(jnp.int32, (1, 128), 1)
        for j in range(LEN_Y // 128):
            if j % 4 == 0:
                top = (base + j * 256) ^ key_high
                top = top ^ srl(top, 16)
                delta = jnp.where(((top ^ key_low) & 1) == 0, MULT, -MULT)
            freq_y = (lane + j * 128).astype(jnp.float32) * (math.pi / LEN_Y)
            denom = row_part + freq_y * freq_y * -const
            a = (top ^ (((lane + (j % 4) * 128) * 2) ^ key_low)) * MULT
            b = a + delta
            a = (a ^ srl(a, 16)) * MULT
            b = (b ^ srl(b, 16)) * MULT
            a = srl(a ^ srl(a, 16), 8)
            b = (b ^ srl(b, 16)) >> 8
            u = a.astype(jnp.float32) * 2.0 ** (-24) + 2.0 ** (-25)
            turns = b.astype(jnp.float32) * 2.0 ** (-24) + 2.0 ** (-25)
            bits = jnp.minimum(jnp.log2(u), -1e-30)
            size = bits * lax.rsqrt(bits * denom)
            value = size * cos_turns(turns, const, negative=True)
            out_ref[at, j * 128 : (j + 1) * 128] = value.astype(jnp.bfloat16)
        return carry

    lax.fori_loop(0, LEN_X // rows, part, 0)


def transform_into(out_refs, left_ref, coef_ref, rows_ref, basis_ref):
    for n in range(0, LEN_Y, 256):
        cols = slice(n, n + 256)
        rows_ref[:, cols] = jnp.dot(
            left_ref[...], coef_ref[:, cols], preferred_element_type=jnp.float32
        ).astype(jnp.bfloat16)
    size = rows_ref.shape[0] // len(out_refs)
    for n in range(0, LEN_Y, 256):
        cols = slice(n, n + 256)
        value = contract_last(rows_ref[...], basis_ref[cols, :])
        for m, out_ref in enumerate(out_refs):
            out_ref[:, cols] = value[m * size : (m + 1) * size].astype(jnp.bfloat16)


def first_planes_kernel(
    scalars, out_ref, basis_out, folded_out, basis, folded, coef, rows, small_cos, small_sin, big_cos, big_sin,
    one_cos, one_sin, two_cos, two_sin, sem, *, depth, count, tiles
):
    key, index = scalars[0], scalars[1]
    first = (one_cos, one_sin)
    second = (two_cos.at[pl.ds(0, 8)], two_sin.at[pl.ds(0, 8)])
    basis_into(
        basis, (small_cos.at[pl.ds(0, 64)], small_sin.at[pl.ds(0, 64)]), (big_cos, big_sin), first, second
    )
    folded_basis_into(
        folded,
        (small_cos, small_sin),
        (big_cos.at[pl.ds(0, 8)], big_sin.at[pl.ds(0, 8)]),
        first,
        (two_cos, two_sin),
        (index >> 3) * (8 * count),
        count,
        tiles,
    )
    copies = [
        pltpu.make_async_copy(basis, basis_out, sem.at[0]),
        pltpu.make_async_copy(folded, folded_out, sem.at[1]),
    ]
    for copy in copies:
        copy.start()
    coefficients_into(coef, key, index & 7, depth, 64)
    transform_into([out_ref], folded, coef, rows, basis)
    for copy in copies:
        copy.wait()


def first_planes(scalars, depth, count, tiles):
    total = 8 * tiles * FOLD
    bits = jnp.bfloat16
    return pl.pallas_call(
        functools.partial(first_planes_kernel, depth=depth, count=count, tiles=tiles),
        in_specs=[pl.BlockSpec(memory_space=pltpu.SMEM)],
        out_specs=[pl.BlockSpec(memory_space=pltpu.VMEM)] + [pl.BlockSpec(memory_space=pl.ANY)] * 2,
        out_shape=[
            jax.ShapeDtypeStruct((total, LEN_Y), bits),
            jax.ShapeDtypeStruct((LEN_X, LEN_X), bits),
            jax.ShapeDtypeStruct((total, LEN_X), bits),
        ],
        scratch_shapes=[
            pltpu.VMEM((LEN_X, LEN_X), bits),
            pltpu.VMEM((total, LEN_X), bits),
            pltpu.VMEM((LEN_X, LEN_Y), bits),
            pltpu.VMEM((total, LEN_Y), bits),
            pltpu.VMEM((8 * FOLD, LEN_X), jnp.float32),
            pltpu.VMEM((8 * FOLD, LEN_X), jnp.float32),
            pltpu.VMEM((LEN_X // 64, LEN_X), jnp.float32),
            pltpu.VMEM((LEN_X // 64, LEN_X), jnp.float32),
            pltpu.VMEM((8, LEN_X), jnp.float32),
            pltpu.VMEM((8, LEN_X), jnp.float32),
            pltpu.VMEM((FOLD, LEN_X), jnp.float32),
            pltpu.VMEM((FOLD, LEN_X), jnp.float32),
            pltpu.SemaphoreType.DMA((2,)),
        ],
        compiler_params=pltpu.CompilerParams(vmem_limit_bytes=VMEM_LIMIT),
        cost_estimate=pl.CostEstimate(flops=25_000_000_000, transcendentals=0, bytes_accessed=8_000_000),
        name="first_planes",
    )(scalars)


def shared_mode(index, depth):
    color = (index >> 1 ^ index >> 2) & 1
    return depth // 2 + 4 * color + 2 * (index & 1)


def beside_bit(core, offset):
    return 4 >> (core ^ offset)


def more_planes_kernel(scalars, basis_in, folded_in, *refs, depth, offset):
    out_refs = refs[:PARTS]
    basis, left, coef, rows, sem = refs[PARTS:]
    size = out_refs[0].shape[0]
    key, index = scalars[0], scalars[1]
    mode = shared_mode(index, depth) + offset
    copies = [pltpu.make_async_copy(basis_in, basis, sem.at[PARTS])]
    bit = beside_bit(index & 1, offset)
    for n, flip in enumerate((0, 1, bit, bit ^ 1)):
        source = folded_in.at[pl.ds(pl.multiple_of((index & 7 ^ flip) * size, size), size), :]
        copies.append(pltpu.make_async_copy(source, left.at[pl.ds(n * size, size), :], sem.at[n]))
    for copy in copies:
        copy.start()
    coefficients_into(coef, key, mode, depth, 64)
    for copy in copies:
        copy.wait()
    transform_into(out_refs, left, coef, rows, basis)


def more_planes(scalars, basis, folded, depth, size, offset):
    anywhere = pl.BlockSpec(memory_space=pl.ANY)
    return pl.pallas_call(
        functools.partial(more_planes_kernel, depth=depth, offset=offset),
        in_specs=[pl.BlockSpec(memory_space=pltpu.SMEM), anywhere, anywhere],
        out_specs=[pl.BlockSpec(memory_space=pltpu.VMEM)] * PARTS,
        out_shape=[jax.ShapeDtypeStruct((size, LEN_Y), jnp.bfloat16)] * PARTS,
        scratch_shapes=[
            pltpu.VMEM((LEN_X, LEN_X), jnp.bfloat16),
            pltpu.VMEM((PARTS * size, LEN_X), jnp.bfloat16),
            pltpu.VMEM((LEN_X, LEN_Y), jnp.bfloat16),
            pltpu.VMEM((PARTS * size, LEN_Y), jnp.bfloat16),
            pltpu.SemaphoreType.DMA((PARTS + 1,)),
        ],
        compiler_params=pltpu.CompilerParams(vmem_limit_bytes=VMEM_LIMIT),
        cost_estimate=pl.CostEstimate(flops=20_000_000_000, transcendentals=0, bytes_accessed=8_000_000),
        name="more_planes",
    )(scalars, basis, folded)


def folded_row(index, tiles):
    return index % FOLD * tiles + index // FOLD


def fold_kernel(f_ref, low_ref, high_ref, out_ref, edge):
    _, count, _ = f_ref.shape
    padded = out_ref.shape[1]
    shape = (padded, count + TILE)
    row = folded_row(lax.broadcasted_iota(jnp.int32, shape, 0), padded // FOLD)
    source = jnp.where(row < HALO, row + count, jnp.where(row < HALO + count, row - HALO, row))
    spread = (lax.broadcasted_iota(jnp.int32, shape, 1) == source).astype(jnp.bfloat16)

    @pl.when(pl.program_id(0) == 0)
    def _():
        edge[...] = jnp.zeros(edge.shape, edge.dtype)

    for m in range(f_ref.shape[0]):
        edge[0:HALO, :] = low_ref[m]
        edge[HALO : 2 * HALO, :] = high_ref[m]
        rows = jnp.concatenate([f_ref[m], edge[...]], axis=0)
        for n in range(0, LEN_Y, 512):
            cols = slice(n, n + 512)
            out_ref[m, :, cols] = jnp.dot(spread, rows[:, cols], preferred_element_type=jnp.float32).astype(
                jnp.bfloat16
            )


def fold(forcing, low, high, padded):
    depth, count, _ = forcing.shape
    return pl.pallas_call(
        fold_kernel,
        grid=(depth // 2,),
        in_specs=[
            pl.BlockSpec((2, count, LEN_Y), lambda z: (z, 0, 0)),
            pl.BlockSpec((2, HALO, LEN_Y), lambda z: (z, 0, 0)),
            pl.BlockSpec((2, HALO, LEN_Y), lambda z: (z, 0, 0)),
        ],
        out_specs=pl.BlockSpec((2, padded, LEN_Y), lambda z: (z, 0, 0)),
        out_shape=jax.ShapeDtypeStruct((depth, padded, LEN_Y), jnp.bfloat16),
        scratch_shapes=[pltpu.VMEM((TILE, LEN_Y), jnp.bfloat16)],
        compiler_params=pltpu.CompilerParams(vmem_limit_bytes=VMEM_LIMIT),
        cost_estimate=pl.CostEstimate(flops=1_300_000_000, transcendentals=0, bytes_accessed=10_000_000),
        name="fold",
    )(forcing, low, high)


def chebyshev():
    sigma = THETA / DELTA
    rho = 1.0 / sigma
    pairs = []
    for _ in range(ITERS - 1):
        rho_next = 1.0 / (2.0 * sigma - rho)
        pairs.append((rho_next * rho, 2.0 * rho_next / DELTA))
        rho = rho_next
    return pairs


def solve_kernel(scalars, slot_modes, forcing, block, *refs):
    planes = refs[:-12]
    out_ref, k_ref, y_ref, f_ref, p_two, p_three, b_two, b_three, stage, turned, sems, sem_out = refs[-12:]
    modes = block.shape[0]
    depth, padded, _ = k_ref.shape
    count = out_ref.shape[1]
    tiles = padded // FOLD
    blocks = LEN_Y // 128
    index = scalars[1]

    def cols(j):
        return slice(j * 128, (j + 1) * 128)

    def copies(t, slot):
        at = pl.ds(t * FOLD, FOLD)
        found = [pltpu.make_async_copy(block.at[:, at, :], stage.at[slot, pl.ds(0, modes)], sems.at[slot, 0])]
        for n, plane in enumerate(planes):
            found.append(pltpu.make_async_copy(plane.at[at, :], stage.at[slot, modes + n], sems.at[slot, n + 1]))
        return found

    for copy in copies(0, 0):
        copy.start()
    forcing_copy = pltpu.make_async_copy(forcing, f_ref, sems.at[2, 0])

    size = depth * FOLD
    row = lax.broadcasted_iota(jnp.int32, (size, size), 0)
    col = lax.broadcasted_iota(jnp.int32, (size, size), 1)
    mode = jnp.broadcast_to(slot_modes[...], (size, size))
    phase = ((2 * (row // FOLD) + 1) * mode).astype(jnp.float32)
    weight = jnp.where(mode == 0, math.sqrt(1.0 / depth), math.sqrt(2.0 / depth))
    cosine = cos_turns(turns_of(phase, 4.0 * depth), 1.0)
    mixing = jnp.where(row % FOLD == col % FOLD, weight * cosine, 0.0).astype(jnp.bfloat16)

    def inside(start):
        row = folded_row(lax.broadcasted_iota(jnp.int32, (FOLD, 128), 0) + start, tiles)
        outside = ((row < HALO) & (index == 0)) | ((row >= HALO + count) & (index == WIDE - 1))
        return jnp.where(outside, 0.0, 1.0)

    for t in range(tiles):
        slot = t % 2
        if t + 1 < tiles:
            for copy in copies(t + 1, 1 - slot):
                copy.start()
        else:
            forcing_copy.start()
        for copy in copies(t, slot):
            copy.wait()
        keep = inside(t * FOLD)
        for n in range(0, LEN_Y, 512):
            field = jnp.dot(
                mixing,
                stage[slot, :, :, n : n + 512].reshape(size, 512),
                preferred_element_type=jnp.float32,
            ).reshape(depth, FOLD, 512)
            for j in range(n // 128, n // 128 + 4):
                part = field[:, :, j * 128 - n : j * 128 - n + 128]
                value = jnp.exp(1.5 * jnp.tanh(2.0 * part)) * keep[None]
                k_ref[:, t * FOLD : t * FOLD + FOLD, cols(j)] = value.astype(jnp.bfloat16)
    lane = lax.broadcasted_iota(jnp.int32, (FOLD, 128), 1)
    nothing = jnp.zeros((FOLD, 128), jnp.bfloat16)

    def faces(g, carry):
        at = pl.ds(pl.multiple_of(g // (depth // 4) * FOLD, FOLD), FOLD)
        sums = []
        for u in range(4):
            z = g % (depth // 4) * 4 + u
            here = [k_ref[z, at, cols(j)] for j in range(blocks)]
            turns = [pltpu.roll(k, 127, 1) for k in here] + [nothing]
            sums.append((z, [here[j] + jnp.where(lane == 127, turns[j + 1], turns[j]) for j in range(blocks)]))
        for z, values in sums:
            for j in range(blocks):
                y_ref[z, at, cols(j)] = values[j]
        return carry

    lax.fori_loop(0, tiles * depth // 4, faces, 0)
    forcing_copy.wait()

    def sweep(src, store):
        def tile(i, below, above):
            at = pl.ds(pl.multiple_of(i * FOLD, FOLD), FOLD)
            factor = inside(i * FOLD)

            def level(z, top, flows_z):
                outs = []
                next_flows = []
                k_all = [k_ref[z, at, cols(j)] for j in range(blocks)]
                p_all = [src[z, at, cols(j)] for j in range(blocks)]
                turns = [pltpu.roll(p, 127, 1) for p in p_all] + [nothing]
                before = None
                for j in range(blocks):
                    k, p = k_all[j], p_all[j]
                    flow_y = y_ref[z, at, cols(j)] * (p - jnp.where(lane == 127, turns[j + 1], turns[j]))
                    flow_turn = pltpu.roll(flow_y, 1, 1)
                    left = jnp.where(lane == 0, -k * p if before is None else before, flow_turn)
                    before = flow_turn
                    if top:
                        flow_z = k * p
                    else:
                        flow_z = (k + k_ref[z + 1, at, cols(j)]) * (p - src[z + 1, at, cols(j)])
                    flow_x = (k + above(k_ref, z, j)) * (p - above(src, z, j))
                    flow_w = (k + below(k_ref, z, j)) * (p - below(src, z, j))
                    outs.append((flow_x + flow_w) + ((flow_y - left) + (flow_z - flows_z[j])))
                    next_flows.append(flow_z)
                return next_flows, outs

            def keep(z, outs):
                for j in range(blocks):
                    store(z, j, at, outs[j].astype(jnp.float32), factor)

            def levels(first, flows_z):
                found = []
                for u in range(UNROLL):
                    z = first + u
                    flows_z, outs = level(z, isinstance(z, int) and z == depth - 1, flows_z)
                    found.append(outs)
                for u, outs in enumerate(found):
                    keep(first + u, outs)
                return flows_z

            def group(g, flows_z):
                return levels(g * UNROLL, flows_z)

            flows = [-k_ref[0, at, cols(j)] * src[0, at, cols(j)] for j in range(blocks)]
            groups = depth // UNROLL - 1
            flows = lax.fori_loop(0, groups, group, flows)
            levels(groups * UNROLL, flows)

        def plain(step):
            def load(ref, z, j, i):
                return ref[z, pl.ds(pl.multiple_of((i + step) * FOLD, FOLD), FOLD), cols(j)]

            return load

        def first(ref, z, j):
            return pltpu.roll(ref[z, padded - FOLD : padded, cols(j)], 1, 0)

        def last(ref, z, j):
            return pltpu.roll(ref[z, 0:FOLD, cols(j)], FOLD - 1, 0)

        def inner(i, carry):
            tile(
                i,
                lambda ref, z, j: plain(-1)(ref, z, j, i),
                lambda ref, z, j: plain(1)(ref, z, j, i),
            )
            return carry

        tile(0, first, lambda ref, z, j: plain(1)(ref, z, j, 0))
        lax.fori_loop(1, tiles - 1, inner, 0)
        tile(tiles - 1, lambda ref, z, j: plain(-1)(ref, z, j, tiles - 1), last)

    (a1, b1), (a2, b2), (a3, b3) = chebyshev()

    def store_one(z, j, at, out, factor):
        source = f_ref[z, at, cols(j)].astype(jnp.float32)
        value = ((1.0 + a1) / THETA + b1) * source - (0.5 * b1 / THETA * factor) * out
        p_two[z, at, cols(j)] = value
        b_two[z, at, cols(j)] = value.astype(jnp.bfloat16)

    def store_two(z, j, at, out, factor):
        source = f_ref[z, at, cols(j)].astype(jnp.float32)
        value = (1.0 + a2) * p_two[z, at, cols(j)] + (b2 - a2 / THETA) * source - (0.5 * b2 * factor) * out
        p_three[z, at, cols(j)] = value
        b_three[z, at, cols(j)] = value.astype(jnp.bfloat16)

    def store_three(z, j, at, out, factor):
        source = f_ref[z, at, cols(j)].astype(jnp.float32)
        old = (1.0 + a3) * p_three[z, at, cols(j)] - a3 * p_two[z, at, cols(j)]
        b_two[z, at, cols(j)] = (old + (b3 * source - 0.5 * b3 * out)).astype(jnp.bfloat16)

    sweep(f_ref, store_one)
    sweep(b_two, store_two)
    sweep(b_three, store_three)

    shape = (count, padded)
    place = folded_row(lax.broadcasted_iota(jnp.int32, shape, 1), tiles)
    unfold = (lax.broadcasted_iota(jnp.int32, shape, 0) + HALO == place).astype(jnp.bfloat16)

    def leave(z, slot):
        return pltpu.make_async_copy(turned.at[slot], out_ref.at[z], sem_out.at[slot])

    for z in range(depth):
        slot = z % 2
        if z > 1:
            leave(z - 2, slot).wait()
        for n in range(0, LEN_Y, 512):
            turned[slot, :, n : n + 512] = jnp.dot(
                unfold, b_two[z, :, n : n + 512], preferred_element_type=jnp.float32
            ).astype(jnp.bfloat16)
        leave(z, slot).start()
    for z in (depth - 2, depth - 1):
        leave(z, z % 2).wait()


def solve(scalars, slot_modes, forcing, block, planes, count):
    depth, padded, _ = forcing.shape
    anywhere = pl.BlockSpec(memory_space=pl.ANY)
    narrow = pltpu.VMEM((depth, padded, LEN_Y), jnp.bfloat16)
    whole = pltpu.VMEM((depth, padded, LEN_Y), jnp.float32)
    return pl.pallas_call(
        solve_kernel,
        in_specs=[pl.BlockSpec(memory_space=pltpu.SMEM), pl.BlockSpec(memory_space=pltpu.VMEM)]
        + [anywhere] * (2 + len(planes)),
        out_specs=anywhere,
        out_shape=jax.ShapeDtypeStruct((depth, count, LEN_Y), jnp.bfloat16),
        scratch_shapes=[
            narrow,
            narrow,
            narrow,
            whole,
            whole,
            narrow,
            narrow,
            pltpu.VMEM((2, depth, FOLD, LEN_Y), jnp.bfloat16),
            pltpu.VMEM((2, count, LEN_Y), jnp.bfloat16),
            pltpu.SemaphoreType.DMA((3, 1 + len(planes))),
            pltpu.SemaphoreType.DMA((2,)),
        ],
        compiler_params=pltpu.CompilerParams(vmem_limit_bytes=VMEM_LIMIT),
        name="solve",
    )(scalars, slot_modes, forcing, block, *planes)


def body(stream_index, forcing):
    depth, count, _ = forcing.shape
    index = lax.axis_index("wide")
    scalars = jnp.stack([scramble(stream_index[0] ^ 1540483477), index]).astype(jnp.int32)
    tiles = -(-(count + 2 * HALO) // FOLD)
    padded = tiles * FOLD
    own, basis, folded = first_planes(scalars, depth, count, tiles)
    groups = [list(range(8)), list(range(8, 16))]
    block = lax.all_to_all(
        own.reshape(8, padded, LEN_Y), "wide", 0, 0, axis_index_groups=groups, tiled=True
    )

    def pairwise(offset):
        out = more_planes(scalars, basis, folded, depth, padded, offset)
        routes = [
            [(i, i ^ 1) for i in range(WIDE)],
            [(i, i ^ beside_bit(i & 1, offset)) for i in range(WIDE)],
            [(i, i ^ beside_bit(i & 1, offset) ^ 1) for i in range(WIDE)],
        ]
        return [out[0]] + [lax.ppermute(piece, "wide", route) for piece, route in zip(out[1:], routes)]

    planes = pairwise(0) + pairwise(1)
    slot = lax.broadcasted_iota(jnp.int32, (1, depth * FOLD), 1) // FOLD
    offset = (slot >= 12).astype(jnp.int32)
    source = index ^ (slot & 1)
    source = source ^ jnp.where((slot & 2) == 0, 0, beside_bit(source & 1, offset))
    slot_modes = jnp.where(slot < 8, slot, shared_mode(source, depth) + offset)
    forward = [(i, i + 1) for i in range(WIDE - 1)]
    backward = [(target, source) for source, target in forward]
    low = lax.ppermute(forcing[:, -HALO:], "wide", forward)
    high = lax.ppermute(forcing[:, :HALO], "wide", backward)
    return solve(scalars, slot_modes, fold(forcing, low, high, padded), block, planes, count)


def solution(mesh):
    special = mesh.shape["wide"] == WIDE
    return jax.shard_map(
        body if special else plain_body,
        mesh=mesh,
        in_specs=(P("group"), P("group", "wide", None)),
        out_specs=P("group", "wide", None),
        check_vma=False,
    )
```

```python
import functools
import math

import jax
import jax.numpy as jnp
from jax import lax
from jax.experimental import pallas as pl
from jax.experimental.pallas import tpu as pltpu
from jax.sharding import PartitionSpec as P

LEN_X = 1536
LEN_Y = 1536
ITERS = 4


def with_halo(block, sides, width):
    for axis, dim in sides:
        count = lax.axis_size(axis)
        forward = [(i, i + 1) for i in range(count - 1)]
        backward = [(target, source) for source, target in forward]
        low = lax.ppermute(
            lax.slice_in_dim(block, block.shape[dim] - width, None, axis=dim), axis, forward
        )
        high = lax.ppermute(lax.slice_in_dim(block, 0, width, axis=dim), axis, backward)
        block = jnp.concatenate([low, block, high], axis=dim)
    return block


def scramble(value):
    value = value ^ value >> 16 & 65535
    value = value * 73244475
    value = value ^ value >> 16 & 65535
    value = value * 73244475
    value = value ^ value >> 16 & 65535
    return value


def cosine_basis(length):
    row_idx = lax.broadcasted_iota(jnp.int32, (length, length), 0)
    mode_idx = lax.broadcasted_iota(jnp.int32, (length, length), 1)
    phase = (2 * row_idx + 1) * mode_idx % (4 * length)
    angle = phase.astype(jnp.float32) * (math.pi / (2.0 * length))
    weights = jnp.where(mode_idx == 0, math.sqrt(1.0 / length), math.sqrt(2.0 / length))
    return (weights * jnp.cos(angle)).astype(jnp.bfloat16)


def coefficient_plane(stream_key, mode_z, depth):
    mode_x = lax.broadcasted_iota(jnp.int32, (LEN_X, LEN_Y), 0)
    mode_y = lax.broadcasted_iota(jnp.int32, (LEN_X, LEN_Y), 1)
    counter = (mode_z * LEN_X + mode_x) * LEN_Y + mode_y
    bits_a = scramble(2 * counter ^ stream_key)
    bits_b = scramble(2 * counter + 1 ^ stream_key)
    uniform_a = (bits_a >> 8 & 16777215).astype(jnp.float32) * 2.0 ** (-24) + 2.0 ** (-25)
    uniform_b = (bits_b >> 8 & 16777215).astype(jnp.float32) * 2.0 ** (-24) + 2.0 ** (-25)
    noise = jnp.sqrt(-2.0 * jnp.log(uniform_a)) * jnp.cos(2.0 * math.pi * uniform_b)
    freq_x = mode_x.astype(jnp.float32) * (math.pi / LEN_X)
    freq_y = mode_y.astype(jnp.float32) * (math.pi / LEN_Y)
    freq_z = mode_z.astype(jnp.float32) * (math.pi / depth)
    amplitude = 1.0 / jnp.sqrt(0.05 + freq_x * freq_x + freq_y * freq_y + freq_z * freq_z)
    return (amplitude * noise).astype(jnp.bfloat16)


def contract_last(left, table):
    return lax.dot_general(
        left, table, (((left.ndim - 1,), (1,)), ((), ())), preferred_element_type=jnp.float32
    )


def operate(wide_p, wide_k):
    center_p = wide_p[:, 1:-1]
    center_k = wide_k[:, 1:-1]
    total = 0.5 * (center_k + wide_k[:, 2:]) * (center_p - wide_p[:, 2:])
    total = total + 0.5 * (center_k + wide_k[:, :-2]) * (center_p - wide_p[:, :-2])
    for axis in (0, 2):
        widths = [(0, 0), (0, 0), (0, 0)]
        widths[axis] = (1, 1)
        padded_p = jnp.pad(center_p, widths)
        padded_k = jnp.pad(center_k, widths)
        size_here = center_p.shape[axis]
        for start in (0, 2):
            near_p = lax.slice_in_dim(padded_p, start, start + size_here, axis=axis)
            near_k = lax.slice_in_dim(padded_k, start, start + size_here, axis=axis)
            total = total + 0.5 * (center_k + near_k) * (center_p - near_p)
    return total


def plain_body(stream_index, forcing):
    depth = forcing.shape[0]
    planes_here = depth // lax.axis_size("wide")
    stream_key = scramble(stream_index[0] ^ 1540483477)
    basis_x = cosine_basis(LEN_X)
    basis_y = cosine_basis(LEN_Y)
    basis_z = cosine_basis(depth)
    first_mode = lax.axis_index("wide") * planes_here
    own_modes = first_mode + jnp.arange(planes_here, dtype=jnp.int32)

    def rows_for(mode_z):
        coeff = coefficient_plane(stream_key, mode_z, depth)
        return jnp.dot(basis_x, coeff, preferred_element_type=jnp.float32).astype(jnp.bfloat16)

    def both_axes(mode_z):
        return contract_last(rows_for(mode_z), basis_y).astype(jnp.bfloat16)

    planes = lax.map(both_axes, own_modes)
    block = lax.all_to_all(planes, "wide", split_axis=1, concat_axis=0, tiled=True)
    count_z, count_x, count_y = block.shape
    field = jnp.dot(
        basis_z, block.reshape(count_z, count_x * count_y), preferred_element_type=jnp.float32
    )
    field = field.reshape(count_z, count_x, count_y)
    perm = jnp.exp(1.5 * jnp.tanh(2.0 * field))
    source = forcing.astype(jnp.float32)
    theta = 27.9
    delta = 26.1
    sigma = theta / delta
    rho = 1.0 / sigma
    step = source / theta
    press = step
    perm_wide = with_halo(perm.astype(jnp.bfloat16), (("wide", 1),), 1).astype(perm.dtype)
    for count in range(ITERS - 1):
        press_wide = with_halo(press, (("wide", 1),), 1)
        resid = source - operate(press_wide, perm_wide)
        rho_next = 1.0 / (2.0 * sigma - rho)
        step = rho_next * rho * step + 2.0 * rho_next / delta * resid
        press = press + step
        rho = rho_next
    return press.astype(jnp.bfloat16)


WIDE = 16
DEPTH = 16
HALO = ITERS - 1
PARTS = 4
UNROLL = 4
TILE = 16
FOLD = 16
VMEM_LIMIT = 60 << 20
THETA = 27.9
DELTA = 26.1
SIN_PI = (
    3.141592640144167, -5.16771008404795, 2.550077528430638, -0.5982912997813382, 0.077657661199004
)
MULT = 73244475


def cos_turns(turns, amplitude, negative=False):
    coeffs = [c * math.sqrt(2.0 * amplitude) for c in SIN_PI]
    square = turns * turns
    poly = coeffs[4] * square + coeffs[3]
    for c in coeffs[2::-1]:
        poly = poly * square + c
    sine = poly * turns
    return sine * sine - amplitude if negative else amplitude - sine * sine


def turns_of(phase, period):
    return (phase - jnp.floor(phase * (1.0 / period) + 0.5) * period) * (1.0 / period)


def srl(value, count):
    return lax.shift_right_logical(value, jnp.int32(count))


def angle_tables(cos_out, sin_out, of_row, length, weighted):
    period = 4.0 * length

    def part(i, carry):
        r = lax.broadcasted_iota(jnp.int32, (8, 128), 0) + i * 8
        factor = of_row(r).astype(jnp.float32)
        at = pl.ds(pl.multiple_of(i * 8, 8), 8)
        for j in range(length // 128):
            k = lax.broadcasted_iota(jnp.int32, (8, 128), 1).astype(jnp.float32) + 128.0 * j
            phase = factor * k
            cosine = cos_turns(turns_of(phase, period), 1.0)
            sine = cos_turns(turns_of(phase - length, period), 1.0)
            if weighted:
                weight = jnp.where(k == 0.0, math.sqrt(1.0 / length), math.sqrt(2.0 / length))
                cosine = cosine * weight
                sine = sine * weight
            cos_out[at, j * 128 : (j + 1) * 128] = cosine
            sin_out[at, j * 128 : (j + 1) * 128] = sine
        return carry

    lax.fori_loop(0, cos_out.shape[0] // 8, part, 0)


def angle_sums(out, first, second):
    rows, length = second[0].shape
    for m in range(out[0].shape[0] // rows):
        for j in range(length // 128):
            cols = slice(j * 128, (j + 1) * 128)
            cos_a, sin_a = first[0][m : m + 1, cols], first[1][m : m + 1, cols]
            cos_b, sin_b = second[0][:, cols], second[1][:, cols]
            out[0][m * rows : (m + 1) * rows, cols] = cos_a * cos_b - sin_a * sin_b
            out[1][m * rows : (m + 1) * rows, cols] = sin_a * cos_b + cos_a * sin_b


def basis_into(out_ref, small, big, first, second):
    rows = small[0].shape[0]
    length = out_ref.shape[1]
    angle_tables(*first, lambda m: 16 * m, length, True)
    angle_tables(*second, lambda r: 2 * r + 1, length, False)
    angle_sums(small, first, second)
    angle_tables(*big, lambda t: 2 * rows * t, length, False)

    def group(g, carry):
        group_at = pl.ds(pl.multiple_of(g * 8, 8), 8)
        for j in range(length // 128):
            cols = slice(j * 128, (j + 1) * 128)
            big_cos = big[0][group_at, cols]
            big_sin = big[1][group_at, cols]
            for t in range(8):
                at = pl.ds(pl.multiple_of((g * 8 + t) * rows, rows), rows)
                value = small[0][:, cols] * big_cos[t : t + 1] - small[1][:, cols] * big_sin[t : t + 1]
                out_ref[at, cols] = value.astype(jnp.bfloat16)
        return carry

    lax.fori_loop(0, big[0].shape[0] // 8, group, 0)


def folded_basis_into(out_ref, small, big, first, second, first_row, count, tiles):
    length = out_ref.shape[1]

    angle_tables(*first, lambda d: 2 * (first_row + d * count - HALO) + 1, length, True)
    angle_tables(*second, lambda r: 2 * tiles * r, length, False)
    angle_sums(small, first, second)
    angle_tables(*big, lambda i: 2 * i, length, False)

    def device(d, carry):
        at = pl.ds(pl.multiple_of(d * FOLD, FOLD), FOLD)
        for i in range(tiles):
            to = pl.ds(pl.multiple_of((d * tiles + i) * FOLD, FOLD), FOLD)
            for j in range(length // 128):
                cols = slice(j * 128, (j + 1) * 128)
                value = small[0][at, cols] * big[0][i : i + 1, cols] - small[1][at, cols] * big[1][i : i + 1, cols]
                out_ref[to, cols] = value.astype(jnp.bfloat16)
        return carry

    lax.fori_loop(0, small[0].shape[0] // FOLD, device, 0)


def coefficients_into(out_ref, key, mode_z, depth, rows):
    const = 2.0 * math.log(2.0)
    key_low = key & 1023
    key_high = key & ~1023

    def part(i, carry):
        r = lax.broadcasted_iota(jnp.int32, (rows, 128), 0) + i * rows
        at = pl.ds(pl.multiple_of(i * rows, rows), rows)
        freq_x = r.astype(jnp.float32) * (math.pi / LEN_X)
        freq_z = mode_z.astype(jnp.float32) * (math.pi / depth)
        row_part = (0.05 + freq_x * freq_x + freq_z * freq_z) * -const
        base = (r + mode_z * LEN_X) * (2 * LEN_Y)
        lane = lax.broadcasted_iota(jnp.int32, (1, 128), 1)
        for j in range(LEN_Y // 128):
            if j % 4 == 0:
                top = (base + j * 256) ^ key_high
                top = top ^ srl(top, 16)
                delta = jnp.where(((top ^ key_low) & 1) == 0, MULT, -MULT)
            freq_y = (lane + j * 128).astype(jnp.float32) * (math.pi / LEN_Y)
            denom = row_part + freq_y * freq_y * -const
            a = (top ^ (((lane + (j % 4) * 128) * 2) ^ key_low)) * MULT
            b = a + delta
            a = (a ^ srl(a, 16)) * MULT
            b = (b ^ srl(b, 16)) * MULT
            a = srl(a ^ srl(a, 16), 8)
            b = (b ^ srl(b, 16)) >> 8
            u = a.astype(jnp.float32) * 2.0 ** (-24) + 2.0 ** (-25)
            turns = b.astype(jnp.float32) * 2.0 ** (-24) + 2.0 ** (-25)
            bits = jnp.minimum(jnp.log2(u), -1e-30)
            size = bits * lax.rsqrt(bits * denom)
            value = size * cos_turns(turns, const, negative=True)
            out_ref[at, j * 128 : (j + 1) * 128] = value.astype(jnp.bfloat16)
        return carry

    lax.fori_loop(0, LEN_X // rows, part, 0)


def transform_into(out_refs, left_ref, coef_ref, rows_ref, basis_ref):
    for n in range(0, LEN_Y, 512):
        cols = slice(n, n + 512)
        rows_ref[:, cols] = jnp.dot(
            left_ref[...], coef_ref[:, cols], preferred_element_type=jnp.float32
        ).astype(jnp.bfloat16)
    size = rows_ref.shape[0] // len(out_refs)
    for n in range(0, LEN_Y, 512):
        cols = slice(n, n + 512)
        value = contract_last(rows_ref[...], basis_ref[cols, :])
        for m, out_ref in enumerate(out_refs):
            out_ref[:, cols] = value[m * size : (m + 1) * size].astype(jnp.bfloat16)


def first_planes_kernel(
    scalars, out_ref, basis_out, folded_out, basis, folded, coef, rows, small_cos, small_sin, big_cos, big_sin,
    one_cos, one_sin, two_cos, two_sin, sem, *, depth, count, tiles
):
    key, index = scalars[0], scalars[1]
    first = (one_cos, one_sin)
    second = (two_cos.at[pl.ds(0, 8)], two_sin.at[pl.ds(0, 8)])
    basis_into(
        basis, (small_cos.at[pl.ds(0, 64)], small_sin.at[pl.ds(0, 64)]), (big_cos, big_sin), first, second
    )
    folded_basis_into(
        folded,
        (small_cos, small_sin),
        (big_cos.at[pl.ds(0, 8)], big_sin.at[pl.ds(0, 8)]),
        first,
        (two_cos, two_sin),
        (index >> 3) * (8 * count),
        count,
        tiles,
    )
    copies = [
        pltpu.make_async_copy(basis, basis_out, sem.at[0]),
        pltpu.make_async_copy(folded, folded_out, sem.at[1]),
    ]
    for copy in copies:
        copy.start()
    coefficients_into(coef, key, index & 7, depth, 64)
    transform_into([out_ref], folded, coef, rows, basis)
    for copy in copies:
        copy.wait()


def first_planes(scalars, depth, count, tiles):
    total = 8 * tiles * FOLD
    bits = jnp.bfloat16
    return pl.pallas_call(
        functools.partial(first_planes_kernel, depth=depth, count=count, tiles=tiles),
        in_specs=[pl.BlockSpec(memory_space=pltpu.SMEM)],
        out_specs=[pl.BlockSpec(memory_space=pltpu.VMEM)] + [pl.BlockSpec(memory_space=pl.ANY)] * 2,
        out_shape=[
            jax.ShapeDtypeStruct((total, LEN_Y), bits),
            jax.ShapeDtypeStruct((LEN_X, LEN_X), bits),
            jax.ShapeDtypeStruct((total, LEN_X), bits),
        ],
        scratch_shapes=[
            pltpu.VMEM((LEN_X, LEN_X), bits),
            pltpu.VMEM((total, LEN_X), bits),
            pltpu.VMEM((LEN_X, LEN_Y), bits),
            pltpu.VMEM((total, LEN_Y), bits),
            pltpu.VMEM((8 * FOLD, LEN_X), jnp.float32),
            pltpu.VMEM((8 * FOLD, LEN_X), jnp.float32),
            pltpu.VMEM((LEN_X // 64, LEN_X), jnp.float32),
            pltpu.VMEM((LEN_X // 64, LEN_X), jnp.float32),
            pltpu.VMEM((8, LEN_X), jnp.float32),
            pltpu.VMEM((8, LEN_X), jnp.float32),
            pltpu.VMEM((FOLD, LEN_X), jnp.float32),
            pltpu.VMEM((FOLD, LEN_X), jnp.float32),
            pltpu.SemaphoreType.DMA((2,)),
        ],
        compiler_params=pltpu.CompilerParams(vmem_limit_bytes=VMEM_LIMIT),
        cost_estimate=pl.CostEstimate(flops=25_000_000_000, transcendentals=0, bytes_accessed=8_000_000),
        name="first_planes",
    )(scalars)


def shared_mode(index, depth):
    color = (index >> 1 ^ index >> 2) & 1
    return depth // 2 + 4 * color + 2 * (index & 1)


def beside_bit(core, offset):
    return 4 >> (core ^ offset)


def more_planes_kernel(scalars, basis_in, folded_in, *refs, depth, offset):
    out_refs = refs[:PARTS]
    basis, left, coef, rows, sem = refs[PARTS:]
    size = out_refs[0].shape[0]
    key, index = scalars[0], scalars[1]
    mode = shared_mode(index, depth) + offset
    copies = [pltpu.make_async_copy(basis_in, basis, sem.at[PARTS])]
    bit = beside_bit(index & 1, offset)
    for n, flip in enumerate((0, 1, bit, bit ^ 1)):
        source = folded_in.at[pl.ds(pl.multiple_of((index & 7 ^ flip) * size, size), size), :]
        copies.append(pltpu.make_async_copy(source, left.at[pl.ds(n * size, size), :], sem.at[n]))
    for copy in copies:
        copy.start()
    coefficients_into(coef, key, mode, depth, 64)
    for copy in copies:
        copy.wait()
    transform_into(out_refs, left, coef, rows, basis)


def more_planes(scalars, basis, folded, depth, size, offset):
    anywhere = pl.BlockSpec(memory_space=pl.ANY)
    return pl.pallas_call(
        functools.partial(more_planes_kernel, depth=depth, offset=offset),
        in_specs=[pl.BlockSpec(memory_space=pltpu.SMEM), anywhere, anywhere],
        out_specs=[pl.BlockSpec(memory_space=pltpu.VMEM)] * PARTS,
        out_shape=[jax.ShapeDtypeStruct((size, LEN_Y), jnp.bfloat16)] * PARTS,
        scratch_shapes=[
            pltpu.VMEM((LEN_X, LEN_X), jnp.bfloat16),
            pltpu.VMEM((PARTS * size, LEN_X), jnp.bfloat16),
            pltpu.VMEM((LEN_X, LEN_Y), jnp.bfloat16),
            pltpu.VMEM((PARTS * size, LEN_Y), jnp.bfloat16),
            pltpu.SemaphoreType.DMA((PARTS + 1,)),
        ],
        compiler_params=pltpu.CompilerParams(vmem_limit_bytes=VMEM_LIMIT),
        cost_estimate=pl.CostEstimate(flops=20_000_000_000, transcendentals=0, bytes_accessed=8_000_000),
        name="more_planes",
    )(scalars, basis, folded)


def folded_row(index, tiles):
    return index % FOLD * tiles + index // FOLD


def fold_kernel(f_ref, low_ref, high_ref, out_ref, edge):
    _, count, _ = f_ref.shape
    padded = out_ref.shape[1]
    shape = (padded, count + TILE)
    row = folded_row(lax.broadcasted_iota(jnp.int32, shape, 0), padded // FOLD)
    source = jnp.where(row < HALO, row + count, jnp.where(row < HALO + count, row - HALO, row))
    spread = (lax.broadcasted_iota(jnp.int32, shape, 1) == source).astype(jnp.bfloat16)

    @pl.when(pl.program_id(0) == 0)
    def _():
        edge[...] = jnp.zeros(edge.shape, edge.dtype)

    for m in range(f_ref.shape[0]):
        edge[0:HALO, :] = low_ref[m]
        edge[HALO : 2 * HALO, :] = high_ref[m]
        rows = jnp.concatenate([f_ref[m], edge[...]], axis=0)
        for n in range(0, LEN_Y, 512):
            cols = slice(n, n + 512)
            out_ref[m, :, cols] = jnp.dot(spread, rows[:, cols], preferred_element_type=jnp.float32).astype(
                jnp.bfloat16
            )


def fold(forcing, low, high, padded):
    depth, count, _ = forcing.shape
    return pl.pallas_call(
        fold_kernel,
        grid=(depth // 2,),
        in_specs=[
            pl.BlockSpec((2, count, LEN_Y), lambda z: (z, 0, 0)),
            pl.BlockSpec((2, HALO, LEN_Y), lambda z: (z, 0, 0)),
            pl.BlockSpec((2, HALO, LEN_Y), lambda z: (z, 0, 0)),
        ],
        out_specs=pl.BlockSpec((2, padded, LEN_Y), lambda z: (z, 0, 0)),
        out_shape=jax.ShapeDtypeStruct((depth, padded, LEN_Y), jnp.bfloat16),
        scratch_shapes=[pltpu.VMEM((TILE, LEN_Y), jnp.bfloat16)],
        compiler_params=pltpu.CompilerParams(vmem_limit_bytes=VMEM_LIMIT),
        cost_estimate=pl.CostEstimate(flops=1_300_000_000, transcendentals=0, bytes_accessed=10_000_000),
        name="fold",
    )(forcing, low, high)


def chebyshev():
    sigma = THETA / DELTA
    rho = 1.0 / sigma
    pairs = []
    for _ in range(ITERS - 1):
        rho_next = 1.0 / (2.0 * sigma - rho)
        pairs.append((rho_next * rho, 2.0 * rho_next / DELTA))
        rho = rho_next
    return pairs


def solve_kernel(scalars, slot_modes, forcing, block, *refs):
    planes = refs[:-12]
    out_ref, k_ref, y_ref, f_ref, p_two, p_three, b_two, b_three, stage, turned, sems, sem_out = refs[-12:]
    modes = block.shape[0]
    depth, padded, _ = k_ref.shape
    count = out_ref.shape[1]
    tiles = padded // FOLD
    blocks = LEN_Y // 128
    index = scalars[1]

    def cols(j):
        return slice(j * 128, (j + 1) * 128)

    def copies(t, slot):
        at = pl.ds(t * FOLD, FOLD)
        found = [pltpu.make_async_copy(block.at[:, at, :], stage.at[slot, pl.ds(0, modes)], sems.at[slot, 0])]
        for n, plane in enumerate(planes):
            found.append(pltpu.make_async_copy(plane.at[at, :], stage.at[slot, modes + n], sems.at[slot, n + 1]))
        return found

    for copy in copies(0, 0):
        copy.start()
    forcing_copy = pltpu.make_async_copy(forcing, f_ref, sems.at[2, 0])

    size = depth * FOLD
    row = lax.broadcasted_iota(jnp.int32, (size, size), 0)
    col = lax.broadcasted_iota(jnp.int32, (size, size), 1)
    mode = jnp.broadcast_to(slot_modes[...], (size, size))
    phase = ((2 * (row // FOLD) + 1) * mode).astype(jnp.float32)
    weight = jnp.where(mode == 0, math.sqrt(1.0 / depth), math.sqrt(2.0 / depth))
    cosine = cos_turns(turns_of(phase, 4.0 * depth), 1.0)
    mixing = jnp.where(row % FOLD == col % FOLD, weight * cosine, 0.0).astype(jnp.bfloat16)

    def inside(start):
        row = folded_row(lax.broadcasted_iota(jnp.int32, (FOLD, 128), 0) + start, tiles)
        outside = ((row < HALO) & (index == 0)) | ((row >= HALO + count) & (index == WIDE - 1))
        return jnp.where(outside, 0.0, 1.0)

    for t in range(tiles):
        slot = t % 2
        if t + 1 < tiles:
            for copy in copies(t + 1, 1 - slot):
                copy.start()
        else:
            forcing_copy.start()
        for copy in copies(t, slot):
            copy.wait()
        keep = inside(t * FOLD)
        for n in range(0, LEN_Y, 512):
            field = jnp.dot(
                mixing,
                stage[slot, :, :, n : n + 512].reshape(size, 512),
                preferred_element_type=jnp.float32,
            ).reshape(depth, FOLD, 512)
            for j in range(n // 128, n // 128 + 4):
                part = field[:, :, j * 128 - n : j * 128 - n + 128]
                value = jnp.exp(1.5 * jnp.tanh(2.0 * part)) * keep[None]
                k_ref[:, t * FOLD : t * FOLD + FOLD, cols(j)] = value.astype(jnp.bfloat16)
    lane = lax.broadcasted_iota(jnp.int32, (FOLD, 128), 1)
    nothing = jnp.zeros((FOLD, 128), jnp.bfloat16)

    def faces(g, carry):
        at = pl.ds(pl.multiple_of(g // (depth // 4) * FOLD, FOLD), FOLD)
        sums = []
        for u in range(4):
            z = g % (depth // 4) * 4 + u
            here = [k_ref[z, at, cols(j)] for j in range(blocks)]
            turns = [pltpu.roll(k, 127, 1) for k in here] + [nothing]
            sums.append((z, [here[j] + jnp.where(lane == 127, turns[j + 1], turns[j]) for j in range(blocks)]))
        for z, values in sums:
            for j in range(blocks):
                y_ref[z, at, cols(j)] = values[j]
        return carry

    lax.fori_loop(0, tiles * depth // 4, faces, 0)
    forcing_copy.wait()

    def sweep(src, store):
        def tile(i, below, above):
            at = pl.ds(pl.multiple_of(i * FOLD, FOLD), FOLD)
            factor = inside(i * FOLD)

            def level(z, top, flows_z):
                outs = []
                next_flows = []
                k_all = [k_ref[z, at, cols(j)] for j in range(blocks)]
                p_all = [src[z, at, cols(j)] for j in range(blocks)]
                turns = [pltpu.roll(p, 127, 1) for p in p_all] + [nothing]
                before = None
                for j in range(blocks):
                    k, p = k_all[j], p_all[j]
                    flow_y = y_ref[z, at, cols(j)] * (p - jnp.where(lane == 127, turns[j + 1], turns[j]))
                    flow_turn = pltpu.roll(flow_y, 1, 1)
                    left = jnp.where(lane == 0, -k * p if before is None else before, flow_turn)
                    before = flow_turn
                    if top:
                        flow_z = k * p
                    else:
                        flow_z = (k + k_ref[z + 1, at, cols(j)]) * (p - src[z + 1, at, cols(j)])
                    flow_x = (k + above(k_ref, z, j)) * (p - above(src, z, j))
                    flow_w = (k + below(k_ref, z, j)) * (p - below(src, z, j))
                    outs.append((flow_x + flow_w) + ((flow_y - left) + (flow_z - flows_z[j])))
                    next_flows.append(flow_z)
                return next_flows, outs

            def keep(z, outs):
                for j in range(blocks):
                    store(z, j, at, outs[j].astype(jnp.float32), factor)

            def levels(first, flows_z):
                found = []
                for u in range(UNROLL):
                    z = first + u
                    flows_z, outs = level(z, isinstance(z, int) and z == depth - 1, flows_z)
                    found.append(outs)
                for u, outs in enumerate(found):
                    keep(first + u, outs)
                return flows_z

            def group(g, flows_z):
                return levels(g * UNROLL, flows_z)

            flows = [-k_ref[0, at, cols(j)] * src[0, at, cols(j)] for j in range(blocks)]
            groups = depth // UNROLL - 1
            flows = lax.fori_loop(0, groups, group, flows)
            levels(groups * UNROLL, flows)

        def plain(step):
            def load(ref, z, j, i):
                return ref[z, pl.ds(pl.multiple_of((i + step) * FOLD, FOLD), FOLD), cols(j)]

            return load

        def first(ref, z, j):
            return pltpu.roll(ref[z, padded - FOLD : padded, cols(j)], 1, 0)

        def last(ref, z, j):
            return pltpu.roll(ref[z, 0:FOLD, cols(j)], FOLD - 1, 0)

        def inner(i, carry):
            tile(
                i,
                lambda ref, z, j: plain(-1)(ref, z, j, i),
                lambda ref, z, j: plain(1)(ref, z, j, i),
            )
            return carry

        tile(0, first, lambda ref, z, j: plain(1)(ref, z, j, 0))
        lax.fori_loop(1, tiles - 1, inner, 0)
        tile(tiles - 1, lambda ref, z, j: plain(-1)(ref, z, j, tiles - 1), last)

    (a1, b1), (a2, b2), (a3, b3) = chebyshev()

    def store_one(z, j, at, out, factor):
        source = f_ref[z, at, cols(j)].astype(jnp.float32)
        value = ((1.0 + a1) / THETA + b1) * source - (0.5 * b1 / THETA * factor) * out
        p_two[z, at, cols(j)] = value
        b_two[z, at, cols(j)] = value.astype(jnp.bfloat16)

    def store_two(z, j, at, out, factor):
        source = f_ref[z, at, cols(j)].astype(jnp.float32)
        value = (1.0 + a2) * p_two[z, at, cols(j)] + (b2 - a2 / THETA) * source - (0.5 * b2 * factor) * out
        p_three[z, at, cols(j)] = value
        b_three[z, at, cols(j)] = value.astype(jnp.bfloat16)

    def store_three(z, j, at, out, factor):
        source = f_ref[z, at, cols(j)].astype(jnp.float32)
        old = (1.0 + a3) * p_three[z, at, cols(j)] - a3 * p_two[z, at, cols(j)]
        b_two[z, at, cols(j)] = (old + (b3 * source - 0.5 * b3 * out)).astype(jnp.bfloat16)

    sweep(f_ref, store_one)
    sweep(b_two, store_two)
    sweep(b_three, store_three)

    shape = (count, padded)
    place = folded_row(lax.broadcasted_iota(jnp.int32, shape, 1), tiles)
    unfold = (lax.broadcasted_iota(jnp.int32, shape, 0) + HALO == place).astype(jnp.bfloat16)

    def leave(z, slot):
        return pltpu.make_async_copy(turned.at[slot], out_ref.at[z], sem_out.at[slot])

    for z in range(depth):
        slot = z % 2
        if z > 1:
            leave(z - 2, slot).wait()
        for n in range(0, LEN_Y, 512):
            turned[slot, :, n : n + 512] = jnp.dot(
                unfold, b_two[z, :, n : n + 512], preferred_element_type=jnp.float32
            ).astype(jnp.bfloat16)
        leave(z, slot).start()
    for z in (depth - 2, depth - 1):
        leave(z, z % 2).wait()


def solve(scalars, slot_modes, forcing, block, planes, count):
    depth, padded, _ = forcing.shape
    anywhere = pl.BlockSpec(memory_space=pl.ANY)
    narrow = pltpu.VMEM((depth, padded, LEN_Y), jnp.bfloat16)
    whole = pltpu.VMEM((depth, padded, LEN_Y), jnp.float32)
    return pl.pallas_call(
        solve_kernel,
        in_specs=[pl.BlockSpec(memory_space=pltpu.SMEM), pl.BlockSpec(memory_space=pltpu.VMEM)]
        + [anywhere] * (2 + len(planes)),
        out_specs=anywhere,
        out_shape=jax.ShapeDtypeStruct((depth, count, LEN_Y), jnp.bfloat16),
        scratch_shapes=[
            narrow,
            narrow,
            narrow,
            whole,
            whole,
            narrow,
            narrow,
            pltpu.VMEM((2, depth, FOLD, LEN_Y), jnp.bfloat16),
            pltpu.VMEM((2, count, LEN_Y), jnp.bfloat16),
            pltpu.SemaphoreType.DMA((3, 1 + len(planes))),
            pltpu.SemaphoreType.DMA((2,)),
        ],
        compiler_params=pltpu.CompilerParams(vmem_limit_bytes=VMEM_LIMIT),
        name="solve",
    )(scalars, slot_modes, forcing, block, *planes)


def body(stream_index, forcing):
    depth, count, _ = forcing.shape
    index = lax.axis_index("wide")
    scalars = jnp.stack([scramble(stream_index[0] ^ 1540483477), index]).astype(jnp.int32)
    tiles = -(-(count + 2 * HALO) // FOLD)
    padded = tiles * FOLD
    own, basis, folded = first_planes(scalars, depth, count, tiles)
    groups = [list(range(8)), list(range(8, 16))]
    block = lax.all_to_all(
        own.reshape(8, padded, LEN_Y), "wide", 0, 0, axis_index_groups=groups, tiled=True
    )

    def pairwise(offset):
        out = more_planes(scalars, basis, folded, depth, padded, offset)
        routes = [
            [(i, i ^ 1) for i in range(WIDE)],
            [(i, i ^ beside_bit(i & 1, offset)) for i in range(WIDE)],
            [(i, i ^ beside_bit(i & 1, offset) ^ 1) for i in range(WIDE)],
        ]
        return [out[0]] + [lax.ppermute(piece, "wide", route) for piece, route in zip(out[1:], routes)]

    planes = pairwise(0) + pairwise(1)
    slot = lax.broadcasted_iota(jnp.int32, (1, depth * FOLD), 1) // FOLD
    offset = (slot >= 12).astype(jnp.int32)
    source = index ^ (slot & 1)
    source = source ^ jnp.where((slot & 2) == 0, 0, beside_bit(source & 1, offset))
    slot_modes = jnp.where(slot < 8, slot, shared_mode(source, depth) + offset)
    forward = [(i, i + 1) for i in range(WIDE - 1)]
    backward = [(target, source) for source, target in forward]
    low = lax.ppermute(forcing[:, -HALO:], "wide", forward)
    high = lax.ppermute(forcing[:, :HALO], "wide", backward)
    return solve(scalars, slot_modes, fold(forcing, low, high, padded), block, planes, count)


def solution(mesh):
    special = mesh.shape["wide"] == WIDE
    return jax.shard_map(
        body if special else plain_body,
        mesh=mesh,
        in_specs=(P("group"), P("group", "wide", None)),
        out_specs=P("group", "wide", None),
        check_vma=False,
    )
```
